32 devices in a mesh: col: 16 (over z, x, core), row: 2 (over y).
Axes of the slice: x: 2, y: 2, z: 4, core: 2. Of those that a mesh axis runs over, the one named last changes fastest.
Arguments:
- matrix: float32 [2048, 2048], P('row', 'col'), as said below
- row_diag: float32 [2, 2048], P(None, 'row'), may hold values from 0.8 to 1.2
- col_diag: float32 [2, 2048], P(None, 'col'), may hold values from 0.8 to 1.2
Outputs:
- factored: float32 [2048, 2048], P('row', 'col')
The draws below stay inside these ranges and needn't reach their ends.
Inputs may be any that keep to these rules, and one draw needn't show every extreme that they name: `matrix`: off the diagonal the entries lie within -6 and 6; the diagonal entries exceed 1.5 * sqrt(512) - 6.
All inputs are finite; a program needn't handle non-finite values.
Results may differ from the reference program's by a relative error of at most 0.0001.
Values sent between devices are 32-bit elements; how exact they have to be, the bound alone decides.
No kernel may reach another device: no remote copies, remote signals or barrier semaphores. Data moves between devices by JAX's collectives and lax.ppermute only.
A program may use at most 64 MiB of HBM per device.

```python
import jax
import jax.numpy as jnp
from jax import lax

PW = 256
PANELS = 2
NORD = 2048


def draw_matrix(key, part):
    noise_key = jax.random.fold_in(key, 11)
    diag_key = jax.random.fold_in(key, 23)
    noise = jnp.clip(jax.random.normal(noise_key, (NORD, NORD), jnp.float32), -6.0, 6.0)
    leading = jax.random.uniform(diag_key, (NORD,), jnp.float32, 1.5, 2.5) * jnp.sqrt(jnp.float32(PANELS * PW))
    return noise + jnp.diag(leading)


def setup_inputs(seed: int = 0) -> dict:
    key_list = jax.random.split(jax.random.key(seed), 4)
    matrix = draw_matrix(jax.random.fold_in(key_list[3], 71), 0)
    row_diag = jnp.clip(1.0 + 0.04 * jax.random.normal(key_list[1], (2, NORD), jnp.float32), 0.8, 1.2)
    col_diag = jnp.clip(1.0 + 0.04 * jax.random.normal(key_list[2], (2, NORD), jnp.float32), 0.8, 1.2)
    return {"matrix": matrix, "row_diag": row_diag, "col_diag": col_diag}


inv_root = 0.7071067811865476


def mix_halves(values, scales, axis):
    half = values.shape[axis] // 2
    if axis == 0:
        upper_part, lower_part = values[:half], values[half:]
        first, second = scales[:half, None], scales[half:, None]
    else:
        upper_part, lower_part = values[:, :half], values[:, half:]
        first, second = scales[None, :half], scales[None, half:]
    return jnp.concatenate([first * (upper_part + lower_part) * inv_root, second * (upper_part - lower_part) * inv_root], axis)


def level_two(values, scales, axis):
    half = values.shape[axis] // 2
    if axis == 0:
        left_part, right_part = values[:half], values[half:]
    else:
        left_part, right_part = values[:, :half], values[:, half:]
    return jnp.concatenate([mix_halves(left_part, scales[:half], axis), mix_halves(right_part, scales[half:], axis)], axis)


def lu_block(block):
    size = block.shape[0]
    places = jnp.arange(size)

    def eliminate(step, current):
        pivot = current[step, step]
        below = places > step
        column = jnp.where(below, current[:, step] / pivot, 0.0)
        across = jnp.where(below, current[step, :], 0.0)
        current = current - column[:, None] * across[None, :]
        return jnp.where((places == step)[None, :] & below[:, None], column[:, None], current)

    return lax.fori_loop(0, size, eliminate, block)


def hdot(left, right):
    return jnp.dot(left, right, precision=lax.Precision.HIGHEST, preferred_element_type=jnp.float32)


def strict_inverse(strict):
    size = strict.shape[0]
    identity = jnp.eye(size, dtype=strict.dtype)
    result = identity - strict
    power = strict
    exponent = 1
    while exponent * 2 < size:
        power = hdot(power, power)
        exponent = exponent * 2
        result = hdot(result, identity + power)
    return result


def inverses(packed):
    upper_factor = jnp.triu(packed)
    lower_inverse = strict_inverse(jnp.tril(packed, -1))
    pivots = jnp.diagonal(packed)
    scaled = jnp.triu(packed, 1) / pivots[:, None]
    upper_inverse = strict_inverse(scaled) / pivots[None, :]
    return lower_inverse, upper_inverse, upper_factor


def reference(matrix, row_diag, col_diag):
    current = mix_halves(matrix, row_diag[0], 0)
    current = level_two(current, row_diag[1], 0)
    current = mix_halves(current, col_diag[0], 1)
    current = level_two(current, col_diag[1], 1)
    for panel in range(PANELS):
        start = panel * PW
        stop = start + PW
        packed = lu_block(current[start:stop, start:stop])
        lower_inverse, upper_inverse, upper_factor = inverses(packed)
        lower_rows = hdot(current[stop:, start:stop], upper_inverse)
        upper_cols = hdot(lower_inverse, current[start:stop, stop:])
        trailing = current[stop:, stop:] - hdot(lower_rows, upper_cols)
        current = current.at[start:stop, start:stop].set(packed)
        current = current.at[stop:, start:stop].set(lower_rows)
        current = current.at[start:stop, stop:].set(upper_cols)
        current = current.at[stop:, stop:].set(trailing)
    return current
```

```python
import jax
import jax.numpy as jnp
from jax import lax
from jax.experimental import pallas as pl
from jax.experimental.pallas import tpu as pltpu
from jax.sharding import PartitionSpec as P

PW = 256
PANELS = 2
LEAD = PW * PANELS

inv_root = 0.7071067811865476

SUB = 8
BLK = 128


def swapped(x, axis, mask):
    return lax.ppermute(x, axis, [(i, i ^ mask) for i in range(lax.axis_size(axis))])


def hdot(left, right):
    return jnp.dot(left, right, precision=lax.Precision.HIGHEST, preferred_element_type=jnp.float32)


def tree_sum(terms):
    while len(terms) > 1:
        terms = [terms[i] + terms[i + 1] if i + 1 < len(terms) else terms[i] for i in range(0, len(terms), 2)]
    return terms[0]


def factor(block):
    count = BLK // SUB
    shape = (SUB, BLK)
    sub = lax.broadcasted_iota(jnp.int32, shape, 0)
    lane = lax.broadcasted_iota(jnp.int32, shape, 1)

    def row(x, j):
        return jnp.broadcast_to(x[j : j + 1, :], shape)

    def col(x, j):
        return jnp.broadcast_to(x[:, j : j + 1], shape)

    strips = [block[SUB * i : SUB * (i + 1)] for i in range(count)]
    extra = [jnp.where(lane == sub + SUB * i, 1.0, 0.0) for i in range(count)]
    pending = [jnp.zeros(shape, jnp.float32) for _ in range(count)]
    upper = []
    small = []
    for t in range(count):
        base = SUB * t
        inside = (lane >= base) & (lane < base + SUB)
        for i in range(t, count):
            pending[i] = jnp.where(inside, strips[i], pending[i])
        c = [col(strips[t], base + m) for m in range(SUB)]
        w, x, forward = strips[t], extra[t], strips[t]
        g = jnp.where(lane == sub + base, 1.0, 0.0)
        for j in range(SUB):
            r = 1.0 / row(c[j], j)
            here = sub == j
            cj = c[j]
            for m in range(j + 1, SUB):
                scaled = row(c[m], j) * r
                c[m] = jnp.where(here, scaled, c[m] - cj * scaled)
            scaled = row(w, j) * r
            w = jnp.where(here, scaled, w - cj * scaled)
            scaled = row(x, j) * r
            x = jnp.where(here, scaled, x - cj * scaled)
            scaled = row(g, j) * r
            g = jnp.where(sub > j, g, jnp.where(here, scaled, g - cj * scaled))
            if j < SUB - 1:
                forward = jnp.where(sub > j, forward - (cj * r) * row(forward, j), forward)
        upper.append(forward)
        small.append(g)
        w_rows = [row(w, m) for m in range(SUB)]
        x_rows = [row(x, m) for m in range(SUB)]
        for i in list(range(t + 1, count)) + list(range(t)):
            b = [col(strips[i], base + m) for m in range(SUB)]
            strips[i] = strips[i] - tree_sum([b[m] * w_rows[m] for m in range(SUB)])
            extra[i] = extra[i] - tree_sum([b[m] * x_rows[m] for m in range(SUB)])
        strips[t], extra[t] = w, x
    upper, pending, small, inverse = (jnp.concatenate(v, 0) for v in (upper, pending, small, extra))
    return upper, hdot(pending, small), inverse


def lu_kernel(info, *refs):
    blocks = LEAD // BLK
    panel_refs = refs[:blocks]
    own_top, own, out, work, rhs, packed, reduced = refs[blocks:]
    is_panel = info[0] == 1
    slot = info[1]
    is_top = info[2] == 1
    for j in range(blocks):
        work[j] = panel_refs[j][0:LEAD, :]
    rhs[...] = own_top[...]
    for k in range(blocks):
        here = pl.ds(BLK * k, BLK)
        upper, lower, inverse = factor(work[k, here, :])
        size = (BLK, BLK)
        above = lax.broadcasted_iota(jnp.int32, size, 0) <= lax.broadcasted_iota(jnp.int32, size, 1)
        upper = jnp.where(above, upper, 0.0)
        packed[k, here, :] = jnp.where(above, upper, lower)
        upper_inverse = hdot(inverse, lower)
        solved = [hdot(inverse, work[j, here, :]) for j in range(k + 1, blocks)]
        solved_rhs = hdot(inverse, rhs[here, :])
        if k + 1 < blocks:
            rest = pl.ds(BLK * (k + 1), LEAD - BLK * (k + 1))
            left = work[k, rest, :]
            for n, j in enumerate(range(k + 1, blocks)):
                work[j, rest, :] = work[j, rest, :] - hdot(left, solved[n])
            rhs[rest, :] = rhs[rest, :] - hdot(left, solved_rhs)
            packed[k, rest, :] = hdot(left, upper_inverse)
        for n, j in enumerate(range(k + 1, blocks)):
            packed[j, here, :] = hdot(upper, solved[n])
            work[j, here, :] = solved[n]
        out[here, :] = hdot(upper, solved_rhs)
        mine = jnp.where(slot == k, upper_inverse, 0.0)
        reduced[here, :] = jnp.where(is_panel, mine, solved_rhs)
    for k in range(blocks - 2, -1, -1):
        here = pl.ds(BLK * k, BLK)
        terms = [hdot(work[j, here, :], reduced[pl.ds(BLK * j, BLK), :]) for j in range(k + 1, blocks)]
        reduced[here, :] = reduced[here, :] - tree_sum(terms)
    top = jnp.where(is_panel, packed[slot], out[0:LEAD, :])
    height = out.shape[0]

    def below(first, rows):
        where = pl.ds(first, rows)
        terms = [
            hdot(panel_refs[j][pl.ds(LEAD + first, rows), :], reduced[pl.ds(BLK * j, BLK), :]) for j in range(blocks)
        ]
        total = tree_sum(terms)
        return jnp.where(is_panel, total, own[where, :] - total)

    for first in range(0, LEAD, 256):
        part = below(first, 256)
        out[pl.ds(first, 256), :] = jnp.where(is_top, top[first : first + 256], part)
    if height - LEAD <= 512:
        for first in range(LEAD, height, 256):
            out[pl.ds(first, 256), :] = below(first, 256)
    else:

        def step(n, carry):
            first = pl.multiple_of(LEAD + n * 256, 256)
            out[pl.ds(first, 256), :] = below(first, 256)
            return carry

        lax.fori_loop(0, (height - LEAD) // 256, step, 0)


def shards(matrix, row_diag, col_diag):
    height, width = matrix.shape
    row_pos = lax.axis_index("row")
    col_pos = lax.axis_index("col")
    half = height // 2
    blocks = LEAD // width
    block_bits = blocks.bit_length() - 1
    high_bit = lax.axis_size("col").bit_length() - 2
    high, low = 2**high_bit, 2 ** (high_bit - 1)
    is_first = row_pos == 0

    partner = swapped(matrix, "row", 1)
    other_rows = swapped(row_diag, "row", 1)
    others = {mask: swapped(col_diag, "col", mask) for mask in (low, high, high | low)}
    first_diag = jnp.where(is_first, row_diag, other_rows)
    total = matrix + partner
    mixed = row_diag[0][:, None] * jnp.where(is_first, total, partner - matrix) * inv_root
    upper_part, lower_part = mixed[:half], mixed[half:]
    first_mixed = first_diag[0][:, None] * total * inv_root
    top_rows = first_diag[1][:LEAD, None] * (first_mixed[:LEAD] + first_mixed[half : half + LEAD]) * inv_root
    current = jnp.concatenate(
        [
            top_rows,
            row_diag[1][:half, None] * (upper_part + lower_part) * inv_root,
            row_diag[1][half:, None] * (upper_part - lower_part) * inv_root,
        ],
        0,
    )

    in_high = (col_pos & high) != 0
    in_low = (col_pos & low) != 0
    by_mask = {0: col_diag, **others}

    def diag_of(h, l):
        mask = jnp.where(in_high != h, high, 0) + jnp.where(in_low != l, low, 0)
        picked = col_diag
        for m, value in others.items():
            picked = jnp.where(mask == m, value, picked)
        return picked

    partner = swapped(current, "col", low)
    even = jnp.where(in_low, partner, current)
    odd = jnp.where(in_low, current, partner)

    def contribution(h, l):
        scale_even = diag_of(h, jnp.bool_(False))[0]
        scale_odd = diag_of(h, jnp.bool_(True))[0]
        sign = jnp.where(in_high & h, -0.5, 0.5)
        return (sign * scale_even) * even + (jnp.where(l, -sign, sign) * scale_odd) * odd

    none = jnp.bool_(False)
    sent = contribution(~in_high, ~in_low)
    kept = contribution(in_high, in_low)
    lead = contribution(none, none)
    received = swapped(sent, "col", high | low)
    received_lead = swapped(lead, "col", high | low)
    own = col_diag[1] * (kept + received)
    panel = diag_of(none, none)[1] * (lead + received_lead)

    for bit in range(block_bits, high_bit - 1):
        arrived = swapped(panel, "col", 2**bit)
        panel = jnp.where((col_pos & 2**bit) != 0, arrived, panel)
    pieces = [panel]
    for bit in range(block_bits - 1, -1, -1):
        arrived = [swapped(p, "col", 2**bit) for p in pieces]
        second = (col_pos & 2**bit) != 0
        pieces = [
            piece
            for a, b in zip(pieces, arrived)
            for piece in (jnp.where(second, b, a), jnp.where(second, a, b))
        ]

    info = jnp.stack(
        [(col_pos < blocks).astype(jnp.int32), jnp.minimum(col_pos, blocks - 1).astype(jnp.int32), is_first.astype(jnp.int32)]
    )
    vmem = pl.BlockSpec(memory_space=pltpu.VMEM)
    return pl.pallas_call(
        lu_kernel,
        out_shape=jax.ShapeDtypeStruct((height, width), jnp.float32),
        in_specs=[pl.BlockSpec(memory_space=pltpu.SMEM)] + [vmem] * (blocks + 2),
        out_specs=vmem,
        scratch_shapes=[
            pltpu.VMEM((blocks, LEAD, width), jnp.float32),
            pltpu.VMEM((LEAD, width), jnp.float32),
            pltpu.VMEM((blocks, LEAD, width), jnp.float32),
            pltpu.VMEM((LEAD, width), jnp.float32),
        ],
        name="panel_lu",
    )(info, *pieces, own[:LEAD], own[LEAD:])


def solution(mesh):
    in_specs = (P("row", "col"), P(None, "row"), P(None, "col"))
    out_specs = P("row", "col")
    return jax.shard_map(shards, mesh=mesh, in_specs=in_specs, out_specs=out_specs, check_vma=False)
```

```python
import functools

import jax
import jax.numpy as jnp
from jax import lax
from jax.experimental import pallas as pl
from jax.experimental.pallas import tpu as pltpu
from jax.sharding import PartitionSpec as P

PW = 256
PANELS = 2
LEAD = PW * PANELS

SUB = 8
BLK = 128


def swapped(x, axis, mask):
    return lax.ppermute(x, axis, [(i, i ^ mask) for i in range(lax.axis_size(axis))])


def hdot(left, right):
    return jnp.dot(left, right, precision=lax.Precision.HIGHEST, preferred_element_type=jnp.float32)


def tree_sum(terms):
    while len(terms) > 1:
        terms = [terms[i] + terms[i + 1] if i + 1 < len(terms) else terms[i] for i in range(0, len(terms), 2)]
    return terms[0]


def factor(block):
    count = BLK // SUB
    shape = (SUB, BLK)
    sub = lax.broadcasted_iota(jnp.int32, shape, 0)
    lane = lax.broadcasted_iota(jnp.int32, shape, 1)

    def row(x, j):
        return jnp.broadcast_to(x[j : j + 1, :], shape)

    def col(x, j):
        return jnp.broadcast_to(x[:, j : j + 1], shape)

    strips = [block[SUB * i : SUB * (i + 1)] for i in range(count)]
    extra = [jnp.where(lane == sub + SUB * i, 1.0, 0.0) for i in range(count)]
    pending = [jnp.zeros(shape, jnp.float32) for _ in range(count)]
    upper = []
    small = []
    for t in range(count):
        base = SUB * t
        inside = (lane >= base) & (lane < base + SUB)
        for i in range(t, count):
            pending[i] = jnp.where(inside, strips[i], pending[i])
        c = [col(strips[t], base + m) for m in range(SUB)]
        w, x, forward = strips[t], extra[t], strips[t]
        g = jnp.where(lane == sub + base, 1.0, 0.0)
        for j in range(SUB):
            r = 1.0 / row(c[j], j)
            here = sub == j
            cj = c[j]
            for m in range(j + 1, SUB):
                scaled = row(c[m], j) * r
                c[m] = jnp.where(here, scaled, c[m] - cj * scaled)
            scaled = row(w, j) * r
            w = jnp.where(here, scaled, w - cj * scaled)
            scaled = row(x, j) * r
            x = jnp.where(here, scaled, x - cj * scaled)
            scaled = row(g, j) * r
            g = jnp.where(sub > j, g, jnp.where(here, scaled, g - cj * scaled))
            if j < SUB - 1:
                forward = jnp.where(sub > j, forward - (cj * r) * row(forward, j), forward)
        upper.append(forward)
        small.append(g)
        w_rows = [row(w, m) for m in range(SUB)]
        x_rows = [row(x, m) for m in range(SUB)]
        for i in list(range(t + 1, count)) + list(range(t)):
            b = [col(strips[i], base + m) for m in range(SUB)]
            strips[i] = strips[i] - tree_sum([b[m] * w_rows[m] for m in range(SUB)])
            extra[i] = extra[i] - tree_sum([b[m] * x_rows[m] for m in range(SUB)])
        strips[t], extra[t] = w, x
    upper, pending, small, inverse = (jnp.concatenate(v, 0) for v in (upper, pending, small, extra))
    return upper, hdot(pending, small), inverse


def eliminate_block(k, work, packed, inverted):
    blocks = LEAD // BLK
    here = pl.ds(BLK * k, BLK)
    upper, lower, inverse = factor(work[k, here, :])
    size = (BLK, BLK)
    above = lax.broadcasted_iota(jnp.int32, size, 0) <= lax.broadcasted_iota(jnp.int32, size, 1)
    upper = jnp.where(above, upper, 0.0)
    packed[k, here, :] = jnp.where(above, upper, lower)
    upper_inverse = hdot(inverse, lower)
    inverted[here, :] = upper_inverse
    work[k, here, :] = inverse
    later = range(k + 1, blocks)
    solved = {j: hdot(inverse, work[j, here, :]) for j in later}
    if k + 1 < blocks:
        rest = pl.ds(BLK * (k + 1), LEAD - BLK * (k + 1))
        left = work[k, rest, :]
        for j in later:
            work[j, rest, :] = work[j, rest, :] - hdot(left, solved[j])
        packed[k, rest, :] = hdot(left, upper_inverse)
    for j in later:
        packed[j, here, :] = hdot(upper, solved[j])
        work[j, here, :] = solved[j]


def first_kernel(*refs):
    blocks = LEAD // BLK
    pieces, (work, packed, inverted) = refs[:blocks], refs[blocks:]
    for j in range(blocks):
        work[j] = pieces[j][...]
    eliminate_block(0, work, packed, inverted)


def next_kernel(k, old_work, old_packed, old_inverted, work, packed, inverted):
    eliminate_block(k, work, packed, inverted)


def last_kernel(info, work, packed, inverted, own_top, own, *refs):
    blocks = LEAD // BLK
    pieces, (out, rhs, reduced, top) = refs[:blocks], refs[blocks:]
    is_panel = info[0] == 1
    slot = info[1]
    is_top = info[2] == 1
    rhs[...] = own_top[...]
    size = (BLK, BLK)
    above = lax.broadcasted_iota(jnp.int32, size, 0) <= lax.broadcasted_iota(jnp.int32, size, 1)
    for k in range(blocks):
        here = pl.ds(BLK * k, BLK)
        solved = hdot(work[k, here, :], rhs[here, :])
        for i in range(k + 1, blocks):
            there = pl.ds(BLK * i, BLK)
            rhs[there, :] = rhs[there, :] - hdot(work[k, there, :], solved)
        upper = jnp.where(above, packed[k, here, :], 0.0)
        top[here, :] = jnp.where(is_panel, packed[slot, here, :], hdot(upper, solved))
        mine = jnp.where(slot == k, inverted[here, :], 0.0)
        reduced[here, :] = jnp.where(is_panel, mine, solved)
    for k in range(blocks - 2, -1, -1):
        here = pl.ds(BLK * k, BLK)
        terms = [hdot(work[j, here, :], reduced[pl.ds(BLK * j, BLK), :]) for j in range(k + 1, blocks)]
        reduced[here, :] = reduced[here, :] - tree_sum(terms)
    height = out.shape[0]

    def below(first, rows):
        where = pl.ds(first, rows)
        terms = [hdot(pieces[j][where, :], reduced[pl.ds(BLK * j, BLK), :]) for j in range(blocks)]
        total = tree_sum(terms)
        return jnp.where(is_panel, total, own[where, :] - total)

    for first in range(0, LEAD, 256):
        out[pl.ds(first, 256), :] = jnp.where(is_top, top[pl.ds(first, 256), :], below(first, 256))

    def step(n, carry):
        first = pl.multiple_of(LEAD + n * 256, 256)
        out[pl.ds(first, 256), :] = below(first, 256)
        return carry

    lax.fori_loop(0, (height - LEAD) // 256, step, 0)


def shards(matrix, row_diag, col_diag):
    height, width = matrix.shape
    row_pos = lax.axis_index("row")
    col_pos = lax.axis_index("col")
    half = height // 2
    blocks = LEAD // width
    block_bits = blocks.bit_length() - 1
    high_bit = lax.axis_size("col").bit_length() - 2
    high, low = 2**high_bit, 2 ** (high_bit - 1)
    is_first = row_pos == 0
    in_high = (col_pos & high) != 0
    in_low = (col_pos & low) != 0

    partner = swapped(matrix, "row", 1)
    other_rows = swapped(row_diag, "row", 1)
    pair = jnp.concatenate([col_diag, swapped(col_diag, "col", low)], 0)
    far_pair = swapped(pair, "col", high)

    def diag_of(h, l):
        near = in_high == h
        chosen = jnp.where(near, pair, far_pair)
        return jnp.where(in_low == l, chosen[:2], chosen[2:])

    first_diag = jnp.where(is_first, row_diag, other_rows)
    total = matrix + partner
    lead_sum = [first_diag[0][a : a + LEAD, None] * total[a : a + LEAD] for a in (0, half)]
    top_rows = (0.5 * first_diag[1][:LEAD])[:, None] * (lead_sum[0] + lead_sum[1])
    mixed = row_diag[0][:, None] * jnp.where(is_first, total, partner - matrix)
    upper_part, lower_part = mixed[:half], mixed[half:]
    own_rows = jnp.concatenate(
        [
            (0.5 * row_diag[1][:half])[:, None] * (upper_part + lower_part),
            (0.5 * row_diag[1][half:])[:, None] * (upper_part - lower_part),
        ],
        0,
    )

    none, yes = jnp.bool_(False), jnp.bool_(True)

    def halves(values):
        other = swapped(values, "col", low)
        return jnp.where(in_low, other, values), jnp.where(in_low, values, other)

    def contribution(parts, h, l):
        even, odd = parts
        sign = jnp.where(in_high & h, -0.5, 0.5)
        scale_even = sign * diag_of(h, none)[0]
        scale_odd = jnp.where(l, -sign, sign) * diag_of(h, yes)[0]
        return scale_even * even + scale_odd * odd

    def spread(values):
        for bit in range(block_bits, high_bit - 1):
            arrived = swapped(values, "col", 2**bit)
            values = jnp.where((col_pos & 2**bit) != 0, arrived, values)
        return values

    def gather(pieces, bit):
        arrived = [swapped(p, "col", 2**bit) for p in pieces]
        second = (col_pos & 2**bit) != 0
        return [
            piece
            for a, b in zip(pieces, arrived)
            for piece in (jnp.where(second, b, a), jnp.where(second, a, b))
        ]

    lead_scale = diag_of(none, none)[1]
    top_parts = halves(top_rows)
    lead = contribution(top_parts, none, none)
    lead = spread(lead_scale * (lead + swapped(lead, "col", high)))
    own_parts = halves(own_rows)
    lead_pieces = [lead]
    for bit in range(block_bits - 1, -1, -1):
        lead_pieces = gather(lead_pieces, bit)

    panel = contribution(own_parts, none, none)
    panel_half = jnp.where(in_low, panel[half:], panel[:half])
    far_half, _ = lax.optimization_barrier((swapped(panel_half, "col", high), lead))
    panel_half = lead_scale * (panel_half + far_half)
    sent = jnp.concatenate(
        [contribution(top_parts, ~in_high, in_low), contribution(own_parts, ~in_high, in_low)], 0
    )
    kept = jnp.concatenate([contribution(top_parts, in_high, in_low), contribution(own_parts, in_high, in_low)], 0)
    received = swapped(sent, "col", high)
    other_half = swapped(panel_half, "col", low)
    panel = spread(
        jnp.where(
            in_low,
            jnp.concatenate([other_half, panel_half], 0),
            jnp.concatenate([panel_half, other_half], 0),
        )
    )
    panel_pieces = [panel]

    vmem = pl.BlockSpec(memory_space=pltpu.VMEM)
    cost = pl.CostEstimate(flops=4_000_000_000, bytes_accessed=12_000_000, transcendentals=0)
    size = 4 * width * (5 * blocks * LEAD + (blocks + 4) * (height + LEAD))
    params = pltpu.CompilerParams(vmem_limit_bytes=2 * size)
    stack = jax.ShapeDtypeStruct((blocks, LEAD, width), jnp.float32)
    state_shapes = (stack, stack, jax.ShapeDtypeStruct((LEAD, width), jnp.float32))
    state = pl.pallas_call(
        first_kernel,
        out_shape=state_shapes,
        in_specs=[vmem] * blocks,
        out_specs=(vmem,) * 3,
        cost_estimate=cost,
        compiler_params=params,
        name="eliminate_0",
    )(*lead_pieces)
    for k in range(1, blocks):
        state = pl.pallas_call(
            functools.partial(next_kernel, k),
            out_shape=state_shapes,
            in_specs=[vmem] * 3,
            out_specs=(vmem,) * 3,
            input_output_aliases={0: 0, 1: 1, 2: 2},
            cost_estimate=cost,
            compiler_params=params,
            name=f"eliminate_{k}",
        )(*state)

    for bit in range(block_bits - 1, -1, -1):
        panel_pieces = gather(panel_pieces, bit)
    whole = diag_of(in_high, in_low)[1] * (kept + received)

    info = jnp.stack(
        [
            (col_pos < blocks).astype(jnp.int32),
            jnp.minimum(col_pos, blocks - 1).astype(jnp.int32),
            is_first.astype(jnp.int32),
        ]
    )
    return pl.pallas_call(
        last_kernel,
        out_shape=jax.ShapeDtypeStruct((height, width), jnp.float32),
        in_specs=[pl.BlockSpec(memory_space=pltpu.SMEM)] + [vmem] * (blocks + 5),
        out_specs=vmem,
        scratch_shapes=[pltpu.VMEM((LEAD, width), jnp.float32)] * 3,
        cost_estimate=cost,
        compiler_params=params,
        name="own_columns",
    )(info, *state, whole[:LEAD], whole[LEAD:], *panel_pieces)


def solution(mesh):
    in_specs = (P("row", "col"), P(None, "row"), P(None, "col"))
    out_specs = P("row", "col")
    return jax.shard_map(shards, mesh=mesh, in_specs=in_specs, out_specs=out_specs, check_vma=False)
```

```python
import functools

import jax
import jax.numpy as jnp
from jax import lax
from jax.experimental import pallas as pl
from jax.experimental.pallas import tpu as pltpu
from jax.sharding import PartitionSpec as P

PW = 256
PANELS = 2
LEAD = PW * PANELS

SUB = 8
BLK = 128


def swapped(x, axis, mask):
    return lax.ppermute(x, axis, [(i, i ^ mask) for i in range(lax.axis_size(axis))])


def hdot(left, right):
    return jnp.dot(left, right, precision=lax.Precision.HIGHEST, preferred_element_type=jnp.float32)


def tree_sum(terms):
    while len(terms) > 1:
        terms = [terms[i] + terms[i + 1] if i + 1 < len(terms) else terms[i] for i in range(0, len(terms), 2)]
    return terms[0]


def factor(block):
    count = BLK // SUB
    shape = (SUB, BLK)
    sub = lax.broadcasted_iota(jnp.int32, shape, 0)
    lane = lax.broadcasted_iota(jnp.int32, shape, 1)

    def row(x, j):
        return jnp.broadcast_to(x[j : j + 1, :], shape)

    def col(x, j):
        return jnp.broadcast_to(x[:, j : j + 1], shape)

    strips = [block[SUB * i : SUB * (i + 1)] for i in range(count)]
    extra = [jnp.where(lane == sub + SUB * i, 1.0, 0.0) for i in range(count)]
    pending = [jnp.zeros(shape, jnp.float32) for _ in range(count)]
    upper = []
    small = []
    for t in range(count):
        base = SUB * t
        inside = (lane >= base) & (lane < base + SUB)
        for i in range(t, count):
            pending[i] = jnp.where(inside, strips[i], pending[i])
        c = [col(strips[t], base + m) for m in range(SUB)]
        w, x, forward = strips[t], extra[t], strips[t]
        g = jnp.where(lane == sub + base, 1.0, 0.0)
        for j in range(SUB):
            r = 1.0 / row(c[j], j)
            here = sub == j
            cj = c[j]
            for m in range(j + 1, SUB):
                scaled = row(c[m], j) * r
                c[m] = jnp.where(here, scaled, c[m] - cj * scaled)
            scaled = row(w, j) * r
            w = jnp.where(here, scaled, w - cj * scaled)
            scaled = row(x, j) * r
            x = jnp.where(here, scaled, x - cj * scaled)
            scaled = row(g, j) * r
            g = jnp.where(sub > j, g, jnp.where(here, scaled, g - cj * scaled))
            if j < SUB - 1:
                forward = jnp.where(sub > j, forward - (cj * r) * row(forward, j), forward)
        upper.append(forward)
        small.append(g)
        w_rows = [row(w, m) for m in range(SUB)]
        x_rows = [row(x, m) for m in range(SUB)]
        for i in list(range(t + 1, count)) + list(range(t)):
            b = [col(strips[i], base + m) for m in range(SUB)]
            strips[i] = strips[i] - tree_sum([b[m] * w_rows[m] for m in range(SUB)])
            extra[i] = extra[i] - tree_sum([b[m] * x_rows[m] for m in range(SUB)])
        strips[t], extra[t] = w, x
    upper, pending, small, inverse = (jnp.concatenate(v, 0) for v in (upper, pending, small, extra))
    return upper, hdot(pending, small), inverse


def eliminate_block(k, work, packed, inverted):
    blocks = LEAD // BLK
    here = pl.ds(BLK * k, BLK)
    upper, lower, inverse = factor(work[k, here, :])
    size = (BLK, BLK)
    above = lax.broadcasted_iota(jnp.int32, size, 0) <= lax.broadcasted_iota(jnp.int32, size, 1)
    upper = jnp.where(above, upper, 0.0)
    packed[k, here, :] = jnp.where(above, upper, lower)
    upper_inverse = hdot(inverse, lower)
    inverted[here, :] = upper_inverse
    work[k, here, :] = inverse
    later = range(k + 1, blocks)
    solved = {j: hdot(inverse, work[j, here, :]) for j in later}
    if k + 1 < blocks:
        rest = pl.ds(BLK * (k + 1), LEAD - BLK * (k + 1))
        left = work[k, rest, :]
        for j in later:
            work[j, rest, :] = work[j, rest, :] - hdot(left, solved[j])
        packed[k, rest, :] = hdot(left, upper_inverse)
    for j in later:
        packed[j, here, :] = hdot(upper, solved[j])
        work[j, here, :] = solved[j]


def first_kernel(*refs):
    blocks = LEAD // BLK
    pieces, (work, packed, inverted) = refs[:blocks], refs[blocks:]
    for j in range(blocks):
        work[j] = pieces[j][...]
    eliminate_block(0, work, packed, inverted)


def next_kernel(k, old_work, old_packed, old_inverted, work, packed, inverted):
    eliminate_block(k, work, packed, inverted)


def last_kernel(info, work, packed, inverted, own_top, own, *refs):
    blocks = LEAD // BLK
    pieces, (out, rhs, reduced, top) = refs[:blocks], refs[blocks:]
    is_panel = info[0] == 1
    slot = info[1]
    is_top = info[2] == 1
    rhs[...] = own_top[...]
    size = (BLK, BLK)
    above = lax.broadcasted_iota(jnp.int32, size, 0) <= lax.broadcasted_iota(jnp.int32, size, 1)
    for k in range(blocks):
        here = pl.ds(BLK * k, BLK)
        solved = hdot(work[k, here, :], rhs[here, :])
        for i in range(k + 1, blocks):
            there = pl.ds(BLK * i, BLK)
            rhs[there, :] = rhs[there, :] - hdot(work[k, there, :], solved)
        upper = jnp.where(above, packed[k, here, :], 0.0)
        top[here, :] = jnp.where(is_panel, packed[slot, here, :], hdot(upper, solved))
        mine = jnp.where(slot == k, inverted[here, :], 0.0)
        reduced[here, :] = jnp.where(is_panel, mine, solved)
    for k in range(blocks - 2, -1, -1):
        here = pl.ds(BLK * k, BLK)
        terms = [hdot(work[j, here, :], reduced[pl.ds(BLK * j, BLK), :]) for j in range(k + 1, blocks)]
        reduced[here, :] = reduced[here, :] - tree_sum(terms)
    height = out.shape[0]

    def below(first, rows):
        where = pl.ds(first, rows)
        terms = [hdot(pieces[j][where, :], reduced[pl.ds(BLK * j, BLK), :]) for j in range(blocks)]
        total = tree_sum(terms)
        return jnp.where(is_panel, total, own[where, :] - total)

    for first in range(0, LEAD, 256):
        out[pl.ds(first, 256), :] = jnp.where(is_top, top[pl.ds(first, 256), :], below(first, 256))

    def step(n, carry):
        first = pl.multiple_of(LEAD + n * 256, 256)
        out[pl.ds(first, 256), :] = below(first, 256)
        return carry

    lax.fori_loop(0, (height - LEAD) // 256, step, 0)


def shards(matrix, row_diag, col_diag):
    height, width = matrix.shape
    row_pos = lax.axis_index("row")
    col_pos = lax.axis_index("col")
    half = height // 2
    blocks = LEAD // width
    block_bits = blocks.bit_length() - 1
    high_bit = lax.axis_size("col").bit_length() - 2
    high, low = 2**high_bit, 2 ** (high_bit - 1)
    is_first = row_pos == 0
    in_high = (col_pos & high) != 0
    in_low = (col_pos & low) != 0

    partner = swapped(matrix, "row", 1)
    other_rows = swapped(row_diag, "row", 1)
    pair = jnp.concatenate([col_diag, swapped(col_diag, "col", low)], 0)
    far_pair = swapped(pair, "col", high)

    def diag_of(h, l):
        near = in_high == h
        chosen = jnp.where(near, pair, far_pair)
        return jnp.where(in_low == l, chosen[:2], chosen[2:])

    first_diag = jnp.where(is_first, row_diag, other_rows)
    total = matrix + partner
    lead_sum = [first_diag[0][a : a + LEAD, None] * total[a : a + LEAD] for a in (0, half)]
    top_rows = (0.5 * first_diag[1][:LEAD])[:, None] * (lead_sum[0] + lead_sum[1])
    none, yes = jnp.bool_(False), jnp.bool_(True)

    def halves(values):
        other = swapped(values, "col", low)
        return jnp.where(in_low, other, values), jnp.where(in_low, values, other)

    def contribution(parts, h, l):
        even, odd = parts
        sign = jnp.where(in_high & h, -0.5, 0.5)
        scale_even = sign * diag_of(h, none)[0]
        scale_odd = jnp.where(l, -sign, sign) * diag_of(h, yes)[0]
        return scale_even * even + scale_odd * odd

    def spread(values):
        for bit in range(block_bits, high_bit - 1):
            arrived = swapped(values, "col", 2**bit)
            values = jnp.where((col_pos & 2**bit) != 0, arrived, values)
        return values

    def gather(pieces, bit):
        return joined(pieces, [swapped(p, "col", 2**bit) for p in pieces], bit)

    def joined(pieces, arrived, bit):
        second = (col_pos & 2**bit) != 0
        return [
            piece
            for a, b in zip(pieces, arrived)
            for piece in (jnp.where(second, b, a), jnp.where(second, a, b))
        ]

    lead_scale = diag_of(none, none)[1]
    top_parts = halves(top_rows)
    *top_parts, local, remote = lax.optimization_barrier((*top_parts, matrix, partner))
    lead = contribution(top_parts, none, none)
    lead = spread(lead_scale * (lead + swapped(lead, "col", high)))
    mixed = row_diag[0][:, None] * jnp.where(is_first, local + remote, remote - local)
    upper_part, lower_part = mixed[:half], mixed[half:]
    own_rows = jnp.concatenate(
        [
            (0.5 * row_diag[1][:half])[:, None] * (upper_part + lower_part),
            (0.5 * row_diag[1][half:])[:, None] * (upper_part - lower_part),
        ],
        0,
    )

    own_parts = halves(own_rows)
    lead_pieces = [lead]
    for bit in range(block_bits - 1, -1, -1):
        lead_pieces = gather(lead_pieces, bit)

    panel = contribution(own_parts, none, none)
    panel_half = jnp.where(in_low, panel[half:], panel[:half])
    far_half = swapped(panel_half, "col", high)
    sent = jnp.concatenate(
        [contribution(top_parts, ~in_high, in_low), contribution(own_parts, ~in_high, in_low)], 0
    )
    kept = jnp.concatenate([contribution(top_parts, in_high, in_low), contribution(own_parts, in_high, in_low)], 0)
    received = swapped(sent, "col", high)
    vmem = pl.BlockSpec(memory_space=pltpu.VMEM)
    cost = pl.CostEstimate(flops=4_000_000_000, bytes_accessed=12_000_000, transcendentals=0)
    size = 4 * width * (5 * blocks * LEAD + (blocks + 4) * (height + LEAD))
    params = pltpu.CompilerParams(vmem_limit_bytes=2 * size)
    stack = jax.ShapeDtypeStruct((blocks, LEAD, width), jnp.float32)
    state_shapes = (stack, stack, jax.ShapeDtypeStruct((LEAD, width), jnp.float32))
    state = pl.pallas_call(
        first_kernel,
        out_shape=state_shapes,
        in_specs=[vmem] * blocks,
        out_specs=(vmem,) * 3,
        cost_estimate=cost,
        compiler_params=params,
        name="eliminate_0",
    )(*lead_pieces)
    far_half, *state = lax.optimization_barrier((far_half, *state))
    panel_half = lead_scale * (panel_half + far_half)
    other_half = swapped(panel_half, "col", low)
    panel_pieces = []

    for k in range(1, blocks):
        state = pl.pallas_call(
            functools.partial(next_kernel, k),
            out_shape=state_shapes,
            in_specs=[vmem] * 3,
            out_specs=(vmem,) * 3,
            input_output_aliases={0: 0, 1: 1, 2: 2},
            cost_estimate=cost,
            compiler_params=params,
            name=f"eliminate_{k}",
        )(*state)
        bit = block_bits - k + 1
        arrived = [other_half] if k == 1 else [swapped(p, "col", 2**bit) for p in panel_pieces]
        if k == blocks - 1:
            arrived.append(received)
        *arrived, state0, state1, state2 = lax.optimization_barrier((*arrived, *state))
        state = (state0, state1, state2)
        if k == blocks - 1:
            received = arrived.pop()
        if k == 1:
            ordered = jnp.where(in_low, arrived[0], panel_half), jnp.where(in_low, panel_half, arrived[0])
            panel_pieces = [spread(jnp.concatenate(ordered, 0))]
        else:
            panel_pieces = joined(panel_pieces, arrived, bit)

    whole = diag_of(in_high, in_low)[1] * (kept + received)

    info = jnp.stack(
        [
            (col_pos < blocks).astype(jnp.int32),
            jnp.minimum(col_pos, blocks - 1).astype(jnp.int32),
            is_first.astype(jnp.int32),
        ]
    )
    return pl.pallas_call(
        last_kernel,
        out_shape=jax.ShapeDtypeStruct((height, width), jnp.float32),
        in_specs=[pl.BlockSpec(memory_space=pltpu.SMEM)] + [vmem] * (blocks + 5),
        out_specs=vmem,
        scratch_shapes=[pltpu.VMEM((LEAD, width), jnp.float32)] * 3,
        cost_estimate=cost,
        compiler_params=params,
        name="own_columns",
    )(info, *state, whole[:LEAD], whole[LEAD:], *panel_pieces)


def solution(mesh):
    in_specs = (P("row", "col"), P(None, "row"), P(None, "col"))
    out_specs = P("row", "col")
    return jax.shard_map(shards, mesh=mesh, in_specs=in_specs, out_specs=out_specs, check_vma=False)
```

```python
import functools


import jax
import jax.numpy as jnp
from jax import lax
from jax.experimental import pallas as pl
from jax.experimental.pallas import tpu as pltpu
from jax.sharding import PartitionSpec as P

PW = 256
PANELS = 2
LEAD = PW * PANELS
SPLIT = LEAD // 2

SUB = 8
BLK = 128


def swapped(x, axis, mask):
    return lax.ppermute(x, axis, [(i, i ^ mask) for i in range(lax.axis_size(axis))])


def hdot(left, right):
    return jnp.dot(left, right, precision=lax.Precision.HIGHEST, preferred_element_type=jnp.float32)


def tree_sum(terms):
    while len(terms) > 1:
        terms = [terms[i] + terms[i + 1] if i + 1 < len(terms) else terms[i] for i in range(0, len(terms), 2)]
    return terms[0]


def factor(block):
    count = BLK // SUB
    shape = (SUB, BLK)
    sub = lax.broadcasted_iota(jnp.int32, shape, 0)
    lane = lax.broadcasted_iota(jnp.int32, shape, 1)

    def row(x, j):
        return jnp.broadcast_to(x[j : j + 1, :], shape)

    def col(x, j):
        return jnp.broadcast_to(x[:, j : j + 1], shape)

    strips = [block[SUB * i : SUB * (i + 1)] for i in range(count)]
    extra = [jnp.where(lane == sub + SUB * i, 1.0, 0.0) for i in range(count)]
    pending = [jnp.zeros(shape, jnp.float32) for _ in range(count)]
    upper = []
    small = []
    for t in range(count):
        base = SUB * t
        inside = (lane >= base) & (lane < base + SUB)
        for i in range(t, count):
            pending[i] = jnp.where(inside, strips[i], pending[i])
        c = [col(strips[t], base + m) for m in range(SUB)]
        w, x, forward = strips[t], extra[t], strips[t]
        g = jnp.where(lane == sub + base, 1.0, 0.0)
        for j in range(SUB):
            r = 1.0 / row(c[j], j)
            here = sub == j
            cj = c[j]
            for m in range(j + 1, SUB):
                scaled = row(c[m], j) * r
                c[m] = jnp.where(here, scaled, c[m] - cj * scaled)
            scaled = row(w, j) * r
            w = jnp.where(here, scaled, w - cj * scaled)
            scaled = row(x, j) * r
            x = jnp.where(here, scaled, x - cj * scaled)
            scaled = row(g, j) * r
            g = jnp.where(sub > j, g, jnp.where(here, scaled, g - cj * scaled))
            if j < SUB - 1:
                forward = jnp.where(sub > j, forward - (cj * r) * row(forward, j), forward)
        upper.append(forward)
        small.append(g)
        w_rows = [row(w, m) for m in range(SUB)]
        x_rows = [row(x, m) for m in range(SUB)]
        for i in list(range(t + 1, count)) + list(range(t)):
            b = [col(strips[i], base + m) for m in range(SUB)]
            strips[i] = strips[i] - tree_sum([b[m] * w_rows[m] for m in range(SUB)])
            extra[i] = extra[i] - tree_sum([b[m] * x_rows[m] for m in range(SUB)])
        strips[t], extra[t] = w, x
    upper, pending, small, inverse = (jnp.concatenate(v, 0) for v in (upper, pending, small, extra))
    return upper, hdot(pending, small), inverse


def eliminate_block(k, work, packed, inverted):
    blocks = LEAD // BLK
    here = pl.ds(BLK * k, BLK)
    upper, lower, inverse = factor(work[k, here, :])
    size = (BLK, BLK)
    above = lax.broadcasted_iota(jnp.int32, size, 0) <= lax.broadcasted_iota(jnp.int32, size, 1)
    upper = jnp.where(above, upper, 0.0)
    packed[k, here, :] = jnp.where(above, upper, lower)
    upper_inverse = hdot(inverse, lower)
    inverted[here, :] = upper_inverse
    work[k, here, :] = inverse
    later = range(k + 1, blocks)
    solved = {j: hdot(inverse, work[j, here, :]) for j in later}
    if k + 1 < blocks:
        rest = pl.ds(BLK * (k + 1), LEAD - BLK * (k + 1))
        left = work[k, rest, :]
        for j in later:
            work[j, rest, :] = work[j, rest, :] - hdot(left, solved[j])
        packed[k, rest, :] = hdot(left, upper_inverse)
    for j in later:
        packed[j, here, :] = hdot(upper, solved[j])
        work[j, here, :] = solved[j]


def first_kernel(*refs):
    blocks = LEAD // BLK
    pieces, (work, packed, inverted) = refs[:blocks], refs[blocks:]
    for j in range(blocks):
        work[j] = pieces[j][...]
    eliminate_block(0, work, packed, inverted)


def next_kernel(k, old_work, old_packed, old_inverted, work, packed, inverted):
    eliminate_block(k, work, packed, inverted)


def last_kernel(info, work, packed, inverted, own_top, *refs):
    blocks = LEAD // BLK
    own, pieces = refs[:2], refs[2 : 2 + 2 * blocks]
    out, rhs, reduced, top = refs[2 + 2 * blocks :]
    is_panel = info[0] == 1
    slot = info[1]
    is_top = info[2] == 1
    rhs[...] = own_top[...]
    size = (BLK, BLK)
    above = lax.broadcasted_iota(jnp.int32, size, 0) <= lax.broadcasted_iota(jnp.int32, size, 1)
    for k in range(blocks):
        here = pl.ds(BLK * k, BLK)
        solved = hdot(work[k, here, :], rhs[here, :])
        for i in range(k + 1, blocks):
            there = pl.ds(BLK * i, BLK)
            rhs[there, :] = rhs[there, :] - hdot(work[k, there, :], solved)
        upper = jnp.where(above, packed[k, here, :], 0.0)
        top[here, :] = jnp.where(is_panel, packed[slot, here, :], hdot(upper, solved))
        mine = jnp.where(slot == k, inverted[here, :], 0.0)
        reduced[here, :] = jnp.where(is_panel, mine, solved)
    for k in range(blocks - 2, -1, -1):
        here = pl.ds(BLK * k, BLK)
        terms = [hdot(work[j, here, :], reduced[pl.ds(BLK * j, BLK), :]) for j in range(k + 1, blocks)]
        reduced[here, :] = reduced[here, :] - tree_sum(terms)
    part_rows = own[0].shape[0]

    def below(part, first):
        where = pl.ds(first, SPLIT)
        terms = [hdot(pieces[2 * j + part][where, :], reduced[pl.ds(BLK * j, BLK), :]) for j in range(blocks)]
        total = tree_sum(terms)
        return jnp.where(is_panel, total, own[part][where, :] - total)

    for part in range(2):
        where = pl.ds(SPLIT * part, SPLIT)
        out[where, :] = jnp.where(is_top, top[where, :], below(part, 0))

    def step(n, carry):
        for part in range(2):
            first = pl.multiple_of(n * SPLIT, SPLIT)
            out[pl.ds(pl.multiple_of(n * LEAD, LEAD) + SPLIT * part, SPLIT), :] = below(part, first)
        return carry

    if part_rows // SPLIT <= 2:
        for n in range(1, part_rows // SPLIT):
            step(n, 0)
    else:
        lax.fori_loop(1, part_rows // SPLIT, step, 0)


def shards(matrix, row_diag, col_diag):
    height, width = matrix.shape
    row_pos = lax.axis_index("row")
    col_pos = lax.axis_index("col")
    half = height // 2
    blocks = LEAD // width
    block_bits = blocks.bit_length() - 1
    high_bit = lax.axis_size("col").bit_length() - 2
    high, low = 2**high_bit, 2 ** (high_bit - 1)
    is_first = row_pos == 0
    in_high = (col_pos & high) != 0
    in_low = (col_pos & low) != 0
    part_rows = half // 2

    def parts_of(values):
        grouped = values.reshape(2, half // LEAD, 2, SPLIT, *values.shape[1:])
        return [grouped[:, :, p].reshape(2, part_rows, *values.shape[1:]) for p in range(2)]

    rows_p, rows_q = parts_of(matrix)
    other_p = swapped(rows_p, "row", 1)
    near_q = swapped(rows_q, "col", low)
    other_rows = swapped(row_diag, "row", 1)
    pair = jnp.concatenate([col_diag, swapped(col_diag, "col", low)], 0)
    far_pair = swapped(pair, "col", high)

    def diag_of(h, l):
        chosen = jnp.where(in_high == h, pair, far_pair)
        return jnp.where(in_low == l, chosen[:2], chosen[2:])

    none, yes = jnp.bool_(False), jnp.bool_(True)

    def contribution(parts, h, l):
        even, odd = parts
        sign = jnp.where(in_high & h, -0.5, 0.5)
        scale_even = sign * diag_of(h, none)[0]
        scale_odd = jnp.where(l, -sign, sign) * diag_of(h, yes)[0]
        return scale_even * even + scale_odd * odd

    first_diag = jnp.where(is_first, row_diag, other_rows)
    own_scales = [parts_of(row_diag[level]) for level in range(2)]
    first_scales = [parts_of(first_diag[level]) for level in range(2)]

    def own_mixed(part, local, remote):
        scale0, scale1 = own_scales[0][part][..., None], own_scales[1][part][..., None]
        mixed = scale0 * jnp.where(is_first, local + remote, remote - local)
        return 0.5 * scale1[0] * (mixed[0] + mixed[1]), 0.5 * scale1[1] * (mixed[0] - mixed[1])

    def lead_mixed(part, values):
        scale0 = first_scales[0][part][:, :SPLIT, None]
        scale1 = first_scales[1][part][0, :SPLIT, None]
        return 0.5 * scale1 * (scale0[0] * values[0][:SPLIT] + scale0[1] * values[1][:SPLIT])

    even_q = jnp.where(in_low, near_q, rows_q)
    odd_q = jnp.where(in_low, rows_q, near_q)
    lead_own = lead_mixed(0, [rows_p[i, :SPLIT] + other_p[i, :SPLIT] for i in range(2)])
    lead_own = (0.5 * diag_of(none, in_low)[0]) * lead_own
    lead_near = lead_mixed(1, contribution((even_q[:, :SPLIT], odd_q[:, :SPLIT]), none, none))
    lead_p = lead_own + swapped(lead_own, "col", low)
    lead_q = lead_near + swapped(lead_near, "row", 1)
    lead = jnp.concatenate([lead_p, lead_q], 0)
    lead, rows_p, other_p, even_q, odd_q = lax.optimization_barrier((lead, rows_p, other_p, even_q, odd_q))

    def spread(values):
        for bit in range(block_bits, high_bit - 1):
            arrived = swapped(values, "col", 2**bit)
            values = jnp.where((col_pos & 2**bit) != 0, arrived, values)
        return values

    def gather(pieces, bit):
        return joined(pieces, [swapped(p, "col", 2**bit) for p in pieces], bit)

    def joined(pieces, arrived, bit):
        second = (col_pos & 2**bit) != 0
        return [
            piece
            for a, b in zip(pieces, arrived)
            for piece in (jnp.where(second, b, a), jnp.where(second, a, b))
        ]

    lead_scale = diag_of(none, none)[1]
    far_lead = swapped(lead, "col", high)
    lead_pieces = [spread(lead_scale * (lead + far_lead))]
    for bit in range(block_bits - 1, -1, -1):
        lead_pieces = gather(lead_pieces, bit)

    own_p = jnp.stack(own_mixed(0, rows_p, other_p))
    near_p = swapped(own_p, "col", low)
    even_p = jnp.where(in_low, near_p, own_p)
    odd_p = jnp.where(in_low, own_p, near_p)
    other_even, other_odd = swapped(even_q, "row", 1), swapped(odd_q, "row", 1)
    even_q = jnp.stack(own_mixed(1, even_q, other_even))
    odd_q = jnp.stack(own_mixed(1, odd_q, other_odd))
    flat = lambda values: values.reshape(2 * part_rows, width)
    both = [(flat(even_p), flat(odd_p)), (flat(even_q), flat(odd_q))]

    mine = [jnp.where(in_low, q, p) for p, q in zip(*both)]
    panel_half = contribution(mine, none, none)
    far_half = swapped(panel_half, "col", high)
    received = [swapped(contribution(v, ~in_high, in_low), "col", high) for v in both]
    kept = [contribution(v, in_high, in_low) for v in both]

    vmem = pl.BlockSpec(memory_space=pltpu.VMEM)
    cost = pl.CostEstimate(flops=4_000_000_000, bytes_accessed=12_000_000, transcendentals=0)
    size = 4 * width * (5 * blocks * LEAD + (blocks + 4) * (height + LEAD))
    params = pltpu.CompilerParams(vmem_limit_bytes=2 * size)
    stack = jax.ShapeDtypeStruct((blocks, LEAD, width), jnp.float32)
    state_shapes = (stack, stack, jax.ShapeDtypeStruct((LEAD, width), jnp.float32))
    state = pl.pallas_call(
        first_kernel,
        out_shape=state_shapes,
        in_specs=[vmem] * blocks,
        out_specs=(vmem,) * 3,
        cost_estimate=cost,
        compiler_params=params,
        name="eliminate_0",
    )(*lead_pieces)
    far_half, *state = lax.optimization_barrier((far_half, *state))
    panel_half = lead_scale * (panel_half + far_half)
    other_half = swapped(panel_half, "col", low)
    panel_pieces = []
    own_top = own_parts = None

    for k in range(1, blocks):
        state = pl.pallas_call(
            functools.partial(next_kernel, k),
            out_shape=state_shapes,
            in_specs=[vmem] * 3,
            out_specs=(vmem,) * 3,
            input_output_aliases={0: 0, 1: 1, 2: 2},
            cost_estimate=cost,
            compiler_params=params,
        )(*state)
        bit = block_bits - k + 1
        arrived = [other_half] if k == 1 else [swapped(p, "col", 2**bit) for p in panel_pieces]
        count = len(arrived)
        if k == blocks - 2:
            arrived += received
        if k == blocks - 1:
            arrived += [far_top]
        *arrived, state0, state1, state2 = lax.optimization_barrier((*arrived, *state))
        state = (state0, state1, state2)
        arrived, extra = arrived[:count], arrived[count:]
        if k == blocks - 2:
            scale = diag_of(in_high, in_low)[1]
            own_parts = [scale * (a + b) for a, b in zip(kept, extra)]
            own_top = jnp.concatenate([v[:SPLIT] for v in own_parts], 0)
            far_top = lax.ppermute(own_top, "row", [(0, 1)])
        if k == blocks - 1:
            own_top = jnp.where(is_first, own_top, extra[0])
        if k == 1:
            panel_pieces = [
                spread(jnp.where(in_low, arrived[0], panel_half)),
                spread(jnp.where(in_low, panel_half, arrived[0])),
            ]
        else:
            first = joined(panel_pieces[0::2], arrived[0::2], bit)
            second = joined(panel_pieces[1::2], arrived[1::2], bit)
            panel_pieces = [v for pq in zip(first, second) for v in pq]

    info = jnp.stack(
        [
            (col_pos < blocks).astype(jnp.int32),
            jnp.minimum(col_pos, blocks - 1).astype(jnp.int32),
            is_first.astype(jnp.int32),
        ]
    )
    return pl.pallas_call(
        last_kernel,
        out_shape=jax.ShapeDtypeStruct((height, width), jnp.float32),
        in_specs=[pl.BlockSpec(memory_space=pltpu.SMEM)] + [vmem] * (2 * blocks + 6),
        out_specs=vmem,
        scratch_shapes=[pltpu.VMEM((LEAD, width), jnp.float32)] * 3,
        cost_estimate=cost,
        compiler_params=params,
        name="own_columns",
    )(info, *state, own_top, *own_parts, *panel_pieces)


def solution(mesh):
    in_specs = (P("row", "col"), P(None, "row"), P(None, "col"))
    out_specs = P("row", "col")

    return jax.shard_map(shards, mesh=mesh, in_specs=in_specs, out_specs=out_specs, check_vma=False)
```

```python
import functools


import jax
import jax.numpy as jnp
from jax import lax
from jax.experimental import pallas as pl
from jax.experimental.pallas import tpu as pltpu
from jax.sharding import PartitionSpec as P

PW = 256
PANELS = 2
LEAD = PW * PANELS
SPLIT = LEAD // 2

SUB = 8
BLK = 128


def swapped(x, axis, mask):
    return lax.ppermute(x, axis, [(i, i ^ mask) for i in range(lax.axis_size(axis))])


def hdot(left, right):
    return jnp.dot(left, right, precision=lax.Precision.HIGHEST, preferred_element_type=jnp.float32)


def tree_sum(terms):
    while len(terms) > 1:
        terms = [terms[i] + terms[i + 1] if i + 1 < len(terms) else terms[i] for i in range(0, len(terms), 2)]
    return terms[0]


def factor(block):
    count = BLK // SUB
    shape = (SUB, BLK)
    sub = lax.broadcasted_iota(jnp.int32, shape, 0)
    lane = lax.broadcasted_iota(jnp.int32, shape, 1)

    def row(x, j):
        return jnp.broadcast_to(x[j : j + 1, :], shape)

    def col(x, j):
        return jnp.broadcast_to(x[:, j : j + 1], shape)

    strips = [block[SUB * i : SUB * (i + 1)] for i in range(count)]
    extra = [jnp.where(lane == sub + SUB * i, 1.0, 0.0) for i in range(count)]
    pending = [jnp.zeros(shape, jnp.float32) for _ in range(count)]
    upper = []
    small = []
    for t in range(count):
        base = SUB * t
        inside = (lane >= base) & (lane < base + SUB)
        for i in range(t, count):
            pending[i] = jnp.where(inside, strips[i], pending[i])
        c = [col(strips[t], base + m) for m in range(SUB)]
        w, x, forward = strips[t], extra[t], strips[t]
        g = jnp.where(lane == sub + base, 1.0, 0.0)
        for j in range(SUB):
            r = 1.0 / row(c[j], j)
            here = sub == j
            cj = c[j]
            for m in range(j + 1, SUB):
                scaled = row(c[m], j) * r
                c[m] = jnp.where(here, scaled, c[m] - cj * scaled)
            scaled = row(w, j) * r
            w = jnp.where(here, scaled, w - cj * scaled)
            scaled = row(x, j) * r
            x = jnp.where(here, scaled, x - cj * scaled)
            scaled = row(g, j) * r
            g = jnp.where(sub > j, g, jnp.where(here, scaled, g - cj * scaled))
            if j < SUB - 1:
                forward = jnp.where(sub > j, forward - (cj * r) * row(forward, j), forward)
        upper.append(forward)
        small.append(g)
        w_rows = [row(w, m) for m in range(SUB)]
        x_rows = [row(x, m) for m in range(SUB)]
        for i in list(range(t + 1, count)) + list(range(t)):
            b = [col(strips[i], base + m) for m in range(SUB)]
            strips[i] = strips[i] - tree_sum([b[m] * w_rows[m] for m in range(SUB)])
            extra[i] = extra[i] - tree_sum([b[m] * x_rows[m] for m in range(SUB)])
        strips[t], extra[t] = w, x
    upper, pending, small, inverse = (jnp.concatenate(v, 0) for v in (upper, pending, small, extra))
    return upper, hdot(pending, small), inverse


def eliminate_block(k, work, packed, inverted):
    blocks = LEAD // BLK
    here = pl.ds(BLK * k, BLK)
    upper, lower, inverse = factor(work[k, here, :])
    size = (BLK, BLK)
    above = lax.broadcasted_iota(jnp.int32, size, 0) <= lax.broadcasted_iota(jnp.int32, size, 1)
    upper = jnp.where(above, upper, 0.0)
    packed[k, here, :] = jnp.where(above, upper, lower)
    upper_inverse = hdot(inverse, lower)
    inverted[here, :] = upper_inverse
    work[k, here, :] = inverse
    later = range(k + 1, blocks)
    solved = {j: hdot(inverse, work[j, here, :]) for j in later}
    if k + 1 < blocks:
        rest = pl.ds(BLK * (k + 1), LEAD - BLK * (k + 1))
        left = work[k, rest, :]
        for j in later:
            work[j, rest, :] = work[j, rest, :] - hdot(left, solved[j])
        packed[k, rest, :] = hdot(left, upper_inverse)
    for j in later:
        packed[j, here, :] = hdot(upper, solved[j])
        work[j, here, :] = solved[j]


def first_kernel(*refs):
    blocks = LEAD // BLK
    pieces, (work, packed, inverted) = refs[:blocks], refs[blocks:]
    for j in range(blocks):
        work[j] = pieces[j][...]
    eliminate_block(0, work, packed, inverted)


def next_kernel(k, old_work, old_packed, old_inverted, work, packed, inverted):
    eliminate_block(k, work, packed, inverted)


def last_kernel(info, work, packed, inverted, own_top, *refs):
    blocks = LEAD // BLK
    own, pieces = refs[:2], refs[2 : 2 + 2 * blocks]
    out, rhs, reduced, top = refs[2 + 2 * blocks :]
    is_panel = info[0] == 1
    slot = info[1]
    is_top = info[2] == 1
    rhs[...] = own_top[...]
    size = (BLK, BLK)
    above = lax.broadcasted_iota(jnp.int32, size, 0) <= lax.broadcasted_iota(jnp.int32, size, 1)
    for k in range(blocks):
        here = pl.ds(BLK * k, BLK)
        solved = hdot(work[k, here, :], rhs[here, :])
        for i in range(k + 1, blocks):
            there = pl.ds(BLK * i, BLK)
            rhs[there, :] = rhs[there, :] - hdot(work[k, there, :], solved)
        upper = jnp.where(above, packed[k, here, :], 0.0)
        top[here, :] = jnp.where(is_panel, packed[slot, here, :], hdot(upper, solved))
        mine = jnp.where(slot == k, inverted[here, :], 0.0)
        reduced[here, :] = jnp.where(is_panel, mine, solved)
    for k in range(blocks - 2, -1, -1):
        here = pl.ds(BLK * k, BLK)
        terms = [hdot(work[j, here, :], reduced[pl.ds(BLK * j, BLK), :]) for j in range(k + 1, blocks)]
        reduced[here, :] = reduced[here, :] - tree_sum(terms)
    quarter_runs = own[0].shape[1] // SPLIT

    def below(part, run, quarter, inner):
        where = pl.ds(pl.multiple_of(run * SPLIT, SPLIT), SPLIT)
        local = pl.ds(pl.multiple_of(inner * SPLIT, SPLIT), SPLIT)
        terms = [hdot(pieces[2 * j + part][where, :], reduced[pl.ds(BLK * j, BLK), :]) for j in range(blocks)]
        total = tree_sum(terms)
        return jnp.where(is_panel, total, own[quarter][part, local, :] - total)

    for part in range(2):
        where = pl.ds(SPLIT * part, SPLIT)
        out[where, :] = jnp.where(is_top, top[where, :], below(part, 0, 0, 0))

    def step(quarter, inner):
        run = quarter * quarter_runs + inner
        for part in range(2):
            rows = pl.ds(pl.multiple_of(run * LEAD, LEAD) + SPLIT * part, SPLIT)
            out[rows, :] = below(part, run, quarter, inner)

    for quarter in range(2):
        start = 1 - quarter
        if quarter_runs - start <= 2:
            for inner in range(start, quarter_runs):
                step(quarter, inner)
        else:
            pl.loop(start, quarter_runs)(functools.partial(step, quarter))


def shards(matrix, row_diag, col_diag):
    height, width = matrix.shape
    row_pos = lax.axis_index("row")
    col_pos = lax.axis_index("col")
    half = height // 2
    blocks = LEAD // width
    block_bits = blocks.bit_length() - 1
    high_bit = lax.axis_size("col").bit_length() - 2
    high, low = 2**high_bit, 2 ** (high_bit - 1)
    is_first = row_pos == 0
    in_high = (col_pos & high) != 0
    in_low = (col_pos & low) != 0
    part_rows = half // 2

    def parts_of(values):
        grouped = values.reshape(2, half // LEAD, 2, SPLIT, *values.shape[1:])
        return [grouped[:, :, p].reshape(2, part_rows, *values.shape[1:]) for p in range(2)]

    rows_p, rows_q = parts_of(matrix)
    other_p = swapped(rows_p, "row", 1)
    near_q = swapped(rows_q, "col", low)
    other_rows = swapped(row_diag, "row", 1)
    pair = jnp.concatenate([col_diag, swapped(col_diag, "col", low)], 0)
    far_pair = swapped(pair, "col", high)

    def diag_of(h, l):
        chosen = jnp.where(in_high == h, pair, far_pair)
        return jnp.where(in_low == l, chosen[:2], chosen[2:])

    none, yes = jnp.bool_(False), jnp.bool_(True)

    def contribution(parts, h, l):
        even, odd = parts
        sign = jnp.where(in_high & h, -0.5, 0.5)
        scale_even = sign * diag_of(h, none)[0]
        scale_odd = jnp.where(l, -sign, sign) * diag_of(h, yes)[0]
        return scale_even * even + scale_odd * odd

    first_diag = jnp.where(is_first, row_diag, other_rows)
    own_scales = [parts_of(row_diag[level]) for level in range(2)]
    first_scales = [parts_of(first_diag[level]) for level in range(2)]

    def own_mixed(part, local, remote):
        scale0, scale1 = own_scales[0][part][..., None], own_scales[1][part][..., None]
        mixed = scale0 * jnp.where(is_first, local + remote, remote - local)
        return 0.5 * scale1[0] * (mixed[0] + mixed[1]), 0.5 * scale1[1] * (mixed[0] - mixed[1])

    def lead_mixed(part, values):
        scale0 = first_scales[0][part][:, :SPLIT, None]
        scale1 = first_scales[1][part][0, :SPLIT, None]
        return 0.5 * scale1 * (scale0[0] * values[0][:SPLIT] + scale0[1] * values[1][:SPLIT])

    even_q = jnp.where(in_low, near_q, rows_q)
    odd_q = jnp.where(in_low, rows_q, near_q)
    lead_own = lead_mixed(0, [rows_p[i, :SPLIT] + other_p[i, :SPLIT] for i in range(2)])
    lead_own = (0.5 * diag_of(none, in_low)[0]) * lead_own
    lead_near = lead_mixed(1, contribution((even_q[:, :SPLIT], odd_q[:, :SPLIT]), none, none))
    lead_p = lead_own + swapped(lead_own, "col", low)
    lead_q = lead_near + swapped(lead_near, "row", 1)
    lead = jnp.concatenate([lead_p, lead_q], 0)

    def spread(values):
        for bit in range(block_bits, high_bit - 1):
            arrived = swapped(values, "col", 2**bit)
            values = jnp.where((col_pos & 2**bit) != 0, arrived, values)
        return values

    def gather(pieces, bit):
        return joined(pieces, [swapped(p, "col", 2**bit) for p in pieces], bit)

    def joined(pieces, arrived, bit):
        second = (col_pos & 2**bit) != 0
        return [
            piece
            for a, b in zip(pieces, arrived)
            for piece in (jnp.where(second, b, a), jnp.where(second, a, b))
        ]

    lead_scale = diag_of(none, none)[1]
    far_lead = swapped(lead, "col", high)
    lead_pieces = [spread(lead_scale * (lead + far_lead))]
    for bit in range(block_bits - 1, -1, -1):
        lead_pieces = gather(lead_pieces, bit)

    own_p = jnp.stack(own_mixed(0, rows_p, other_p))
    near_p = swapped(own_p, "col", low)
    even_p = jnp.where(in_low, near_p, own_p)
    odd_p = jnp.where(in_low, own_p, near_p)
    other_even, other_odd = swapped(even_q, "row", 1), swapped(odd_q, "row", 1)
    even_q = jnp.stack(own_mixed(1, even_q, other_even))
    odd_q = jnp.stack(own_mixed(1, odd_q, other_odd))
    flat = lambda values: values.reshape(2 * part_rows, width)
    both = [(flat(even_p), flat(odd_p)), (flat(even_q), flat(odd_q))]

    mine = [jnp.where(in_low, q, p) for p, q in zip(*both)]
    panel_half = contribution(mine, none, none)
    far_half = swapped(panel_half, "col", high)
    both, far_half, *lead_pieces = lax.optimization_barrier((both, far_half, *lead_pieces))
    panel_half = lead_scale * (panel_half + far_half)
    other_half = swapped(panel_half, "col", low)

    def quarter(values, n):
        return jnp.stack([v[n * part_rows : (n + 1) * part_rows] for v in values])

    sent = [quarter([contribution(v, ~in_high, in_low) for v in both], n) for n in range(2)]
    kept = [quarter([contribution(v, in_high, in_low) for v in both], n) for n in range(2)]
    received_lead = swapped(sent[0], "col", high)

    vmem = pl.BlockSpec(memory_space=pltpu.VMEM)
    cost = pl.CostEstimate(flops=4_000_000_000, bytes_accessed=12_000_000, transcendentals=0)
    size = 4 * width * (5 * blocks * LEAD + (blocks + 4) * (height + LEAD))
    params = pltpu.CompilerParams(vmem_limit_bytes=2 * size)
    stack = jax.ShapeDtypeStruct((blocks, LEAD, width), jnp.float32)
    state_shapes = (stack, stack, jax.ShapeDtypeStruct((LEAD, width), jnp.float32))
    state = pl.pallas_call(
        first_kernel,
        out_shape=state_shapes,
        in_specs=[vmem] * blocks,
        out_specs=(vmem,) * 3,
        cost_estimate=cost,
        compiler_params=params,
        name="eliminate_0",
    )(*lead_pieces)
    other_half, rest, *state = lax.optimization_barrier((other_half, sent[1], *state))
    panel_pieces = [
        spread(jnp.where(in_low, other_half, panel_half)),
        spread(jnp.where(in_low, panel_half, other_half)),
    ]
    received_rest = swapped(rest, "col", high)
    scale = diag_of(in_high, in_low)[1]
    own_lead = own_rest = own_top = None

    for k in range(1, blocks):
        arrived = []
        bit = block_bits - k
        if bit >= 0:
            arrived = [swapped(p, "col", 2**bit) for p in panel_pieces]
        state = pl.pallas_call(
            functools.partial(next_kernel, k),
            out_shape=state_shapes,
            in_specs=[vmem] * 3,
            out_specs=(vmem,) * 3,
            input_output_aliases={0: 0, 1: 1, 2: 2},
            cost_estimate=cost,
            compiler_params=params,
        )(*state)
        if k == 1:
            *arrived, received_lead, state0, state1, state2 = lax.optimization_barrier(
                (*arrived, received_lead, *state)
            )
            own_lead = scale * (kept[0] + received_lead)
            own_top = own_lead[:, :SPLIT].reshape(LEAD, width)
            far_top = lax.ppermute(own_top, "row", [(0, 1)])
        elif k == blocks - 1:
            *arrived, far_top, received_rest, state0, state1, state2 = lax.optimization_barrier(
                (*arrived, far_top, received_rest, *state)
            )
            own_rest = scale * (kept[1] + received_rest)
            own_top = jnp.where(is_first, own_top, far_top)
        else:
            *arrived, state0, state1, state2 = lax.optimization_barrier((*arrived, *state))
        state = (state0, state1, state2)
        if bit >= 0:
            first = joined(panel_pieces[0::2], arrived[0::2], bit)
            second = joined(panel_pieces[1::2], arrived[1::2], bit)
            panel_pieces = [v for pq in zip(first, second) for v in pq]

    info = jnp.stack(
        [
            (col_pos < blocks).astype(jnp.int32),
            jnp.minimum(col_pos, blocks - 1).astype(jnp.int32),
            is_first.astype(jnp.int32),
        ]
    )
    return pl.pallas_call(
        last_kernel,
        out_shape=jax.ShapeDtypeStruct((height, width), jnp.float32),
        in_specs=[pl.BlockSpec(memory_space=pltpu.SMEM)] + [vmem] * (2 * blocks + 6),
        out_specs=vmem,
        scratch_shapes=[pltpu.VMEM((LEAD, width), jnp.float32)] * 3,
        cost_estimate=cost,
        compiler_params=params,
        name="own_columns",
    )(info, *state, own_top, own_lead, own_rest, *panel_pieces)


def solution(mesh):
    in_specs = (P("row", "col"), P(None, "row"), P(None, "col"))
    out_specs = P("row", "col")

    return jax.shard_map(shards, mesh=mesh, in_specs=in_specs, out_specs=out_specs, check_vma=False)
```

```python
import functools


import jax
import jax.numpy as jnp
from jax import lax
from jax.experimental import pallas as pl
from jax.experimental.pallas import tpu as pltpu
from jax.sharding import PartitionSpec as P

PW = 256
PANELS = 2
LEAD = PW * PANELS
SPLIT = LEAD // 2

SUB = 8
BLK = 128


def swapped(x, axis, mask):
    return lax.ppermute(x, axis, [(i, i ^ mask) for i in range(lax.axis_size(axis))])


def hdot(left, right):
    return jnp.dot(left, right, precision=lax.Precision.HIGHEST, preferred_element_type=jnp.float32)


def tree_sum(terms):
    while len(terms) > 1:
        terms = [terms[i] + terms[i + 1] if i + 1 < len(terms) else terms[i] for i in range(0, len(terms), 2)]
    return terms[0]


def factor(block):
    count = BLK // SUB
    shape = (SUB, BLK)
    sub = lax.broadcasted_iota(jnp.int32, shape, 0)
    lane = lax.broadcasted_iota(jnp.int32, shape, 1)

    def row(x, j):
        return jnp.broadcast_to(x[j : j + 1, :], shape)

    def col(x, j):
        return jnp.broadcast_to(x[:, j : j + 1], shape)

    strips = [block[SUB * i : SUB * (i + 1)] for i in range(count)]
    extra = [jnp.where(lane == sub + SUB * i, 1.0, 0.0) for i in range(count)]
    pending = [jnp.zeros(shape, jnp.float32) for _ in range(count)]
    upper = []
    small = []
    for t in range(count):
        base = SUB * t
        inside = (lane >= base) & (lane < base + SUB)
        for i in range(t, count):
            pending[i] = jnp.where(inside, strips[i], pending[i])
        c = [col(strips[t], base + m) for m in range(SUB)]
        w, x, forward = strips[t], extra[t], strips[t]
        g = jnp.where(lane == sub + base, 1.0, 0.0)
        for j in range(SUB):
            r = 1.0 / row(c[j], j)
            here = sub == j
            cj = c[j]
            for m in range(j + 1, SUB):
                scaled = row(c[m], j) * r
                c[m] = jnp.where(here, scaled, c[m] - cj * scaled)
            scaled = row(w, j) * r
            w = jnp.where(here, scaled, w - cj * scaled)
            scaled = row(x, j) * r
            x = jnp.where(here, scaled, x - cj * scaled)
            scaled = row(g, j) * r
            g = jnp.where(sub > j, g, jnp.where(here, scaled, g - cj * scaled))
            if j < SUB - 1:
                forward = jnp.where(sub > j, forward - (cj * r) * row(forward, j), forward)
        upper.append(forward)
        small.append(g)
        w_rows = [row(w, m) for m in range(SUB)]
        x_rows = [row(x, m) for m in range(SUB)]
        for i in list(range(t + 1, count)) + list(range(t)):
            b = [col(strips[i], base + m) for m in range(SUB)]
            strips[i] = strips[i] - tree_sum([b[m] * w_rows[m] for m in range(SUB)])
            extra[i] = extra[i] - tree_sum([b[m] * x_rows[m] for m in range(SUB)])
        strips[t], extra[t] = w, x
    upper, pending, small, inverse = (jnp.concatenate(v, 0) for v in (upper, pending, small, extra))
    return upper, hdot(pending, small), inverse


def eliminate_block(k, work, packed, inverted):
    blocks = LEAD // BLK
    here = pl.ds(BLK * k, BLK)
    upper, lower, inverse = factor(work[k, here, :])
    size = (BLK, BLK)
    above = lax.broadcasted_iota(jnp.int32, size, 0) <= lax.broadcasted_iota(jnp.int32, size, 1)
    upper = jnp.where(above, upper, 0.0)
    packed[k, here, :] = jnp.where(above, upper, lower)
    upper_inverse = hdot(inverse, lower)
    inverted[here, :] = upper_inverse
    work[k, here, :] = inverse
    later = range(k + 1, blocks)
    solved = {j: hdot(inverse, work[j, here, :]) for j in later}
    if k + 1 < blocks:
        rest = pl.ds(BLK * (k + 1), LEAD - BLK * (k + 1))
        left = work[k, rest, :]
        for j in later:
            work[j, rest, :] = work[j, rest, :] - hdot(left, solved[j])
        packed[k, rest, :] = hdot(left, upper_inverse)
    for j in later:
        packed[j, here, :] = hdot(upper, solved[j])
        work[j, here, :] = solved[j]


def first_kernel(info, *refs):
    blocks = LEAD // BLK
    pieces, (work, packed, inverted) = refs[:blocks], refs[blocks:]
    for n in range(blocks):
        work[info[3] ^ n] = pieces[n][...]
    eliminate_block(0, work, packed, inverted)


def next_kernel(k, old_work, old_packed, old_inverted, work, packed, inverted):
    eliminate_block(k, work, packed, inverted)


def last_kernel(info, work, packed, inverted, own_top, *refs):
    blocks = LEAD // BLK
    own, pieces = refs[:2], refs[2 : 2 + 2 * blocks]
    out, rhs, reduced, top = refs[2 + 2 * blocks :]
    is_panel = info[0] == 1
    slot = info[1]
    is_top = info[2] == 1
    rhs[...] = own_top[...]
    size = (BLK, BLK)
    above = lax.broadcasted_iota(jnp.int32, size, 0) <= lax.broadcasted_iota(jnp.int32, size, 1)
    for k in range(blocks):
        here = pl.ds(BLK * k, BLK)
        solved = hdot(work[k, here, :], rhs[here, :])
        for i in range(k + 1, blocks):
            there = pl.ds(BLK * i, BLK)
            rhs[there, :] = rhs[there, :] - hdot(work[k, there, :], solved)
        upper = jnp.where(above, packed[k, here, :], 0.0)
        top[here, :] = jnp.where(is_panel, packed[slot, here, :], hdot(upper, solved))
        mine = jnp.where(slot == k, inverted[here, :], 0.0)
        reduced[here, :] = jnp.where(is_panel, mine, solved)
    for k in range(blocks - 2, -1, -1):
        here = pl.ds(BLK * k, BLK)
        terms = [hdot(work[j, here, :], reduced[pl.ds(BLK * j, BLK), :]) for j in range(k + 1, blocks)]
        reduced[here, :] = reduced[here, :] - tree_sum(terms)
    runs = pieces[0].shape[0] // SPLIT

    def below(part, run):
        where = pl.ds(pl.multiple_of(run * SPLIT, SPLIT), SPLIT)
        terms = []
        for n in range(blocks):
            block = pl.ds(pl.multiple_of((info[3] ^ n) * BLK, BLK), BLK)
            terms.append(hdot(pieces[2 * n + part][where, :], reduced[block, :]))
        total = tree_sum(terms)
        return jnp.where(is_panel, total, own[part][where, :] - total)

    for part in range(2):
        where = pl.ds(SPLIT * part, SPLIT)
        out[where, :] = jnp.where(is_top, top[where, :], below(part, 0))

    def step(run):
        for part in range(2):
            rows = pl.ds(pl.multiple_of(run * LEAD, LEAD) + SPLIT * part, SPLIT)
            out[rows, :] = below(part, run)

    if runs <= 2:
        for run in range(1, runs):
            step(run)
    else:
        pl.loop(1, runs)(step)


def shards(matrix, row_diag, col_diag):
    height, width = matrix.shape
    row_pos = lax.axis_index("row")
    col_pos = lax.axis_index("col")
    half = height // 2
    blocks = LEAD // width
    block_bits = blocks.bit_length() - 1
    high_bit = lax.axis_size("col").bit_length() - 2
    high, low = 2**high_bit, 2 ** (high_bit - 1)
    is_first = row_pos == 0
    in_high = (col_pos & high) != 0
    in_low = (col_pos & low) != 0
    part_rows = half // 2

    def parts_of(values):
        grouped = values.reshape(2, half // LEAD, 2, SPLIT, *values.shape[1:])
        return [grouped[:, :, p].reshape(2, part_rows, *values.shape[1:]) for p in range(2)]

    rows_p, rows_q = parts_of(matrix)
    other_p = swapped(rows_p, "row", 1)
    far_q = swapped(rows_q, "col", high)
    other_rows = swapped(row_diag, "row", 1)
    pair = jnp.concatenate([col_diag, swapped(col_diag, "col", low)], 0)
    far_pair = swapped(pair, "col", high)

    def diag_of(h, l):
        chosen = jnp.where(in_high == h, pair, far_pair)
        return jnp.where(in_low == l, chosen[:2], chosen[2:])

    none, yes = jnp.bool_(False), jnp.bool_(True)

    def of_half(parts, h, l):
        even, odd = parts
        sign = jnp.where(in_high & h, -0.5, 0.5)
        scale_even = sign * diag_of(h, none)[0]
        scale_odd = jnp.where(l, -sign, sign) * diag_of(h, yes)[0]
        return scale_even * even + scale_odd * odd

    def of_bit(parts, h, l):
        scale = jnp.where(in_low & l, -0.5, 0.5) * diag_of(h, in_low)[0]
        return scale * (parts[0] + jnp.where(h, -parts[1], parts[1]))

    first_diag = jnp.where(is_first, row_diag, other_rows)
    own_scales = [parts_of(row_diag[level]) for level in range(2)]
    first_scales = [parts_of(first_diag[level]) for level in range(2)]

    def own_mixed(part, local, remote):
        scale0, scale1 = own_scales[0][part][..., None], own_scales[1][part][..., None]
        mixed = scale0 * jnp.where(is_first, local + remote, remote - local)
        return 0.5 * scale1[0] * (mixed[0] + mixed[1]), 0.5 * scale1[1] * (mixed[0] - mixed[1])

    def lead_mixed(part, values):
        scale0 = first_scales[0][part][:, :SPLIT, None]
        scale1 = first_scales[1][part][0, :SPLIT, None]
        return 0.5 * scale1 * (scale0[0] * values[0][:SPLIT] + scale0[1] * values[1][:SPLIT])

    first_q = jnp.where(in_high, far_q, rows_q)
    second_q = jnp.where(in_high, rows_q, far_q)
    lead_own = lead_mixed(0, [rows_p[i, :SPLIT] + other_p[i, :SPLIT] for i in range(2)])
    lead_own = (0.5 * diag_of(none, in_low)[0]) * lead_own
    lead_bit = lead_mixed(1, of_bit((first_q[:, :SPLIT], second_q[:, :SPLIT]), none, none))
    lead_p = lead_own + swapped(lead_own, "col", low)
    lead_q = lead_bit + swapped(lead_bit, "row", 1)
    far_lead = swapped(lead_p, "col", high)
    near_lead = swapped(lead_q, "col", low)

    def spread(values):
        for bit in range(block_bits, high_bit - 1):
            arrived = swapped(values, "col", 2**bit)
            values = jnp.where((col_pos & 2**bit) != 0, arrived, values)
        return values

    def gather(values):
        pieces = {0: values}
        for bit in range(block_bits - 1, -1, -1):
            for n in sorted(pieces):
                pieces[n ^ 2**bit] = swapped(pieces[n], "col", 2**bit)
        return [pieces[n] for n in range(blocks)]

    lead_scale = diag_of(none, none)[1]
    lead = lead_scale * jnp.concatenate([lead_p + far_lead, lead_q + near_lead], 0)
    lead_pieces = gather(spread(lead))

    own_p = jnp.stack(own_mixed(0, rows_p, other_p))
    near_p = swapped(own_p, "col", low)
    other_q = swapped(first_q, "row", 1), swapped(second_q, "row", 1)

    def flat(values):
        return values.reshape(2 * part_rows, width)

    parts_p = flat(jnp.where(in_low, near_p, own_p)), flat(jnp.where(in_low, own_p, near_p))
    parts_q = [flat(jnp.stack(own_mixed(1, a, b))) for a, b in zip((first_q, second_q), other_q)]
    panel_p = of_half(parts_p, none, none)
    panel_q = of_bit(parts_q, none, none)
    far_p = swapped(panel_p, "col", high)
    near_q = swapped(panel_q, "col", low)

    info = jnp.stack(
        [
            (col_pos < blocks).astype(jnp.int32),
            jnp.minimum(col_pos, blocks - 1).astype(jnp.int32),
            is_first.astype(jnp.int32),
            (col_pos & (blocks - 1)).astype(jnp.int32),
        ]
    )
    smem = pl.BlockSpec(memory_space=pltpu.SMEM)
    vmem = pl.BlockSpec(memory_space=pltpu.VMEM)
    cost = pl.CostEstimate(flops=4_000_000_000, bytes_accessed=12_000_000, transcendentals=0)
    size = 4 * width * (5 * blocks * LEAD + (blocks + 4) * (height + LEAD))
    params = pltpu.CompilerParams(vmem_limit_bytes=2 * size)
    stack = jax.ShapeDtypeStruct((blocks, LEAD, width), jnp.float32)
    state_shapes = (stack, stack, jax.ShapeDtypeStruct((LEAD, width), jnp.float32))
    state = pl.pallas_call(
        first_kernel,
        out_shape=state_shapes,
        in_specs=[smem] + [vmem] * blocks,
        out_specs=(vmem,) * 3,
        cost_estimate=cost,
        compiler_params=params,
        name="eliminate_0",
    )(info, *lead_pieces)
    far_p, near_q, parts_p, parts_q, *state = lax.optimization_barrier((far_p, near_q, parts_p, parts_q, *state))
    pieces_p = gather(spread(lead_scale * (panel_p + far_p)))
    pieces_q = gather(spread(lead_scale * (panel_q + near_q)))
    kept_p, kept_q = of_half(parts_p, in_high, in_low), of_bit(parts_q, in_high, in_low)
    received_p = swapped(of_half(parts_p, ~in_high, in_low), "col", high)
    received_q = swapped(of_bit(parts_q, in_high, ~in_low), "col", low)
    scale = diag_of(in_high, in_low)[1]

    for k in range(1, blocks):
        state = pl.pallas_call(
            functools.partial(next_kernel, k),
            out_shape=state_shapes,
            in_specs=[vmem] * 3,
            out_specs=(vmem,) * 3,
            input_output_aliases={0: 0, 1: 1, 2: 2},
            cost_estimate=cost,
            compiler_params=params,
        )(*state)
        if k == blocks - 2:
            received_p, received_q, *state = lax.optimization_barrier((received_p, received_q, *state))
            own = scale * (kept_p + received_p), scale * (kept_q + received_q)
            own_top = jnp.concatenate([v[:SPLIT] for v in own], 0)
            far_top = lax.ppermute(own_top, "row", [(0, 1)])
    far_top, *state = lax.optimization_barrier((far_top, *state))
    own_top = jnp.where(is_first, own_top, far_top)
    panel_pieces = [v for pq in zip(pieces_p, pieces_q) for v in pq]

    return pl.pallas_call(
        last_kernel,
        out_shape=jax.ShapeDtypeStruct((height, width), jnp.float32),
        in_specs=[smem] + [vmem] * (2 * blocks + 6),
        out_specs=vmem,
        scratch_shapes=[pltpu.VMEM((LEAD, width), jnp.float32)] * 3,
        cost_estimate=cost,
        compiler_params=params,
        name="own_columns",
    )(info, *state, own_top, *own, *panel_pieces)


def solution(mesh):
    in_specs = (P("row", "col"), P(None, "row"), P(None, "col"))
    out_specs = P("row", "col")

    return jax.shard_map(shards, mesh=mesh, in_specs=in_specs, out_specs=out_specs, check_vma=False)
```

```python
import functools


import jax
import jax.numpy as jnp
from jax import lax
from jax.experimental import pallas as pl
from jax.experimental.pallas import tpu as pltpu
from jax.sharding import PartitionSpec as P

PW = 256
PANELS = 2
LEAD = PW * PANELS
SPLIT = LEAD // 2

SUB = 8
BLK = 128


def swapped(x, axis, mask):
    return lax.ppermute(x, axis, [(i, i ^ mask) for i in range(lax.axis_size(axis))])


def hdot(left, right):
    return jnp.dot(left, right, precision=lax.Precision.HIGHEST, preferred_element_type=jnp.float32)


def tree_sum(terms):
    while len(terms) > 1:
        terms = [terms[i] + terms[i + 1] if i + 1 < len(terms) else terms[i] for i in range(0, len(terms), 2)]
    return terms[0]


def factor(block):
    count = BLK // SUB
    shape = (SUB, BLK)
    sub = lax.broadcasted_iota(jnp.int32, shape, 0)
    lane = lax.broadcasted_iota(jnp.int32, shape, 1)

    def row(x, j):
        return jnp.broadcast_to(x[j : j + 1, :], shape)

    def col(x, j):
        return jnp.broadcast_to(x[:, j : j + 1], shape)

    strips = [block[SUB * i : SUB * (i + 1)] for i in range(count)]
    extra = [jnp.where(lane == sub + SUB * i, 1.0, 0.0) for i in range(count)]
    pending = [jnp.zeros(shape, jnp.float32) for _ in range(count)]
    upper = []
    small = []
    for t in range(count):
        base = SUB * t
        inside = (lane >= base) & (lane < base + SUB)
        for i in range(t, count):
            pending[i] = jnp.where(inside, strips[i], pending[i])
        c = [col(strips[t], base + m) for m in range(SUB)]
        w, x, forward = strips[t], extra[t], strips[t]
        g = jnp.where(lane == sub + base, 1.0, 0.0)
        for j in range(SUB):
            r = 1.0 / row(c[j], j)
            here = sub == j
            cj = c[j]
            for m in range(j + 1, SUB):
                scaled = row(c[m], j) * r
                c[m] = jnp.where(here, scaled, c[m] - cj * scaled)
            scaled = row(w, j) * r
            w = jnp.where(here, scaled, w - cj * scaled)
            scaled = row(x, j) * r
            x = jnp.where(here, scaled, x - cj * scaled)
            scaled = row(g, j) * r
            g = jnp.where(sub > j, g, jnp.where(here, scaled, g - cj * scaled))
            if j < SUB - 1:
                forward = jnp.where(sub > j, forward - (cj * r) * row(forward, j), forward)
        upper.append(forward)
        small.append(g)
        w_rows = [row(w, m) for m in range(SUB)]
        x_rows = [row(x, m) for m in range(SUB)]
        for i in list(range(t + 1, count)) + list(range(t)):
            b = [col(strips[i], base + m) for m in range(SUB)]
            strips[i] = strips[i] - tree_sum([b[m] * w_rows[m] for m in range(SUB)])
            extra[i] = extra[i] - tree_sum([b[m] * x_rows[m] for m in range(SUB)])
        strips[t], extra[t] = w, x
    upper, pending, small, inverse = (jnp.concatenate(v, 0) for v in (upper, pending, small, extra))
    return upper, hdot(pending, small), inverse


def eliminate_block(k, work, packed, inverted):
    blocks = LEAD // BLK
    here = pl.ds(BLK * k, BLK)
    upper, lower, inverse = factor(work[k, here, :])
    size = (BLK, BLK)
    above = lax.broadcasted_iota(jnp.int32, size, 0) <= lax.broadcasted_iota(jnp.int32, size, 1)
    upper = jnp.where(above, upper, 0.0)
    packed[k, here, :] = jnp.where(above, upper, lower)
    upper_inverse = hdot(inverse, lower)
    inverted[here, :] = upper_inverse
    work[k, here, :] = inverse
    later = range(k + 1, blocks)
    solved = {j: hdot(inverse, work[j, here, :]) for j in later}
    if k + 1 < blocks:
        rest = pl.ds(BLK * (k + 1), LEAD - BLK * (k + 1))
        left = work[k, rest, :]
        for j in later:
            work[j, rest, :] = work[j, rest, :] - hdot(left, solved[j])
        packed[k, rest, :] = hdot(left, upper_inverse)
    for j in later:
        packed[j, here, :] = hdot(upper, solved[j])
        work[j, here, :] = solved[j]


def first_kernel(info, *refs):
    blocks = LEAD // BLK
    pieces, (work, packed, inverted) = refs[:blocks], refs[blocks:]
    for n in range(blocks):
        work[info[3] ^ n] = pieces[n][...]
    eliminate_block(0, work, packed, inverted)


def next_kernel(k, old_work, old_packed, old_inverted, work, packed, inverted):
    eliminate_block(k, work, packed, inverted)


def last_kernel(info, work, packed, inverted, own_top, *refs):
    blocks = LEAD // BLK
    own, pieces = refs[:2], refs[2 : 2 + 2 * blocks]
    out, rhs, reduced, top = refs[2 + 2 * blocks :]
    is_panel = info[0] == 1
    slot = info[1]
    is_top = info[2] == 1
    rhs[...] = own_top[...]
    size = (BLK, BLK)
    above = lax.broadcasted_iota(jnp.int32, size, 0) <= lax.broadcasted_iota(jnp.int32, size, 1)
    for k in range(blocks):
        here = pl.ds(BLK * k, BLK)
        solved = hdot(work[k, here, :], rhs[here, :])
        for i in range(k + 1, blocks):
            there = pl.ds(BLK * i, BLK)
            rhs[there, :] = rhs[there, :] - hdot(work[k, there, :], solved)
        upper = jnp.where(above, packed[k, here, :], 0.0)
        top[here, :] = jnp.where(is_panel, packed[slot, here, :], hdot(upper, solved))
        mine = jnp.where(slot == k, inverted[here, :], 0.0)
        reduced[here, :] = jnp.where(is_panel, mine, solved)
    for k in range(blocks - 2, -1, -1):
        here = pl.ds(BLK * k, BLK)
        terms = [hdot(work[j, here, :], reduced[pl.ds(BLK * j, BLK), :]) for j in range(k + 1, blocks)]
        reduced[here, :] = reduced[here, :] - tree_sum(terms)
    runs = pieces[0].shape[0] // SPLIT

    def below(part, run):
        where = pl.ds(pl.multiple_of(run * SPLIT, SPLIT), SPLIT)
        terms = []
        for n in range(blocks):
            block = pl.ds(pl.multiple_of((info[3] ^ n) * BLK, BLK), BLK)
            terms.append(hdot(pieces[2 * n + part][where, :], reduced[block, :]))
        total = tree_sum(terms)
        return jnp.where(is_panel, total, own[part][where, :] - total)

    for part in range(2):
        where = pl.ds(SPLIT * part, SPLIT)
        out[where, :] = jnp.where(is_top, top[where, :], below(part, 0))

    def step(run):
        for part in range(2):
            rows = pl.ds(pl.multiple_of(run * LEAD, LEAD) + SPLIT * part, SPLIT)
            out[rows, :] = below(part, run)

    if runs <= 2:
        for run in range(1, runs):
            step(run)
    else:
        pl.loop(1, runs)(step)


def shards(matrix, row_diag, col_diag):
    height, width = matrix.shape
    row_pos = lax.axis_index("row")
    col_pos = lax.axis_index("col")
    half = height // 2
    blocks = LEAD // width
    block_bits = blocks.bit_length() - 1
    high_bit = lax.axis_size("col").bit_length() - 2
    high, low = 2**high_bit, 2 ** (high_bit - 1)
    is_first = row_pos == 0
    in_high = (col_pos & high) != 0
    in_low = (col_pos & low) != 0
    part_rows = half // 2

    def parts_of(values):
        grouped = values.reshape(2, half // LEAD, 2, SPLIT, *values.shape[1:])
        return [grouped[:, :, p].reshape(2, part_rows, *values.shape[1:]) for p in range(2)]

    rows_p, rows_q = parts_of(matrix)
    other_p = swapped(rows_p, "row", 1)
    far_q = swapped(rows_q, "col", high)
    other_rows = swapped(row_diag, "row", 1)
    pair = jnp.concatenate([col_diag, swapped(col_diag, "col", low)], 0)
    far_pair = swapped(pair, "col", high)

    def diag_of(h, l):
        chosen = jnp.where(in_high == h, pair, far_pair)
        return jnp.where(in_low == l, chosen[:2], chosen[2:])

    none, yes = jnp.bool_(False), jnp.bool_(True)

    def of_half(parts, h, l):
        even, odd = parts
        sign = jnp.where(in_high & h, -0.5, 0.5)
        scale_even = sign * diag_of(h, none)[0]
        scale_odd = jnp.where(l, -sign, sign) * diag_of(h, yes)[0]
        return scale_even * even + scale_odd * odd

    def of_bit(parts, h, l):
        scale = jnp.where(in_low & l, -0.5, 0.5) * diag_of(h, in_low)[0]
        return scale * (parts[0] + jnp.where(h, -parts[1], parts[1]))

    first_diag = jnp.where(is_first, row_diag, other_rows)
    own_scales = [parts_of(row_diag[level]) for level in range(2)]
    first_scales = [parts_of(first_diag[level]) for level in range(2)]

    def own_mixed(part, local, remote):
        scale0, scale1 = own_scales[0][part][..., None], own_scales[1][part][..., None]
        mixed = scale0 * jnp.where(is_first, local + remote, remote - local)
        return 0.5 * scale1[0] * (mixed[0] + mixed[1]), 0.5 * scale1[1] * (mixed[0] - mixed[1])

    def lead_mixed(part, values):
        scale0 = first_scales[0][part][:, :SPLIT, None]
        scale1 = first_scales[1][part][0, :SPLIT, None]
        return 0.5 * scale1 * (scale0[0] * values[0][:SPLIT] + scale0[1] * values[1][:SPLIT])

    first_q = jnp.where(in_high, far_q, rows_q)
    second_q = jnp.where(in_high, rows_q, far_q)
    lead_own = lead_mixed(0, [rows_p[i, :SPLIT] + other_p[i, :SPLIT] for i in range(2)])
    lead_own = (0.5 * diag_of(none, in_low)[0]) * lead_own
    lead_bit = lead_mixed(1, of_bit((first_q[:, :SPLIT], second_q[:, :SPLIT]), none, none))
    lead_p = lead_own + swapped(lead_own, "col", low)
    lead_q = lead_bit + swapped(lead_bit, "row", 1)
    far_lead = swapped(lead_p, "col", high)
    near_lead = swapped(lead_q, "col", low)

    def spread(values):
        for bit in range(block_bits, high_bit - 1):
            arrived = swapped(values, "col", 2**bit)
            values = jnp.where((col_pos & 2**bit) != 0, arrived, values)
        return values

    def gather(values):
        pieces = {0: values}
        for bit in range(block_bits - 1, -1, -1):
            for n in sorted(pieces):
                pieces[n ^ 2**bit] = swapped(pieces[n], "col", 2**bit)
        return [pieces[n] for n in range(blocks)]

    lead_scale = diag_of(none, none)[1]
    lead = lead_scale * jnp.concatenate([lead_p + far_lead, lead_q + near_lead], 0)
    lead_pieces = gather(spread(lead))

    own_p = jnp.stack(own_mixed(0, rows_p, other_p))
    near_p = swapped(own_p, "col", low)
    other_q = swapped(first_q, "row", 1), swapped(second_q, "row", 1)

    def flat(values):
        return values.reshape(2 * part_rows, width)

    parts_q = [flat(jnp.stack(own_mixed(1, a, b))) for a, b in zip((first_q, second_q), other_q)]
    panel_q = of_bit(parts_q, none, none)
    near_q = swapped(panel_q, "col", low)

    info = jnp.stack(
        [
            (col_pos < blocks).astype(jnp.int32),
            jnp.minimum(col_pos, blocks - 1).astype(jnp.int32),
            is_first.astype(jnp.int32),
            (col_pos & (blocks - 1)).astype(jnp.int32),
        ]
    )
    smem = pl.BlockSpec(memory_space=pltpu.SMEM)
    vmem = pl.BlockSpec(memory_space=pltpu.VMEM)
    cost = pl.CostEstimate(flops=4_000_000_000, bytes_accessed=12_000_000, transcendentals=0)
    size = 4 * width * (5 * blocks * LEAD + (blocks + 4) * (height + LEAD))
    params = pltpu.CompilerParams(vmem_limit_bytes=2 * size)
    stack = jax.ShapeDtypeStruct((blocks, LEAD, width), jnp.float32)
    state_shapes = (stack, stack, jax.ShapeDtypeStruct((LEAD, width), jnp.float32))
    state = pl.pallas_call(
        first_kernel,
        out_shape=state_shapes,
        in_specs=[smem] + [vmem] * blocks,
        out_specs=(vmem,) * 3,
        cost_estimate=cost,
        compiler_params=params,
        name="eliminate_0",
    )(info, *lead_pieces)
    near_q, near_p, parts_q, *state = lax.optimization_barrier((near_q, near_p, parts_q, *state))
    parts_p = flat(jnp.where(in_low, near_p, own_p)), flat(jnp.where(in_low, own_p, near_p))
    panel_p = of_half(parts_p, none, none)
    far_p = swapped(panel_p, "col", high)
    panel_q = spread(lead_scale * (panel_q + near_q))
    pieces_q = gather(panel_q)
    kept_p, kept_q = of_half(parts_p, in_high, in_low), of_bit(parts_q, in_high, in_low)
    received_p = swapped(of_half(parts_p, ~in_high, in_low), "col", high)
    received_q = swapped(of_bit(parts_q, in_high, ~in_low), "col", low)
    scale = diag_of(in_high, in_low)[1]

    for k in range(1, blocks):
        state = pl.pallas_call(
            functools.partial(next_kernel, k),
            out_shape=state_shapes,
            in_specs=[vmem] * 3,
            out_specs=(vmem,) * 3,
            input_output_aliases={0: 0, 1: 1, 2: 2},
            cost_estimate=cost,
            compiler_params=params,
        )(*state)
        if k == 1:
            far_p, _, *state = lax.optimization_barrier((far_p, panel_q, *state))
            pieces_p = gather(spread(lead_scale * (panel_p + far_p)))
        if k == blocks - 2:
            received_p, received_q, *state = lax.optimization_barrier((received_p, received_q, *state))
            own = scale * (kept_p + received_p), scale * (kept_q + received_q)
            own_top = jnp.concatenate([v[:SPLIT] for v in own], 0)
            far_top = lax.ppermute(own_top, "row", [(0, 1)])
    far_top, *state = lax.optimization_barrier((far_top, *state))
    own_top = jnp.where(is_first, own_top, far_top)
    panel_pieces = [v for pq in zip(pieces_p, pieces_q) for v in pq]

    return pl.pallas_call(
        last_kernel,
        out_shape=jax.ShapeDtypeStruct((height, width), jnp.float32),
        in_specs=[smem] + [vmem] * (2 * blocks + 6),
        out_specs=vmem,
        scratch_shapes=[pltpu.VMEM((LEAD, width), jnp.float32)] * 3,
        cost_estimate=cost,
        compiler_params=params,
        name="own_columns",
    )(info, *state, own_top, *own, *panel_pieces)


def solution(mesh):
    in_specs = (P("row", "col"), P(None, "row"), P(None, "col"))
    out_specs = P("row", "col")

    return jax.shard_map(shards, mesh=mesh, in_specs=in_specs, out_specs=out_specs, check_vma=False)
```

```python
import functools


import jax
import jax.numpy as jnp
from jax import lax
from jax.experimental import pallas as pl
from jax.experimental.pallas import tpu as pltpu
from jax.sharding import PartitionSpec as P

PW = 256
PANELS = 2
LEAD = PW * PANELS
SPLIT = LEAD // 2

SUB = 8
BLK = 128


def swapped(x, axis, mask):
    return lax.ppermute(x, axis, [(i, i ^ mask) for i in range(lax.axis_size(axis))])


def hdot(left, right):
    return jnp.dot(left, right, precision=lax.Precision.HIGHEST, preferred_element_type=jnp.float32)


def tree_sum(terms):
    while len(terms) > 1:
        terms = [terms[i] + terms[i + 1] if i + 1 < len(terms) else terms[i] for i in range(0, len(terms), 2)]
    return terms[0]


def factor(block):
    count = BLK // SUB
    shape = (SUB, BLK)
    sub = lax.broadcasted_iota(jnp.int32, shape, 0)
    lane = lax.broadcasted_iota(jnp.int32, shape, 1)

    def row(x, j):
        return jnp.broadcast_to(x[j : j + 1, :], shape)

    def col(x, j):
        return jnp.broadcast_to(x[:, j : j + 1], shape)

    strips = [block[SUB * i : SUB * (i + 1)] for i in range(count)]
    extra = [jnp.where(lane == sub + SUB * i, 1.0, 0.0) for i in range(count)]
    pending = [jnp.zeros(shape, jnp.float32) for _ in range(count)]
    upper = []
    small = []
    for t in range(count):
        base = SUB * t
        inside = (lane >= base) & (lane < base + SUB)
        for i in range(t, count):
            pending[i] = jnp.where(inside, strips[i], pending[i])
        c = [col(strips[t], base + m) for m in range(SUB)]
        w, x, forward = strips[t], extra[t], strips[t]
        g = jnp.where(lane == sub + base, 1.0, 0.0)
        for j in range(SUB):
            r = 1.0 / row(c[j], j)
            here = sub == j
            cj = c[j]
            for m in range(j + 1, SUB):
                scaled = row(c[m], j) * r
                c[m] = jnp.where(here, scaled, c[m] - cj * scaled)
            scaled = row(w, j) * r
            w = jnp.where(here, scaled, w - cj * scaled)
            scaled = row(x, j) * r
            x = jnp.where(here, scaled, x - cj * scaled)
            scaled = row(g, j) * r
            g = jnp.where(sub > j, g, jnp.where(here, scaled, g - cj * scaled))
            if j < SUB - 1:
                forward = jnp.where(sub > j, forward - (cj * r) * row(forward, j), forward)
        upper.append(forward)
        small.append(g)
        w_rows = [row(w, m) for m in range(SUB)]
        x_rows = [row(x, m) for m in range(SUB)]
        for i in list(range(t + 1, count)) + list(range(t)):
            b = [col(strips[i], base + m) for m in range(SUB)]
            strips[i] = strips[i] - tree_sum([b[m] * w_rows[m] for m in range(SUB)])
            extra[i] = extra[i] - tree_sum([b[m] * x_rows[m] for m in range(SUB)])
        strips[t], extra[t] = w, x
    upper, pending, small, inverse = (jnp.concatenate(v, 0) for v in (upper, pending, small, extra))
    return upper, hdot(pending, small), inverse


def eliminate_block(k, work, packed, inverted):
    blocks = LEAD // BLK
    here = pl.ds(BLK * k, BLK)
    upper, lower, inverse = factor(work[k, here, :])
    size = (BLK, BLK)
    above = lax.broadcasted_iota(jnp.int32, size, 0) <= lax.broadcasted_iota(jnp.int32, size, 1)
    upper = jnp.where(above, upper, 0.0)
    packed[k, here, :] = jnp.where(above, upper, lower)
    upper_inverse = hdot(inverse, lower)
    inverted[here, :] = upper_inverse
    work[k, here, :] = inverse
    later = range(k + 1, blocks)
    solved = {j: hdot(inverse, work[j, here, :]) for j in later}
    if k + 1 < blocks:
        rest = pl.ds(BLK * (k + 1), LEAD - BLK * (k + 1))
        left = work[k, rest, :]
        for j in later:
            work[j, rest, :] = work[j, rest, :] - hdot(left, solved[j])
        packed[k, rest, :] = hdot(left, upper_inverse)
    for j in later:
        packed[j, here, :] = hdot(upper, solved[j])
        work[j, here, :] = solved[j]


def first_kernel(info, *refs):
    blocks = LEAD // BLK
    pieces, (work, packed, inverted) = refs[:blocks], refs[blocks:]
    for n in range(blocks):
        work[info[3] ^ n] = pieces[n][...]
    eliminate_block(0, work, packed, inverted)


def next_kernel(k, old_work, old_packed, old_inverted, work, packed, inverted):
    eliminate_block(k, work, packed, inverted)


def last_kernel(info, work, packed, inverted, own_top, *refs):
    blocks = LEAD // BLK
    own, pieces = refs[:2], refs[2 : 2 + 2 * blocks]
    out, rhs, reduced, top = refs[2 + 2 * blocks :]
    is_panel = info[0] == 1
    slot = info[1]
    is_top = info[2] == 1
    rhs[...] = own_top[...]
    size = (BLK, BLK)
    above = lax.broadcasted_iota(jnp.int32, size, 0) <= lax.broadcasted_iota(jnp.int32, size, 1)
    for k in range(blocks):
        here = pl.ds(BLK * k, BLK)
        solved = hdot(work[k, here, :], rhs[here, :])
        for i in range(k + 1, blocks):
            there = pl.ds(BLK * i, BLK)
            rhs[there, :] = rhs[there, :] - hdot(work[k, there, :], solved)
        upper = jnp.where(above, packed[k, here, :], 0.0)
        top[here, :] = jnp.where(is_panel, packed[slot, here, :], hdot(upper, solved))
        mine = jnp.where(slot == k, inverted[here, :], 0.0)
        reduced[here, :] = jnp.where(is_panel, mine, solved)
    for k in range(blocks - 2, -1, -1):
        here = pl.ds(BLK * k, BLK)
        terms = [hdot(work[j, here, :], reduced[pl.ds(BLK * j, BLK), :]) for j in range(k + 1, blocks)]
        reduced[here, :] = reduced[here, :] - tree_sum(terms)
    runs = pieces[0].shape[0] // SPLIT

    def below(part, run):
        where = pl.ds(pl.multiple_of(run * SPLIT, SPLIT), SPLIT)
        terms = []
        for n in range(blocks):
            block = pl.ds(pl.multiple_of((info[3] ^ n) * BLK, BLK), BLK)
            terms.append(hdot(pieces[2 * n + part][where, :], reduced[block, :]))
        total = tree_sum(terms)
        return jnp.where(is_panel, total, own[part][where, :] - total)

    for part in range(2):
        where = pl.ds(SPLIT * part, SPLIT)
        out[where, :] = jnp.where(is_top, top[where, :], below(part, 0))

    def step(run):
        for part in range(2):
            rows = pl.ds(pl.multiple_of(run * LEAD, LEAD) + SPLIT * part, SPLIT)
            out[rows, :] = below(part, run)

    if runs <= 2:
        for run in range(1, runs):
            step(run)
    else:
        pl.loop(1, runs)(step)


def shards(matrix, row_diag, col_diag):
    height, width = matrix.shape
    row_pos = lax.axis_index("row")
    col_pos = lax.axis_index("col")
    half = height // 2
    blocks = LEAD // width
    block_bits = blocks.bit_length() - 1
    high_bit = lax.axis_size("col").bit_length() - 2
    high, low = 2**high_bit, 2 ** (high_bit - 1)
    is_first = row_pos == 0
    in_high = (col_pos & high) != 0
    in_low = (col_pos & low) != 0
    part_rows = half // 2

    def parts_of(values):
        grouped = values.reshape(2, half // LEAD, 2, SPLIT, *values.shape[1:])
        return [grouped[:, :, p].reshape(2, part_rows, *values.shape[1:]) for p in range(2)]

    rows_p, rows_q = parts_of(matrix)
    other_p = swapped(rows_p, "row", 1)
    far_q = swapped(rows_q, "col", high)
    other_rows = swapped(row_diag, "row", 1)
    pair = jnp.concatenate([col_diag, swapped(col_diag, "col", low)], 0)
    far_pair = swapped(pair, "col", high)

    def diag_of(h, l):
        chosen = jnp.where(in_high == h, pair, far_pair)
        return jnp.where(in_low == l, chosen[:2], chosen[2:])

    none, yes = jnp.bool_(False), jnp.bool_(True)

    def of_half(parts, h, l):
        even, odd = parts
        sign = jnp.where(in_high & h, -0.5, 0.5)
        scale_even = sign * diag_of(h, none)[0]
        scale_odd = jnp.where(l, -sign, sign) * diag_of(h, yes)[0]
        return scale_even * even + scale_odd * odd

    def of_bit(parts, h, l):
        scale = jnp.where(in_low & l, -0.5, 0.5) * diag_of(h, in_low)[0]
        return scale * (parts[0] + jnp.where(h, -parts[1], parts[1]))

    first_diag = jnp.where(is_first, row_diag, other_rows)
    own_scales = [parts_of(row_diag[level]) for level in range(2)]
    first_scales = [parts_of(first_diag[level]) for level in range(2)]

    def own_mixed(part, local, remote):
        scale0, scale1 = own_scales[0][part][..., None], own_scales[1][part][..., None]
        mixed = scale0 * jnp.where(is_first, local + remote, remote - local)
        return 0.5 * scale1[0] * (mixed[0] + mixed[1]), 0.5 * scale1[1] * (mixed[0] - mixed[1])

    def lead_mixed(part, values):
        scale0 = first_scales[0][part][:, :SPLIT, None]
        scale1 = first_scales[1][part][0, :SPLIT, None]
        return 0.5 * scale1 * (scale0[0] * values[0][:SPLIT] + scale0[1] * values[1][:SPLIT])

    first_q = jnp.where(in_high, far_q, rows_q)
    second_q = jnp.where(in_high, rows_q, far_q)
    lead_own = lead_mixed(0, [rows_p[i, :SPLIT] + other_p[i, :SPLIT] for i in range(2)])
    lead_own = (0.5 * diag_of(none, in_low)[0]) * lead_own
    lead_bit = lead_mixed(1, of_bit((first_q[:, :SPLIT], second_q[:, :SPLIT]), none, none))
    lead_p = lead_own + swapped(lead_own, "col", low)
    lead_q = lead_bit + swapped(lead_bit, "row", 1)
    far_lead = swapped(lead_p, "col", high)
    near_lead = swapped(lead_q, "col", low)

    def spread(values):
        for bit in range(block_bits, high_bit - 1):
            arrived = swapped(values, "col", 2**bit)
            values = jnp.where((col_pos & 2**bit) != 0, arrived, values)
        return values

    def gather(values):
        pieces = {0: values}
        for bit in range(block_bits - 1, -1, -1):
            for n in sorted(pieces):
                pieces[n ^ 2**bit] = swapped(pieces[n], "col", 2**bit)
        return [pieces[n] for n in range(blocks)]

    lead_scale = diag_of(none, none)[1]
    lead = lead_scale * jnp.concatenate([lead_p + far_lead, lead_q + near_lead], 0)
    lead_pieces = gather(spread(lead))

    own_p = jnp.stack(own_mixed(0, rows_p, other_p))
    near_p = swapped(own_p, "col", low)
    other_q = swapped(first_q, "row", 1), swapped(second_q, "row", 1)

    def flat(values):
        return values.reshape(2 * part_rows, width)

    parts_q = [flat(jnp.stack(own_mixed(1, a, b))) for a, b in zip((first_q, second_q), other_q)]
    panel_q = of_bit(parts_q, none, none)
    near_q = swapped(panel_q, "col", low)

    parts_p = flat(jnp.where(in_low, near_p, own_p)), flat(jnp.where(in_low, own_p, near_p))
    panel_p = of_half(parts_p, none, none)
    far_p = swapped(panel_p, "col", high)
    received_p = swapped(of_half(parts_p, ~in_high, in_low), "col", high)

    info = jnp.stack(
        [
            (col_pos < blocks).astype(jnp.int32),
            jnp.minimum(col_pos, blocks - 1).astype(jnp.int32),
            is_first.astype(jnp.int32),
            (col_pos & (blocks - 1)).astype(jnp.int32),
        ]
    )
    smem = pl.BlockSpec(memory_space=pltpu.SMEM)
    vmem = pl.BlockSpec(memory_space=pltpu.VMEM)
    cost = pl.CostEstimate(flops=4_000_000_000, bytes_accessed=12_000_000, transcendentals=0)
    size = 4 * width * (5 * blocks * LEAD + (blocks + 4) * (height + LEAD))
    params = pltpu.CompilerParams(vmem_limit_bytes=2 * size)
    stack = jax.ShapeDtypeStruct((blocks, LEAD, width), jnp.float32)
    state_shapes = (stack, stack, jax.ShapeDtypeStruct((LEAD, width), jnp.float32))
    state = pl.pallas_call(
        first_kernel,
        out_shape=state_shapes,
        in_specs=[smem] + [vmem] * blocks,
        out_specs=(vmem,) * 3,
        cost_estimate=cost,
        compiler_params=params,
        name="eliminate_0",
    )(info, *lead_pieces)
    near_q, parts_q, *state = lax.optimization_barrier((near_q, parts_q, *state))
    panel_q = spread(lead_scale * (panel_q + near_q))
    pieces_q = gather(panel_q)
    kept_p, kept_q = of_half(parts_p, in_high, in_low), of_bit(parts_q, in_high, in_low)
    received_q = swapped(of_bit(parts_q, in_high, ~in_low), "col", low)
    scale = diag_of(in_high, in_low)[1]

    for k in range(1, blocks):
        state = pl.pallas_call(
            functools.partial(next_kernel, k),
            out_shape=state_shapes,
            in_specs=[vmem] * 3,
            out_specs=(vmem,) * 3,
            input_output_aliases={0: 0, 1: 1, 2: 2},
            cost_estimate=cost,
            compiler_params=params,
        )(*state)
        if k == 1:
            far_p, received_p, received_q, _, *state = lax.optimization_barrier(
                (far_p, received_p, received_q, panel_q, *state)
            )
            pieces_p = gather(spread(lead_scale * (panel_p + far_p)))
            own = scale * (kept_p + received_p), scale * (kept_q + received_q)
            own_top = jnp.concatenate([v[:SPLIT] for v in own], 0)
            far_top = lax.ppermute(own_top, "row", [(0, 1)])
    far_top, *state = lax.optimization_barrier((far_top, *state))
    own_top = jnp.where(is_first, own_top, far_top)
    panel_pieces = [v for pq in zip(pieces_p, pieces_q) for v in pq]

    return pl.pallas_call(
        last_kernel,
        out_shape=jax.ShapeDtypeStruct((height, width), jnp.float32),
        in_specs=[smem] + [vmem] * (2 * blocks + 6),
        out_specs=vmem,
        scratch_shapes=[pltpu.VMEM((LEAD, width), jnp.float32)] * 3,
        cost_estimate=cost,
        compiler_params=params,
        name="own_columns",
    )(info, *state, own_top, *own, *panel_pieces)


def solution(mesh):
    in_specs = (P("row", "col"), P(None, "row"), P(None, "col"))
    out_specs = P("row", "col")

    return jax.shard_map(shards, mesh=mesh, in_specs=in_specs, out_specs=out_specs, check_vma=False)
```

```python
import functools


import jax
import jax.numpy as jnp
from jax import lax
from jax.experimental import pallas as pl
from jax.experimental.pallas import tpu as pltpu
from jax.sharding import PartitionSpec as P

PW = 256
PANELS = 2
LEAD = PW * PANELS
SPLIT = LEAD // 2

SUB = 8
BLK = 128


def swapped(x, axis, mask):
    return lax.ppermute(x, axis, [(i, i ^ mask) for i in range(lax.axis_size(axis))])


def hdot(left, right):
    return jnp.dot(left, right, precision=lax.Precision.HIGHEST, preferred_element_type=jnp.float32)


def tree_sum(terms):
    while len(terms) > 1:
        terms = [terms[i] + terms[i + 1] if i + 1 < len(terms) else terms[i] for i in range(0, len(terms), 2)]
    return terms[0]


def factor(block):
    count = BLK // SUB
    shape = (SUB, BLK)
    sub = lax.broadcasted_iota(jnp.int32, shape, 0)
    lane = lax.broadcasted_iota(jnp.int32, shape, 1)

    def row(x, j):
        return jnp.broadcast_to(x[j : j + 1, :], shape)

    def col(x, j):
        return jnp.broadcast_to(x[:, j : j + 1], shape)

    strips = [block[SUB * i : SUB * (i + 1)] for i in range(count)]
    extra = [jnp.where(lane == sub + SUB * i, 1.0, 0.0) for i in range(count)]
    pending = [jnp.zeros(shape, jnp.float32) for _ in range(count)]
    upper = []
    small = []
    for t in range(count):
        base = SUB * t
        inside = (lane >= base) & (lane < base + SUB)
        for i in range(t, count):
            pending[i] = jnp.where(inside, strips[i], pending[i])
        c = [col(strips[t], base + m) for m in range(SUB)]
        w, x, forward = strips[t], extra[t], strips[t]
        g = jnp.where(lane == sub + base, 1.0, 0.0)
        for j in range(SUB):
            r = 1.0 / row(c[j], j)
            here = sub == j
            cj = c[j]
            for m in range(j + 1, SUB):
                scaled = row(c[m], j) * r
                c[m] = jnp.where(here, scaled, c[m] - cj * scaled)
            scaled = row(w, j) * r
            w = jnp.where(here, scaled, w - cj * scaled)
            scaled = row(x, j) * r
            x = jnp.where(here, scaled, x - cj * scaled)
            scaled = row(g, j) * r
            g = jnp.where(sub > j, g, jnp.where(here, scaled, g - cj * scaled))
            if j < SUB - 1:
                forward = jnp.where(sub > j, forward - (cj * r) * row(forward, j), forward)
        upper.append(forward)
        small.append(g)
        w_rows = [row(w, m) for m in range(SUB)]
        x_rows = [row(x, m) for m in range(SUB)]
        for i in list(range(t + 1, count)) + list(range(t)):
            b = [col(strips[i], base + m) for m in range(SUB)]
            strips[i] = strips[i] - tree_sum([b[m] * w_rows[m] for m in range(SUB)])
            extra[i] = extra[i] - tree_sum([b[m] * x_rows[m] for m in range(SUB)])
        strips[t], extra[t] = w, x
    upper, pending, small, inverse = (jnp.concatenate(v, 0) for v in (upper, pending, small, extra))
    return upper, hdot(pending, small), inverse


def eliminate_block(k, work, packed, inverted):
    blocks = LEAD // BLK
    here = pl.ds(BLK * k, BLK)
    upper, lower, inverse = factor(work[k, here, :])
    size = (BLK, BLK)
    above = lax.broadcasted_iota(jnp.int32, size, 0) <= lax.broadcasted_iota(jnp.int32, size, 1)
    upper = jnp.where(above, upper, 0.0)
    packed[k, here, :] = jnp.where(above, upper, lower)
    upper_inverse = hdot(inverse, lower)
    inverted[here, :] = upper_inverse
    work[k, here, :] = inverse
    later = range(k + 1, blocks)
    solved = {j: hdot(inverse, work[j, here, :]) for j in later}
    if k + 1 < blocks:
        rest = pl.ds(BLK * (k + 1), LEAD - BLK * (k + 1))
        left = work[k, rest, :]
        for j in later:
            work[j, rest, :] = work[j, rest, :] - hdot(left, solved[j])
        packed[k, rest, :] = hdot(left, upper_inverse)
    for j in later:
        packed[j, here, :] = hdot(upper, solved[j])
        work[j, here, :] = solved[j]


def first_kernel(info, *refs):
    blocks = LEAD // BLK
    pieces, (work, packed, inverted) = refs[:blocks], refs[blocks:]
    for n in range(blocks):
        work[info[3] ^ n] = pieces[n][...]
    eliminate_block(0, work, packed, inverted)


def next_kernel(k, old_work, old_packed, old_inverted, work, packed, inverted):
    eliminate_block(k, work, packed, inverted)


def last_kernel(info, work, packed, inverted, own_top, *refs):
    blocks = LEAD // BLK
    own, pieces = refs[:2], refs[2 : 2 + 2 * blocks]
    out, rhs, reduced, top = refs[2 + 2 * blocks :]
    is_panel = info[0] == 1
    slot = info[1]
    is_top = info[2] == 1
    rhs[...] = own_top[...]
    size = (BLK, BLK)
    above = lax.broadcasted_iota(jnp.int32, size, 0) <= lax.broadcasted_iota(jnp.int32, size, 1)
    for k in range(blocks):
        here = pl.ds(BLK * k, BLK)
        solved = hdot(work[k, here, :], rhs[here, :])
        for i in range(k + 1, blocks):
            there = pl.ds(BLK * i, BLK)
            rhs[there, :] = rhs[there, :] - hdot(work[k, there, :], solved)
        upper = jnp.where(above, packed[k, here, :], 0.0)
        top[here, :] = jnp.where(is_panel, packed[slot, here, :], hdot(upper, solved))
        mine = jnp.where(slot == k, inverted[here, :], 0.0)
        reduced[here, :] = jnp.where(is_panel, mine, solved)
    for k in range(blocks - 2, -1, -1):
        here = pl.ds(BLK * k, BLK)
        terms = [hdot(work[j, here, :], reduced[pl.ds(BLK * j, BLK), :]) for j in range(k + 1, blocks)]
        reduced[here, :] = reduced[here, :] - tree_sum(terms)
    runs = pieces[0].shape[0] // SPLIT

    def below(part, run):
        where = pl.ds(pl.multiple_of(run * SPLIT, SPLIT), SPLIT)
        terms = []
        for n in range(blocks):
            block = pl.ds(pl.multiple_of((info[3] ^ n) * BLK, BLK), BLK)
            terms.append(hdot(pieces[2 * n + part][where, :], reduced[block, :]))
        total = tree_sum(terms)
        return jnp.where(is_panel, total, own[part][where, :] - total)

    for part in range(2):
        where = pl.ds(SPLIT * part, SPLIT)
        out[where, :] = jnp.where(is_top, top[where, :], below(part, 0))

    def step(run):
        for part in range(2):
            rows = pl.ds(pl.multiple_of(run * LEAD, LEAD) + SPLIT * part, SPLIT)
            out[rows, :] = below(part, run)

    if runs <= 2:
        for run in range(1, runs):
            step(run)
    else:
        pl.loop(1, runs)(step)


def shards(matrix, row_diag, col_diag):
    height, width = matrix.shape
    row_pos = lax.axis_index("row")
    col_pos = lax.axis_index("col")
    half = height // 2
    blocks = LEAD // width
    block_bits = blocks.bit_length() - 1
    high_bit = lax.axis_size("col").bit_length() - 2
    high, low = 2**high_bit, 2 ** (high_bit - 1)
    is_first = row_pos == 0
    in_high = (col_pos & high) != 0
    in_low = (col_pos & low) != 0
    part_rows = half // 2

    def parts_of(values):
        grouped = values.reshape(2, half // LEAD, 2, SPLIT, *values.shape[1:])
        return [grouped[:, :, p].reshape(2, part_rows, *values.shape[1:]) for p in range(2)]

    rows_p, rows_q = parts_of(matrix)
    other_p = swapped(rows_p, "row", 1)
    near_q = swapped(rows_q, "col", low)
    other_rows = swapped(row_diag, "row", 1)
    pair = jnp.concatenate([col_diag, swapped(col_diag, "col", low)], 0)
    far_pair = swapped(pair, "col", high)

    def diag_of(h, l):
        chosen = jnp.where(in_high == h, pair, far_pair)
        return jnp.where(in_low == l, chosen[:2], chosen[2:])

    none, yes = jnp.bool_(False), jnp.bool_(True)

    def of_half(parts, h, l):
        even, odd = parts
        sign = jnp.where(in_high & h, -0.5, 0.5)
        scale_even = sign * diag_of(h, none)[0]
        scale_odd = jnp.where(l, -sign, sign) * diag_of(h, yes)[0]
        return scale_even * even + scale_odd * odd

    def of_bit(parts, h, l):
        scale = jnp.where(in_low & l, -0.5, 0.5) * diag_of(h, in_low)[0]
        return scale * (parts[0] + jnp.where(h, -parts[1], parts[1]))

    first_diag = jnp.where(is_first, row_diag, other_rows)
    own_scales = [parts_of(row_diag[level]) for level in range(2)]
    first_scales = [parts_of(first_diag[level]) for level in range(2)]

    def own_mixed(part, local, remote):
        scale0, scale1 = own_scales[0][part][..., None], own_scales[1][part][..., None]
        mixed = scale0 * jnp.where(is_first, local + remote, remote - local)
        return 0.5 * scale1[0] * (mixed[0] + mixed[1]), 0.5 * scale1[1] * (mixed[0] - mixed[1])

    def lead_mixed(part, values):
        scale0 = first_scales[0][part][:, :SPLIT, None]
        scale1 = first_scales[1][part][0, :SPLIT, None]
        return 0.5 * scale1 * (scale0[0] * values[0][:SPLIT] + scale0[1] * values[1][:SPLIT])

    even_q = jnp.where(in_low, near_q, rows_q)
    odd_q = jnp.where(in_low, rows_q, near_q)
    lead_own = lead_mixed(0, [rows_p[i, :SPLIT] + other_p[i, :SPLIT] for i in range(2)])
    lead_own = (0.5 * diag_of(none, in_low)[0]) * lead_own
    lead_half = lead_mixed(1, of_half((even_q[:, :SPLIT], odd_q[:, :SPLIT]), none, none))
    lead_p = lead_own + swapped(lead_own, "col", high)
    lead_q = lead_half + swapped(lead_half, "row", 1)
    near_lead = swapped(lead_p, "col", low)
    far_lead = swapped(lead_q, "col", high)

    def spread(values):
        for bit in range(block_bits, high_bit - 1):
            arrived = swapped(values, "col", 2**bit)
            values = jnp.where((col_pos & 2**bit) != 0, arrived, values)
        return values

    def gather(values):
        pieces = {0: values}
        for bit in range(block_bits - 1, -1, -1):
            for n in sorted(pieces):
                pieces[n ^ 2**bit] = swapped(pieces[n], "col", 2**bit)
        return [pieces[n] for n in range(blocks)]

    lead_scale = diag_of(none, none)[1]
    lead = lead_scale * jnp.concatenate([lead_p + near_lead, lead_q + far_lead], 0)
    lead_pieces = gather(spread(lead))

    def flat(values):
        return values.reshape(2 * part_rows, width)

    own_p = jnp.stack(own_mixed(0, rows_p, other_p))
    far_own = swapped(own_p, "col", high)
    other_q = swapped(even_q, "row", 1), swapped(odd_q, "row", 1)
    parts_p = flat(jnp.where(in_high, far_own, own_p)), flat(jnp.where(in_high, own_p, far_own))
    panel_p = of_bit(parts_p, none, none)
    near_p = swapped(panel_p, "col", low)

    info = jnp.stack(
        [
            (col_pos < blocks).astype(jnp.int32),
            jnp.minimum(col_pos, blocks - 1).astype(jnp.int32),
            is_first.astype(jnp.int32),
            (col_pos & (blocks - 1)).astype(jnp.int32),
        ]
    )
    smem = pl.BlockSpec(memory_space=pltpu.SMEM)
    vmem = pl.BlockSpec(memory_space=pltpu.VMEM)
    cost = pl.CostEstimate(flops=4_000_000_000, bytes_accessed=12_000_000, transcendentals=0)
    size = 4 * width * (5 * blocks * LEAD + (blocks + 4) * (height + LEAD))
    params = pltpu.CompilerParams(vmem_limit_bytes=2 * size)
    stack = jax.ShapeDtypeStruct((blocks, LEAD, width), jnp.float32)
    state_shapes = (stack, stack, jax.ShapeDtypeStruct((LEAD, width), jnp.float32))
    state = pl.pallas_call(
        first_kernel,
        out_shape=state_shapes,
        in_specs=[smem] + [vmem] * blocks,
        out_specs=(vmem,) * 3,
        cost_estimate=cost,
        compiler_params=params,
        name="eliminate_0",
    )(info, *lead_pieces)
    near_p, parts_p, even_q, odd_q, other_q, *state = lax.optimization_barrier(
        (near_p, parts_p, even_q, odd_q, other_q, *state)
    )
    parts_q = [flat(jnp.stack(own_mixed(1, a, b))) for a, b in zip((even_q, odd_q), other_q)]
    panel_q = of_half(parts_q, none, none)
    far_q = swapped(panel_q, "col", high)
    received_q = swapped(of_half(parts_q, ~in_high, in_low), "col", high)
    panel_p = spread(lead_scale * (panel_p + near_p))
    pieces_p = gather(panel_p)
    kept_p, kept_q = of_bit(parts_p, in_high, in_low), of_half(parts_q, in_high, in_low)
    received_p = swapped(of_bit(parts_p, in_high, ~in_low), "col", low)
    scale = diag_of(in_high, in_low)[1]

    for k in range(1, blocks):
        state = pl.pallas_call(
            functools.partial(next_kernel, k),
            out_shape=state_shapes,
            in_specs=[vmem] * 3,
            out_specs=(vmem,) * 3,
            input_output_aliases={0: 0, 1: 1, 2: 2},
            cost_estimate=cost,
            compiler_params=params,
        )(*state)
        if k == blocks - 2:
            far_q, received_p, received_q, _, *state = lax.optimization_barrier(
                (far_q, received_p, received_q, panel_p, *state)
            )
            pieces_q = gather(spread(lead_scale * (panel_q + far_q)))
            own = scale * (kept_p + received_p), scale * (kept_q + received_q)
            own_top = jnp.concatenate([v[:SPLIT] for v in own], 0)
            far_top = lax.ppermute(own_top, "row", [(0, 1)])
    far_top, *state = lax.optimization_barrier((far_top, *state))
    own_top = jnp.where(is_first, own_top, far_top)
    panel_pieces = [v for pq in zip(pieces_p, pieces_q) for v in pq]

    return pl.pallas_call(
        last_kernel,
        out_shape=jax.ShapeDtypeStruct((height, width), jnp.float32),
        in_specs=[smem] + [vmem] * (2 * blocks + 6),
        out_specs=vmem,
        scratch_shapes=[pltpu.VMEM((LEAD, width), jnp.float32)] * 3,
        cost_estimate=cost,
        compiler_params=params,
        name="own_columns",
    )(info, *state, own_top, *own, *panel_pieces)


def solution(mesh):
    in_specs = (P("row", "col"), P(None, "row"), P(None, "col"))
    out_specs = P("row", "col")

    return jax.shard_map(shards, mesh=mesh, in_specs=in_specs, out_specs=out_specs, check_vma=False)
```

```python
import functools


import jax
import jax.numpy as jnp
from jax import lax
from jax.experimental import pallas as pl
from jax.experimental.pallas import tpu as pltpu
from jax.sharding import PartitionSpec as P

PW = 256
PANELS = 2
LEAD = PW * PANELS
SPLIT = LEAD // 2

SUB = 8
BLK = 128


def swapped(x, axis, mask):
    return lax.ppermute(x, axis, [(i, i ^ mask) for i in range(lax.axis_size(axis))])


def hdot(left, right):
    return jnp.dot(left, right, precision=lax.Precision.HIGHEST, preferred_element_type=jnp.float32)


def tree_sum(terms):
    while len(terms) > 1:
        terms = [terms[i] + terms[i + 1] if i + 1 < len(terms) else terms[i] for i in range(0, len(terms), 2)]
    return terms[0]


def factor(block):
    count = BLK // SUB
    shape = (SUB, BLK)
    sub = lax.broadcasted_iota(jnp.int32, shape, 0)
    lane = lax.broadcasted_iota(jnp.int32, shape, 1)

    def row(x, j):
        return jnp.broadcast_to(x[j : j + 1, :], shape)

    def col(x, j):
        return jnp.broadcast_to(x[:, j : j + 1], shape)

    strips = [block[SUB * i : SUB * (i + 1)] for i in range(count)]
    extra = [jnp.where(lane == sub + SUB * i, 1.0, 0.0) for i in range(count)]
    pending = [jnp.zeros(shape, jnp.float32) for _ in range(count)]
    upper = []
    small = []
    for t in range(count):
        base = SUB * t
        inside = (lane >= base) & (lane < base + SUB)
        for i in range(t, count):
            pending[i] = jnp.where(inside, strips[i], pending[i])
        c = [col(strips[t], base + m) for m in range(SUB)]
        w, x, forward = strips[t], extra[t], strips[t]
        g = jnp.where(lane == sub + base, 1.0, 0.0)
        for j in range(SUB):
            r = 1.0 / row(c[j], j)
            here = sub == j
            cj = c[j]
            for m in range(j + 1, SUB):
                scaled = row(c[m], j) * r
                c[m] = jnp.where(here, scaled, c[m] - cj * scaled)
            scaled = row(w, j) * r
            w = jnp.where(here, scaled, w - cj * scaled)
            scaled = row(x, j) * r
            x = jnp.where(here, scaled, x - cj * scaled)
            scaled = row(g, j) * r
            g = jnp.where(sub > j, g, jnp.where(here, scaled, g - cj * scaled))
            if j < SUB - 1:
                forward = jnp.where(sub > j, forward - (cj * r) * row(forward, j), forward)
        upper.append(forward)
        small.append(g)
        w_rows = [row(w, m) for m in range(SUB)]
        x_rows = [row(x, m) for m in range(SUB)]
        for i in list(range(t + 1, count)) + list(range(t)):
            b = [col(strips[i], base + m) for m in range(SUB)]
            strips[i] = strips[i] - tree_sum([b[m] * w_rows[m] for m in range(SUB)])
            extra[i] = extra[i] - tree_sum([b[m] * x_rows[m] for m in range(SUB)])
        strips[t], extra[t] = w, x
    upper, pending, small, inverse = (jnp.concatenate(v, 0) for v in (upper, pending, small, extra))
    return upper, hdot(pending, small), inverse


def eliminate_block(k, work, packed, inverted):
    blocks = LEAD // BLK
    here = pl.ds(BLK * k, BLK)
    upper, lower, inverse = factor(work[k, here, :])
    size = (BLK, BLK)
    above = lax.broadcasted_iota(jnp.int32, size, 0) <= lax.broadcasted_iota(jnp.int32, size, 1)
    upper = jnp.where(above, upper, 0.0)
    packed[k, here, :] = jnp.where(above, upper, lower)
    upper_inverse = hdot(inverse, lower)
    inverted[here, :] = upper_inverse
    work[k, here, :] = inverse
    later = range(k + 1, blocks)
    solved = {j: hdot(inverse, work[j, here, :]) for j in later}
    if k + 1 < blocks:
        rest = pl.ds(BLK * (k + 1), LEAD - BLK * (k + 1))
        left = work[k, rest, :]
        for j in later:
            work[j, rest, :] = work[j, rest, :] - hdot(left, solved[j])
        packed[k, rest, :] = hdot(left, upper_inverse)
    for j in later:
        packed[j, here, :] = hdot(upper, solved[j])
        work[j, here, :] = solved[j]


def first_kernel(info, *refs):
    blocks = LEAD // BLK
    pieces, (work, packed, inverted) = refs[:blocks], refs[blocks:]
    for n in range(blocks):
        work[info[3] ^ n] = pieces[n][...]
    eliminate_block(0, work, packed, inverted)


def next_kernel(k, old_work, old_packed, old_inverted, work, packed, inverted):
    eliminate_block(k, work, packed, inverted)


def last_kernel(info, work, packed, inverted, own_top, *refs):
    blocks = LEAD // BLK
    own, pieces = refs[:2], refs[2 : 2 + 2 * blocks]
    out, rhs, reduced, top = refs[2 + 2 * blocks :]
    is_panel = info[0] == 1
    slot = info[1]
    is_top = info[2] == 1
    rhs[...] = own_top[...]
    size = (BLK, BLK)
    above = lax.broadcasted_iota(jnp.int32, size, 0) <= lax.broadcasted_iota(jnp.int32, size, 1)
    for k in range(blocks):
        here = pl.ds(BLK * k, BLK)
        solved = hdot(work[k, here, :], rhs[here, :])
        for i in range(k + 1, blocks):
            there = pl.ds(BLK * i, BLK)
            rhs[there, :] = rhs[there, :] - hdot(work[k, there, :], solved)
        upper = jnp.where(above, packed[k, here, :], 0.0)
        top[here, :] = jnp.where(is_panel, packed[slot, here, :], hdot(upper, solved))
        mine = jnp.where(slot == k, inverted[here, :], 0.0)
        reduced[here, :] = jnp.where(is_panel, mine, solved)
    for k in range(blocks - 2, -1, -1):
        here = pl.ds(BLK * k, BLK)
        terms = [hdot(work[j, here, :], reduced[pl.ds(BLK * j, BLK), :]) for j in range(k + 1, blocks)]
        reduced[here, :] = reduced[here, :] - tree_sum(terms)
    runs = pieces[0].shape[0] // SPLIT

    def below(part, run):
        where = pl.ds(pl.multiple_of(run * SPLIT, SPLIT), SPLIT)
        terms = []
        for n in range(blocks):
            block = pl.ds(pl.multiple_of((info[3] ^ n) * BLK, BLK), BLK)
            terms.append(hdot(pieces[2 * n + part][where, :], reduced[block, :]))
        total = tree_sum(terms)
        return jnp.where(is_panel, total, own[part][where, :] - total)

    for part in range(2):
        where = pl.ds(SPLIT * part, SPLIT)
        out[where, :] = jnp.where(is_top, top[where, :], below(part, 0))

    def step(run):
        for part in range(2):
            rows = pl.ds(pl.multiple_of(run * LEAD, LEAD) + SPLIT * part, SPLIT)
            out[rows, :] = below(part, run)

    if runs <= 2:
        for run in range(1, runs):
            step(run)
    else:
        pl.loop(1, runs)(step)


def shards(matrix, row_diag, col_diag):
    height, width = matrix.shape
    row_pos = lax.axis_index("row")
    col_pos = lax.axis_index("col")
    half = height // 2
    blocks = LEAD // width
    block_bits = blocks.bit_length() - 1
    high_bit = lax.axis_size("col").bit_length() - 2
    high, low = 2**high_bit, 2 ** (high_bit - 1)
    is_first = row_pos == 0
    in_high = (col_pos & high) != 0
    in_low = (col_pos & low) != 0
    part_rows = half // 2

    def parts_of(values):
        grouped = values.reshape(2, half // LEAD, 2, SPLIT, *values.shape[1:])
        return [grouped[:, :, p].reshape(2, part_rows, *values.shape[1:]) for p in range(2)]

    rows_p, rows_q = parts_of(matrix)
    other_p = swapped(rows_p, "row", 1)
    near_q = swapped(rows_q, "col", low)
    other_rows = swapped(row_diag, "row", 1)
    pair = jnp.concatenate([col_diag, swapped(col_diag, "col", low)], 0)
    far_pair = swapped(pair, "col", high)

    def diag_of(h, l):
        chosen = jnp.where(in_high == h, pair, far_pair)
        return jnp.where(in_low == l, chosen[:2], chosen[2:])

    none, yes = jnp.bool_(False), jnp.bool_(True)

    def of_half(parts, h, l):
        even, odd = parts
        sign = jnp.where(in_high & h, -0.5, 0.5)
        scale_even = sign * diag_of(h, none)[0]
        scale_odd = jnp.where(l, -sign, sign) * diag_of(h, yes)[0]
        return scale_even * even + scale_odd * odd

    def of_bit(parts, h, l):
        scale = jnp.where(in_low & l, -0.5, 0.5) * diag_of(h, in_low)[0]
        return scale * (parts[0] + jnp.where(h, -parts[1], parts[1]))

    first_diag = jnp.where(is_first, row_diag, other_rows)
    own_scales = [parts_of(row_diag[level]) for level in range(2)]
    first_scales = [parts_of(first_diag[level]) for level in range(2)]

    def own_mixed(part, local, remote):
        scale0, scale1 = own_scales[0][part][..., None], own_scales[1][part][..., None]
        mixed = scale0 * jnp.where(is_first, local + remote, remote - local)
        return 0.5 * scale1[0] * (mixed[0] + mixed[1]), 0.5 * scale1[1] * (mixed[0] - mixed[1])

    def lead_mixed(part, values):
        scale0 = first_scales[0][part][:, :SPLIT, None]
        scale1 = first_scales[1][part][0, :SPLIT, None]
        return 0.5 * scale1 * (scale0[0] * values[0][:SPLIT] + scale0[1] * values[1][:SPLIT])

    even_q = jnp.where(in_low, near_q, rows_q)
    odd_q = jnp.where(in_low, rows_q, near_q)
    lead_own = lead_mixed(0, [rows_p[i, :SPLIT] + other_p[i, :SPLIT] for i in range(2)])
    lead_own = (0.5 * diag_of(none, in_low)[0]) * lead_own
    lead_half = lead_mixed(1, of_half((even_q[:, :SPLIT], odd_q[:, :SPLIT]), none, none))
    lead_p = lead_own + swapped(lead_own, "col", high)
    lead_q = lead_half + swapped(lead_half, "row", 1)
    near_lead = swapped(lead_p, "col", low)
    far_lead = swapped(lead_q, "col", high)

    def spread(values):
        for bit in range(block_bits, high_bit - 1):
            arrived = swapped(values, "col", 2**bit)
            values = jnp.where((col_pos & 2**bit) != 0, arrived, values)
        return values

    def gather(values):
        pieces = {0: values}
        for bit in range(block_bits - 1, -1, -1):
            for n in sorted(pieces):
                pieces[n ^ 2**bit] = swapped(pieces[n], "col", 2**bit)
        return [pieces[n] for n in range(blocks)]

    lead_scale = diag_of(none, none)[1]
    lead = lead_scale * jnp.concatenate([lead_p + near_lead, lead_q + far_lead], 0)
    lead_pieces = gather(spread(lead))

    def flat(values):
        return values.reshape(2 * part_rows, width)

    own_p = jnp.stack(own_mixed(0, rows_p, other_p))
    far_own = swapped(own_p, "col", high)
    other_q = swapped(even_q, "row", 1), swapped(odd_q, "row", 1)
    parts_q = [flat(jnp.stack(own_mixed(1, a, b))) for a, b in zip((even_q, odd_q), other_q)]
    panel_q = of_half(parts_q, none, none)
    far_q = swapped(panel_q, "col", high)
    received_q = swapped(of_half(parts_q, ~in_high, in_low), "col", high)
    parts_p = flat(jnp.where(in_high, far_own, own_p)), flat(jnp.where(in_high, own_p, far_own))
    panel_p = of_bit(parts_p, none, none)
    near_p = swapped(panel_p, "col", low)
    received_p = swapped(of_bit(parts_p, in_high, ~in_low), "col", low)

    info = jnp.stack(
        [
            (col_pos < blocks).astype(jnp.int32),
            jnp.minimum(col_pos, blocks - 1).astype(jnp.int32),
            is_first.astype(jnp.int32),
            (col_pos & (blocks - 1)).astype(jnp.int32),
        ]
    )
    smem = pl.BlockSpec(memory_space=pltpu.SMEM)
    vmem = pl.BlockSpec(memory_space=pltpu.VMEM)
    cost = pl.CostEstimate(flops=4_000_000_000, bytes_accessed=12_000_000, transcendentals=0)
    size = 4 * width * (5 * blocks * LEAD + (blocks + 4) * (height + LEAD))
    params = pltpu.CompilerParams(vmem_limit_bytes=2 * size)
    stack = jax.ShapeDtypeStruct((blocks, LEAD, width), jnp.float32)
    state_shapes = (stack, stack, jax.ShapeDtypeStruct((LEAD, width), jnp.float32))
    state = pl.pallas_call(
        first_kernel,
        out_shape=state_shapes,
        in_specs=[smem] + [vmem] * blocks,
        out_specs=(vmem,) * 3,
        cost_estimate=cost,
        compiler_params=params,
        name="eliminate_0",
    )(info, *lead_pieces)
    near_p, *state = lax.optimization_barrier((near_p, *state))
    panel_p = spread(lead_scale * (panel_p + near_p))
    pieces_p = gather(panel_p)
    kept_p, kept_q = of_bit(parts_p, in_high, in_low), of_half(parts_q, in_high, in_low)
    scale = diag_of(in_high, in_low)[1]

    for k in range(1, blocks):
        state = pl.pallas_call(
            functools.partial(next_kernel, k),
            out_shape=state_shapes,
            in_specs=[vmem] * 3,
            out_specs=(vmem,) * 3,
            input_output_aliases={0: 0, 1: 1, 2: 2},
            cost_estimate=cost,
            compiler_params=params,
        )(*state)
        if k == 1:
            far_q, received_p, received_q, _, *state = lax.optimization_barrier(
                (far_q, received_p, received_q, panel_p, *state)
            )
            pieces_q = gather(spread(lead_scale * (panel_q + far_q)))
            own = scale * (kept_p + received_p), scale * (kept_q + received_q)
            own_top = jnp.concatenate([v[:SPLIT] for v in own], 0)
            far_top = lax.ppermute(own_top, "row", [(0, 1)])
    far_top, *state = lax.optimization_barrier((far_top, *state))
    own_top = jnp.where(is_first, own_top, far_top)
    panel_pieces = [v for pq in zip(pieces_p, pieces_q) for v in pq]

    return pl.pallas_call(
        last_kernel,
        out_shape=jax.ShapeDtypeStruct((height, width), jnp.float32),
        in_specs=[smem] + [vmem] * (2 * blocks + 6),
        out_specs=vmem,
        scratch_shapes=[pltpu.VMEM((LEAD, width), jnp.float32)] * 3,
        cost_estimate=cost,
        compiler_params=params,
        name="own_columns",
    )(info, *state, own_top, *own, *panel_pieces)


def solution(mesh):
    in_specs = (P("row", "col"), P(None, "row"), P(None, "col"))
    out_specs = P("row", "col")

    return jax.shard_map(shards, mesh=mesh, in_specs=in_specs, out_specs=out_specs, check_vma=False)
```

```python
import functools


import jax
import jax.numpy as jnp
from jax import lax
from jax.experimental import pallas as pl
from jax.experimental.pallas import tpu as pltpu
from jax.sharding import PartitionSpec as P

PW = 256
PANELS = 2
LEAD = PW * PANELS
SPLIT = LEAD // 2

SUB = 8
BLK = 128


def swapped(x, axis, mask):
    return lax.ppermute(x, axis, [(i, i ^ mask) for i in range(lax.axis_size(axis))])


def hdot(left, right):
    return jnp.dot(left, right, precision=lax.Precision.HIGHEST, preferred_element_type=jnp.float32)


def tree_sum(terms):
    while len(terms) > 1:
        terms = [terms[i] + terms[i + 1] if i + 1 < len(terms) else terms[i] for i in range(0, len(terms), 2)]
    return terms[0]


def factor(block):
    count = BLK // SUB
    shape = (SUB, BLK)
    sub = lax.broadcasted_iota(jnp.int32, shape, 0)
    lane = lax.broadcasted_iota(jnp.int32, shape, 1)

    def row(x, j):
        return jnp.broadcast_to(x[j : j + 1, :], shape)

    def col(x, j):
        return jnp.broadcast_to(x[:, j : j + 1], shape)

    strips = [block[SUB * i : SUB * (i + 1)] for i in range(count)]
    extra = [jnp.where(lane == sub + SUB * i, 1.0, 0.0) for i in range(count)]
    pending = [jnp.zeros(shape, jnp.float32) for _ in range(count)]
    upper = []
    small = []
    for t in range(count):
        base = SUB * t
        inside = (lane >= base) & (lane < base + SUB)
        for i in range(t, count):
            pending[i] = jnp.where(inside, strips[i], pending[i])
        c = [col(strips[t], base + m) for m in range(SUB)]
        w, x, forward = strips[t], extra[t], strips[t]
        g = jnp.where(lane == sub + base, 1.0, 0.0)
        for j in range(SUB):
            r = 1.0 / row(c[j], j)
            here = sub == j
            cj = c[j]
            for m in range(j + 1, SUB):
                scaled = row(c[m], j) * r
                c[m] = jnp.where(here, scaled, c[m] - cj * scaled)
            scaled = row(w, j) * r
            w = jnp.where(here, scaled, w - cj * scaled)
            scaled = row(x, j) * r
            x = jnp.where(here, scaled, x - cj * scaled)
            scaled = row(g, j) * r
            g = jnp.where(sub > j, g, jnp.where(here, scaled, g - cj * scaled))
            if j < SUB - 1:
                forward = jnp.where(sub > j, forward - (cj * r) * row(forward, j), forward)
        upper.append(forward)
        small.append(g)
        w_rows = [row(w, m) for m in range(SUB)]
        x_rows = [row(x, m) for m in range(SUB)]
        for i in list(range(t + 1, count)) + list(range(t)):
            b = [col(strips[i], base + m) for m in range(SUB)]
            strips[i] = strips[i] - tree_sum([b[m] * w_rows[m] for m in range(SUB)])
            extra[i] = extra[i] - tree_sum([b[m] * x_rows[m] for m in range(SUB)])
        strips[t], extra[t] = w, x
    upper, pending, small, inverse = (jnp.concatenate(v, 0) for v in (upper, pending, small, extra))
    return upper, hdot(pending, small), inverse


def eliminate_block(k, work, packed, inverted):
    blocks = LEAD // BLK
    here = pl.ds(BLK * k, BLK)
    upper, lower, inverse = factor(work[k, here, :])
    size = (BLK, BLK)
    above = lax.broadcasted_iota(jnp.int32, size, 0) <= lax.broadcasted_iota(jnp.int32, size, 1)
    upper = jnp.where(above, upper, 0.0)
    packed[k, here, :] = jnp.where(above, upper, lower)
    upper_inverse = hdot(inverse, lower)
    inverted[here, :] = upper_inverse
    work[k, here, :] = inverse
    later = range(k + 1, blocks)
    solved = {j: hdot(inverse, work[j, here, :]) for j in later}
    if k + 1 < blocks:
        rest = pl.ds(BLK * (k + 1), LEAD - BLK * (k + 1))
        left = work[k, rest, :]
        for j in later:
            work[j, rest, :] = work[j, rest, :] - hdot(left, solved[j])
        packed[k, rest, :] = hdot(left, upper_inverse)
    for j in later:
        packed[j, here, :] = hdot(upper, solved[j])
        work[j, here, :] = solved[j]


def first_kernel(info, *refs):
    blocks = LEAD // BLK
    pieces, (work, packed, inverted) = refs[:blocks], refs[blocks:]
    for n in range(blocks):
        work[info[3] ^ n] = pieces[n][...]
    eliminate_block(0, work, packed, inverted)


def next_kernel(k, old_work, old_packed, old_inverted, work, packed, inverted):
    eliminate_block(k, work, packed, inverted)


def last_kernel(info, work, packed, inverted, own_top, *refs):
    blocks = LEAD // BLK
    own, pieces = refs[:2], refs[2 : 2 + 2 * blocks]
    out, rhs, reduced, top = refs[2 + 2 * blocks :]
    is_panel = info[0] == 1
    slot = info[1]
    is_top = info[2] == 1
    rhs[...] = own_top[...]
    size = (BLK, BLK)
    above = lax.broadcasted_iota(jnp.int32, size, 0) <= lax.broadcasted_iota(jnp.int32, size, 1)
    for k in range(blocks):
        here = pl.ds(BLK * k, BLK)
        solved = hdot(work[k, here, :], rhs[here, :])
        for i in range(k + 1, blocks):
            there = pl.ds(BLK * i, BLK)
            rhs[there, :] = rhs[there, :] - hdot(work[k, there, :], solved)
        upper = jnp.where(above, packed[k, here, :], 0.0)
        top[here, :] = jnp.where(is_panel, packed[slot, here, :], hdot(upper, solved))
        mine = jnp.where(slot == k, inverted[here, :], 0.0)
        reduced[here, :] = jnp.where(is_panel, mine, solved)
    for k in range(blocks - 2, -1, -1):
        here = pl.ds(BLK * k, BLK)
        terms = [hdot(work[j, here, :], reduced[pl.ds(BLK * j, BLK), :]) for j in range(k + 1, blocks)]
        reduced[here, :] = reduced[here, :] - tree_sum(terms)
    runs = pieces[0].shape[0] // SPLIT

    def below(part, run):
        where = pl.ds(pl.multiple_of(run * SPLIT, SPLIT), SPLIT)
        terms = []
        for n in range(blocks):
            block = pl.ds(pl.multiple_of((info[3] ^ n) * BLK, BLK), BLK)
            terms.append(hdot(pieces[2 * n + part][where, :], reduced[block, :]))
        total = tree_sum(terms)
        return jnp.where(is_panel, total, own[part][where, :] - total)

    for part in range(2):
        where = pl.ds(SPLIT * part, SPLIT)
        out[where, :] = jnp.where(is_top, top[where, :], below(part, 0))

    def step(run):
        for part in range(2):
            rows = pl.ds(pl.multiple_of(run * LEAD, LEAD) + SPLIT * part, SPLIT)
            out[rows, :] = below(part, run)

    if runs <= 2:
        for run in range(1, runs):
            step(run)
    else:
        pl.loop(1, runs)(step)


def shards(matrix, row_diag, col_diag):
    height, width = matrix.shape
    row_pos = lax.axis_index("row")
    col_pos = lax.axis_index("col")
    half = height // 2
    blocks = LEAD // width
    block_bits = blocks.bit_length() - 1
    high_bit = lax.axis_size("col").bit_length() - 2
    high, low = 2**high_bit, 2 ** (high_bit - 1)
    is_first = row_pos == 0
    in_high = (col_pos & high) != 0
    in_low = (col_pos & low) != 0
    part_rows = half // 2

    def parts_of(values):
        grouped = values.reshape(2, half // LEAD, 2, SPLIT, *values.shape[1:])
        return [grouped[:, :, p].reshape(2, part_rows, *values.shape[1:]) for p in range(2)]

    rows_p, rows_q = parts_of(matrix)
    other_p = swapped(rows_p, "row", 1)
    near_q = swapped(rows_q, "col", low)
    other_rows = swapped(row_diag, "row", 1)
    pair = jnp.concatenate([col_diag, swapped(col_diag, "col", low)], 0)
    far_pair = swapped(pair, "col", high)

    def diag_of(h, l):
        chosen = jnp.where(in_high == h, pair, far_pair)
        return jnp.where(in_low == l, chosen[:2], chosen[2:])

    none, yes = jnp.bool_(False), jnp.bool_(True)

    def of_half(parts, h, l):
        even, odd = parts
        sign = jnp.where(in_high & h, -0.5, 0.5)
        scale_even = sign * diag_of(h, none)[0]
        scale_odd = jnp.where(l, -sign, sign) * diag_of(h, yes)[0]
        return scale_even * even + scale_odd * odd

    def of_bit(parts, h, l):
        scale = jnp.where(in_low & l, -0.5, 0.5) * diag_of(h, in_low)[0]
        return scale * (parts[0] + jnp.where(h, -parts[1], parts[1]))

    first_diag = jnp.where(is_first, row_diag, other_rows)
    own_scales = [parts_of(row_diag[level]) for level in range(2)]
    first_scales = [parts_of(first_diag[level]) for level in range(2)]

    def own_mixed(part, local, remote):
        scale0, scale1 = own_scales[0][part][..., None], own_scales[1][part][..., None]
        mixed = scale0 * jnp.where(is_first, local + remote, remote - local)
        return 0.5 * scale1[0] * (mixed[0] + mixed[1]), 0.5 * scale1[1] * (mixed[0] - mixed[1])

    def lead_mixed(part, values):
        scale0 = first_scales[0][part][:, :SPLIT, None]
        scale1 = first_scales[1][part][0, :SPLIT, None]
        return 0.5 * scale1 * (scale0[0] * values[0][:SPLIT] + scale0[1] * values[1][:SPLIT])

    even_q = jnp.where(in_low, near_q, rows_q)
    odd_q = jnp.where(in_low, rows_q, near_q)
    lead_own = lead_mixed(0, [rows_p[i, :SPLIT] + other_p[i, :SPLIT] for i in range(2)])
    lead_own = (0.5 * diag_of(none, in_low)[0]) * lead_own
    lead_half = lead_mixed(1, of_half((even_q[:, :SPLIT], odd_q[:, :SPLIT]), none, none))
    lead_p = lead_own + swapped(lead_own, "col", high)
    lead_q = lead_half + swapped(lead_half, "row", 1)
    near_lead = swapped(lead_p, "col", low)
    far_lead = swapped(lead_q, "col", high)

    def spread(values):
        for bit in range(block_bits, high_bit - 1):
            arrived = swapped(values, "col", 2**bit)
            values = jnp.where((col_pos & 2**bit) != 0, arrived, values)
        return values

    def gather(values):
        pieces = {0: values}
        for bit in range(block_bits - 1, -1, -1):
            for n in sorted(pieces):
                pieces[n ^ 2**bit] = swapped(pieces[n], "col", 2**bit)
        return [pieces[n] for n in range(blocks)]

    lead_scale = diag_of(none, none)[1]
    lead = lead_scale * jnp.concatenate([lead_p + near_lead, lead_q + far_lead], 0)
    lead_pieces = gather(spread(lead))

    def flat(values):
        return values.reshape(2 * part_rows, width)

    own_p = jnp.stack(own_mixed(0, rows_p, other_p))
    far_own = swapped(own_p, "col", high)
    other_q = swapped(even_q, "row", 1), swapped(odd_q, "row", 1)
    parts_q = [flat(jnp.stack(own_mixed(1, a, b))) for a, b in zip((even_q, odd_q), other_q)]
    panel_q = of_half(parts_q, none, none)
    far_q = swapped(panel_q, "col", high)
    received_q = swapped(of_half(parts_q, ~in_high, in_low), "col", high)
    parts_p = flat(jnp.where(in_high, far_own, own_p)), flat(jnp.where(in_high, own_p, far_own))
    panel_p = of_bit(parts_p, none, none)
    near_p = swapped(panel_p, "col", low)
    received_p = swapped(of_bit(parts_p, in_high, ~in_low), "col", low)

    info = jnp.stack(
        [
            (col_pos < blocks).astype(jnp.int32),
            jnp.minimum(col_pos, blocks - 1).astype(jnp.int32),
            is_first.astype(jnp.int32),
            (col_pos & (blocks - 1)).astype(jnp.int32),
        ]
    )
    smem = pl.BlockSpec(memory_space=pltpu.SMEM)
    vmem = pl.BlockSpec(memory_space=pltpu.VMEM)
    cost = pl.CostEstimate(flops=4_000_000_000, bytes_accessed=12_000_000, transcendentals=0)
    size = 4 * width * (5 * blocks * LEAD + (blocks + 4) * (height + LEAD))
    params = pltpu.CompilerParams(vmem_limit_bytes=2 * size)
    stack = jax.ShapeDtypeStruct((blocks, LEAD, width), jnp.float32)
    state_shapes = (stack, stack, jax.ShapeDtypeStruct((LEAD, width), jnp.float32))
    state = pl.pallas_call(
        first_kernel,
        out_shape=state_shapes,
        in_specs=[smem] + [vmem] * blocks,
        out_specs=(vmem,) * 3,
        cost_estimate=cost,
        compiler_params=params,
        name="eliminate_0",
    )(info, *lead_pieces)
    kept_p, kept_q = of_bit(parts_p, in_high, in_low), of_half(parts_q, in_high, in_low)
    scale = diag_of(in_high, in_low)[1]

    for k in range(1, blocks):
        state = pl.pallas_call(
            functools.partial(next_kernel, k),
            out_shape=state_shapes,
            in_specs=[vmem] * 3,
            out_specs=(vmem,) * 3,
            input_output_aliases={0: 0, 1: 1, 2: 2},
            cost_estimate=cost,
            compiler_params=params,
        )(*state)
        if k == 1:
            near_p, far_q, received_p, received_q, *state = lax.optimization_barrier(
                (near_p, far_q, received_p, received_q, *state)
            )
            panel_p = spread(lead_scale * (panel_p + near_p))
            pieces_p = gather(panel_p)
            panel_q, _ = lax.optimization_barrier((panel_q, panel_p))
            pieces_q = gather(spread(lead_scale * (panel_q + far_q)))
            own = scale * (kept_p + received_p), scale * (kept_q + received_q)
            own_top = jnp.concatenate([v[:SPLIT] for v in own], 0)
            far_top = lax.ppermute(own_top, "row", [(0, 1)])
    far_top, *state = lax.optimization_barrier((far_top, *state))
    own_top = jnp.where(is_first, own_top, far_top)
    panel_pieces = [v for pq in zip(pieces_p, pieces_q) for v in pq]

    return pl.pallas_call(
        last_kernel,
        out_shape=jax.ShapeDtypeStruct((height, width), jnp.float32),
        in_specs=[smem] + [vmem] * (2 * blocks + 6),
        out_specs=vmem,
        scratch_shapes=[pltpu.VMEM((LEAD, width), jnp.float32)] * 3,
        cost_estimate=cost,
        compiler_params=params,
        name="own_columns",
    )(info, *state, own_top, *own, *panel_pieces)


def solution(mesh):
    in_specs = (P("row", "col"), P(None, "row"), P(None, "col"))
    out_specs = P("row", "col")

    return jax.shard_map(shards, mesh=mesh, in_specs=in_specs, out_specs=out_specs, check_vma=False)
```

```python
import functools


import jax
import jax.numpy as jnp
from jax import lax
from jax.experimental import pallas as pl
from jax.experimental.pallas import tpu as pltpu
from jax.sharding import PartitionSpec as P

PW = 256
PANELS = 2
LEAD = PW * PANELS
SPLIT = LEAD // 2

SUB = 8
BLK = 128


def swapped(x, axis, mask):
    return lax.ppermute(x, axis, [(i, i ^ mask) for i in range(lax.axis_size(axis))])


def hdot(left, right):
    return jnp.dot(left, right, precision=lax.Precision.HIGHEST, preferred_element_type=jnp.float32)


def tree_sum(terms):
    while len(terms) > 1:
        terms = [terms[i] + terms[i + 1] if i + 1 < len(terms) else terms[i] for i in range(0, len(terms), 2)]
    return terms[0]


def factor(block):
    count = BLK // SUB
    shape = (SUB, BLK)
    sub = lax.broadcasted_iota(jnp.int32, shape, 0)
    lane = lax.broadcasted_iota(jnp.int32, shape, 1)

    def row(x, j):
        return jnp.broadcast_to(x[j : j + 1, :], shape)

    def col(x, j):
        return jnp.broadcast_to(x[:, j : j + 1], shape)

    strips = [block[SUB * i : SUB * (i + 1)] for i in range(count)]
    extra = [jnp.where(lane == sub + SUB * i, 1.0, 0.0) for i in range(count)]
    pending = [jnp.zeros(shape, jnp.float32) for _ in range(count)]
    upper = []
    small = []
    for t in range(count):
        base = SUB * t
        inside = (lane >= base) & (lane < base + SUB)
        for i in range(t, count):
            pending[i] = jnp.where(inside, strips[i], pending[i])
        c = [col(strips[t], base + m) for m in range(SUB)]
        w, x, forward = strips[t], extra[t], strips[t]
        g = jnp.where(lane == sub + base, 1.0, 0.0)
        for j in range(SUB):
            r = 1.0 / row(c[j], j)
            here = sub == j
            cj = c[j]
            for m in range(j + 1, SUB):
                scaled = row(c[m], j) * r
                c[m] = jnp.where(here, scaled, c[m] - cj * scaled)
            scaled = row(w, j) * r
            w = jnp.where(here, scaled, w - cj * scaled)
            scaled = row(x, j) * r
            x = jnp.where(here, scaled, x - cj * scaled)
            scaled = row(g, j) * r
            g = jnp.where(sub > j, g, jnp.where(here, scaled, g - cj * scaled))
            if j < SUB - 1:
                forward = jnp.where(sub > j, forward - (cj * r) * row(forward, j), forward)
        upper.append(forward)
        small.append(g)
        w_rows = [row(w, m) for m in range(SUB)]
        x_rows = [row(x, m) for m in range(SUB)]
        for i in list(range(t + 1, count)) + list(range(t)):
            b = [col(strips[i], base + m) for m in range(SUB)]
            strips[i] = strips[i] - tree_sum([b[m] * w_rows[m] for m in range(SUB)])
            extra[i] = extra[i] - tree_sum([b[m] * x_rows[m] for m in range(SUB)])
        strips[t], extra[t] = w, x
    upper, pending, small, inverse = (jnp.concatenate(v, 0) for v in (upper, pending, small, extra))
    return upper, hdot(pending, small), inverse


def eliminate_block(k, work, packed, inverted):
    blocks = LEAD // BLK
    here = pl.ds(BLK * k, BLK)
    upper, lower, inverse = factor(work[k, here, :])
    size = (BLK, BLK)
    above = lax.broadcasted_iota(jnp.int32, size, 0) <= lax.broadcasted_iota(jnp.int32, size, 1)
    upper = jnp.where(above, upper, 0.0)
    packed[k, here, :] = jnp.where(above, upper, lower)
    upper_inverse = hdot(inverse, lower)
    inverted[here, :] = upper_inverse
    work[k, here, :] = inverse
    later = range(k + 1, blocks)
    solved = {j: hdot(inverse, work[j, here, :]) for j in later}
    if k + 1 < blocks:
        rest = pl.ds(BLK * (k + 1), LEAD - BLK * (k + 1))
        left = work[k, rest, :]
        for j in later:
            work[j, rest, :] = work[j, rest, :] - hdot(left, solved[j])
        packed[k, rest, :] = hdot(left, upper_inverse)
    for j in later:
        packed[j, here, :] = hdot(upper, solved[j])
        work[j, here, :] = solved[j]


def first_kernel(info, *refs):
    blocks = LEAD // BLK
    pieces, (work, packed, inverted) = refs[:blocks], refs[blocks:]
    for n in range(blocks):
        work[info[3] ^ n] = pieces[n][...]
    eliminate_block(0, work, packed, inverted)


def next_kernel(k, old_work, old_packed, old_inverted, work, packed, inverted):
    eliminate_block(k, work, packed, inverted)


def last_kernel(info, work, packed, inverted, own_top, *refs):
    blocks = LEAD // BLK
    own, pieces = refs[:2], refs[2 : 2 + 2 * blocks]
    out, rhs, reduced, top = refs[2 + 2 * blocks :]
    is_panel = info[0] == 1
    slot = info[1]
    is_top = info[2] == 1
    rhs[...] = own_top[...]
    size = (BLK, BLK)
    above = lax.broadcasted_iota(jnp.int32, size, 0) <= lax.broadcasted_iota(jnp.int32, size, 1)
    for k in range(blocks):
        here = pl.ds(BLK * k, BLK)
        solved = hdot(work[k, here, :], rhs[here, :])
        for i in range(k + 1, blocks):
            there = pl.ds(BLK * i, BLK)
            rhs[there, :] = rhs[there, :] - hdot(work[k, there, :], solved)
        upper = jnp.where(above, packed[k, here, :], 0.0)
        top[here, :] = jnp.where(is_panel, packed[slot, here, :], hdot(upper, solved))
        mine = jnp.where(slot == k, inverted[here, :], 0.0)
        reduced[here, :] = jnp.where(is_panel, mine, solved)
    for k in range(blocks - 2, -1, -1):
        here = pl.ds(BLK * k, BLK)
        terms = [hdot(work[j, here, :], reduced[pl.ds(BLK * j, BLK), :]) for j in range(k + 1, blocks)]
        reduced[here, :] = reduced[here, :] - tree_sum(terms)
    runs = pieces[0].shape[0] // SPLIT

    def below(part, run):
        where = pl.ds(pl.multiple_of(run * SPLIT, SPLIT), SPLIT)
        terms = []
        for n in range(blocks):
            block = pl.ds(pl.multiple_of((info[3] ^ n) * BLK, BLK), BLK)
            terms.append(hdot(pieces[2 * n + part][where, :], reduced[block, :]))
        total = tree_sum(terms)
        return jnp.where(is_panel, total, own[part][where, :] - total)

    for part in range(2):
        where = pl.ds(SPLIT * part, SPLIT)
        out[where, :] = jnp.where(is_top, top[where, :], below(part, 0))

    def step(run):
        for part in range(2):
            rows = pl.ds(pl.multiple_of(run * LEAD, LEAD) + SPLIT * part, SPLIT)
            out[rows, :] = below(part, run)

    if runs <= 2:
        for run in range(1, runs):
            step(run)
    else:
        pl.loop(1, runs)(step)


def shards(matrix, row_diag, col_diag):
    height, width = matrix.shape
    row_pos = lax.axis_index("row")
    col_pos = lax.axis_index("col")
    half = height // 2
    blocks = LEAD // width
    block_bits = blocks.bit_length() - 1
    high_bit = lax.axis_size("col").bit_length() - 2
    high, low = 2**high_bit, 2 ** (high_bit - 1)
    is_first = row_pos == 0
    in_high = (col_pos & high) != 0
    in_low = (col_pos & low) != 0
    part_rows = half // 2

    def parts_of(values):
        grouped = values.reshape(2, half // LEAD, 2, SPLIT, *values.shape[1:])
        return [grouped[:, :, p].reshape(2, part_rows, *values.shape[1:]) for p in range(2)]

    rows_p, rows_q = parts_of(matrix)
    other_p = swapped(rows_p, "row", 1)
    near_q = swapped(rows_q, "col", low)
    other_rows = swapped(row_diag, "row", 1)
    pair = jnp.concatenate([col_diag, swapped(col_diag, "col", low)], 0)
    far_pair = swapped(pair, "col", high)

    def diag_of(h, l):
        chosen = jnp.where(in_high == h, pair, far_pair)
        return jnp.where(in_low == l, chosen[:2], chosen[2:])

    none, yes = jnp.bool_(False), jnp.bool_(True)

    def of_half(parts, h, l):
        even, odd = parts
        sign = jnp.where(in_high & h, -0.5, 0.5)
        scale_even = sign * diag_of(h, none)[0]
        scale_odd = jnp.where(l, -sign, sign) * diag_of(h, yes)[0]
        return scale_even * even + scale_odd * odd

    def of_bit(parts, h, l):
        scale = jnp.where(in_low & l, -0.5, 0.5) * diag_of(h, in_low)[0]
        return scale * (parts[0] + jnp.where(h, -parts[1], parts[1]))

    first_diag = jnp.where(is_first, row_diag, other_rows)
    own_scales = [parts_of(row_diag[level]) for level in range(2)]
    first_scales = [parts_of(first_diag[level]) for level in range(2)]

    def own_mixed(part, local, remote):
        scale0, scale1 = own_scales[0][part][..., None], own_scales[1][part][..., None]
        mixed = scale0 * jnp.where(is_first, local + remote, remote - local)
        return 0.5 * scale1[0] * (mixed[0] + mixed[1]), 0.5 * scale1[1] * (mixed[0] - mixed[1])

    def lead_mixed(part, values):
        scale0 = first_scales[0][part][:, :SPLIT, None]
        scale1 = first_scales[1][part][0, :SPLIT, None]
        return 0.5 * scale1 * (scale0[0] * values[0][:SPLIT] + scale0[1] * values[1][:SPLIT])

    even_q = jnp.where(in_low, near_q, rows_q)
    odd_q = jnp.where(in_low, rows_q, near_q)
    lead_own = lead_mixed(0, [rows_p[i, :SPLIT] + other_p[i, :SPLIT] for i in range(2)])
    lead_own = (0.5 * diag_of(none, in_low)[0]) * lead_own
    lead_half = lead_mixed(1, of_half((even_q[:, :SPLIT], odd_q[:, :SPLIT]), none, none))
    lead_p = lead_own + swapped(lead_own, "col", high)
    lead_q = lead_half + swapped(lead_half, "row", 1)
    near_lead = swapped(lead_p, "col", low)
    far_lead = swapped(lead_q, "col", high)

    def spread(values):
        for bit in range(block_bits, high_bit - 1):
            arrived = swapped(values, "col", 2**bit)
            values = jnp.where((col_pos & 2**bit) != 0, arrived, values)
        return values

    def gather(values):
        pieces = {0: values}
        for bit in range(block_bits - 1, -1, -1):
            for n in sorted(pieces):
                pieces[n ^ 2**bit] = swapped(pieces[n], "col", 2**bit)
        return [pieces[n] for n in range(blocks)]

    lead_scale = diag_of(none, none)[1]
    lead = lead_scale * jnp.concatenate([lead_p + near_lead, lead_q + far_lead], 0)
    lead_pieces = gather(spread(lead))

    def flat(values):
        return values.reshape(2 * part_rows, width)

    own_p = jnp.stack(own_mixed(0, rows_p, other_p))
    far_own = swapped(own_p, "col", high)
    other_q = swapped(even_q, "row", 1), swapped(odd_q, "row", 1)
    parts_q = [flat(jnp.stack(own_mixed(1, a, b))) for a, b in zip((even_q, odd_q), other_q)]
    panel_q = of_half(parts_q, none, none)
    far_q = swapped(panel_q, "col", high)
    info = jnp.stack(
        [
            (col_pos < blocks).astype(jnp.int32),
            jnp.minimum(col_pos, blocks - 1).astype(jnp.int32),
            is_first.astype(jnp.int32),
            (col_pos & (blocks - 1)).astype(jnp.int32),
        ]
    )
    smem = pl.BlockSpec(memory_space=pltpu.SMEM)
    vmem = pl.BlockSpec(memory_space=pltpu.VMEM)
    cost = pl.CostEstimate(flops=4_000_000_000, bytes_accessed=12_000_000, transcendentals=0)
    size = 4 * width * (5 * blocks * LEAD + (blocks + 4) * (height + LEAD))
    params = pltpu.CompilerParams(vmem_limit_bytes=2 * size)
    stack = jax.ShapeDtypeStruct((blocks, LEAD, width), jnp.float32)
    state_shapes = (stack, stack, jax.ShapeDtypeStruct((LEAD, width), jnp.float32))
    state = pl.pallas_call(
        first_kernel,
        out_shape=state_shapes,
        in_specs=[smem] + [vmem] * blocks,
        out_specs=(vmem,) * 3,
        cost_estimate=cost,
        compiler_params=params,
        name="eliminate_0",
    )(info, *lead_pieces)
    far_own, parts_q, *state = lax.optimization_barrier((far_own, parts_q, *state))
    parts_p = flat(jnp.where(in_high, far_own, own_p)), flat(jnp.where(in_high, own_p, far_own))
    panel_p = of_bit(parts_p, none, none)
    near_p = swapped(panel_p, "col", low)
    received_q = swapped(of_half(parts_q, ~in_high, in_low), "col", high)
    received_p = swapped(of_bit(parts_p, in_high, ~in_low), "col", low)
    kept_p, kept_q = of_bit(parts_p, in_high, in_low), of_half(parts_q, in_high, in_low)
    scale = diag_of(in_high, in_low)[1]

    for k in range(1, blocks):
        state = pl.pallas_call(
            functools.partial(next_kernel, k),
            out_shape=state_shapes,
            in_specs=[vmem] * 3,
            out_specs=(vmem,) * 3,
            input_output_aliases={0: 0, 1: 1, 2: 2},
            cost_estimate=cost,
            compiler_params=params,
        )(*state)
        if k == 1:
            near_p, far_q, *state = lax.optimization_barrier((near_p, far_q, *state))
            panel_p = spread(lead_scale * (panel_p + near_p))
            pieces_p = gather(panel_p)
            panel_q, _ = lax.optimization_barrier((panel_q, panel_p))
            pieces_q = gather(spread(lead_scale * (panel_q + far_q)))
        if k == blocks - 2:
            received_p, received_q, *state = lax.optimization_barrier((received_p, received_q, *state))
            own = scale * (kept_p + received_p), scale * (kept_q + received_q)
            own_top = jnp.concatenate([v[:SPLIT] for v in own], 0)
            far_top = lax.ppermute(own_top, "row", [(0, 1)])
    far_top, *state = lax.optimization_barrier((far_top, *state))
    own_top = jnp.where(is_first, own_top, far_top)
    panel_pieces = [v for pq in zip(pieces_p, pieces_q) for v in pq]

    return pl.pallas_call(
        last_kernel,
        out_shape=jax.ShapeDtypeStruct((height, width), jnp.float32),
        in_specs=[smem] + [vmem] * (2 * blocks + 6),
        out_specs=vmem,
        scratch_shapes=[pltpu.VMEM((LEAD, width), jnp.float32)] * 3,
        cost_estimate=cost,
        compiler_params=params,
        name="own_columns",
    )(info, *state, own_top, *own, *panel_pieces)


def solution(mesh):
    in_specs = (P("row", "col"), P(None, "row"), P(None, "col"))
    out_specs = P("row", "col")

    return jax.shard_map(shards, mesh=mesh, in_specs=in_specs, out_specs=out_specs, check_vma=False)
```

```python
import functools


import jax
import jax.numpy as jnp
from jax import lax
from jax.experimental import pallas as pl
from jax.experimental.pallas import tpu as pltpu
from jax.sharding import PartitionSpec as P

PW = 256
PANELS = 2
LEAD = PW * PANELS
SPLIT = LEAD // 2

SUB = 8
BLK = 128


def swapped(x, axis, mask):
    return lax.ppermute(x, axis, [(i, i ^ mask) for i in range(lax.axis_size(axis))])


def hdot(left, right):
    return jnp.dot(left, right, precision=lax.Precision.HIGHEST, preferred_element_type=jnp.float32)


def tree_sum(terms):
    while len(terms) > 1:
        terms = [terms[i] + terms[i + 1] if i + 1 < len(terms) else terms[i] for i in range(0, len(terms), 2)]
    return terms[0]


def factor(block):
    count = BLK // SUB
    shape = (SUB, BLK)
    sub = lax.broadcasted_iota(jnp.int32, shape, 0)
    lane = lax.broadcasted_iota(jnp.int32, shape, 1)

    def row(x, j):
        return jnp.broadcast_to(x[j : j + 1, :], shape)

    def col(x, j):
        return jnp.broadcast_to(x[:, j : j + 1], shape)

    strips = [block[SUB * i : SUB * (i + 1)] for i in range(count)]
    extra = [jnp.where(lane == sub + SUB * i, 1.0, 0.0) for i in range(count)]
    pending = [jnp.zeros(shape, jnp.float32) for _ in range(count)]
    upper = []
    small = []
    for t in range(count):
        base = SUB * t
        inside = (lane >= base) & (lane < base + SUB)
        for i in range(t, count):
            pending[i] = jnp.where(inside, strips[i], pending[i])
        c = [col(strips[t], base + m) for m in range(SUB)]
        w, x, forward = strips[t], extra[t], strips[t]
        g = jnp.where(lane == sub + base, 1.0, 0.0)
        for j in range(SUB):
            r = 1.0 / row(c[j], j)
            here = sub == j
            cj = c[j]
            for m in range(j + 1, SUB):
                scaled = row(c[m], j) * r
                c[m] = jnp.where(here, scaled, c[m] - cj * scaled)
            scaled = row(w, j) * r
            w = jnp.where(here, scaled, w - cj * scaled)
            scaled = row(x, j) * r
            x = jnp.where(here, scaled, x - cj * scaled)
            scaled = row(g, j) * r
            g = jnp.where(sub > j, g, jnp.where(here, scaled, g - cj * scaled))
            if j < SUB - 1:
                forward = jnp.where(sub > j, forward - (cj * r) * row(forward, j), forward)
        upper.append(forward)
        small.append(g)
        w_rows = [row(w, m) for m in range(SUB)]
        x_rows = [row(x, m) for m in range(SUB)]
        for i in list(range(t + 1, count)) + list(range(t)):
            b = [col(strips[i], base + m) for m in range(SUB)]
            strips[i] = strips[i] - tree_sum([b[m] * w_rows[m] for m in range(SUB)])
            extra[i] = extra[i] - tree_sum([b[m] * x_rows[m] for m in range(SUB)])
        strips[t], extra[t] = w, x
    upper, pending, small, inverse = (jnp.concatenate(v, 0) for v in (upper, pending, small, extra))
    return upper, hdot(pending, small), inverse


def eliminate_block(k, work, packed, inverted):
    blocks = LEAD // BLK
    here = pl.ds(BLK * k, BLK)
    upper, lower, inverse = factor(work[k, here, :])
    size = (BLK, BLK)
    above = lax.broadcasted_iota(jnp.int32, size, 0) <= lax.broadcasted_iota(jnp.int32, size, 1)
    upper = jnp.where(above, upper, 0.0)
    packed[k, here, :] = jnp.where(above, upper, lower)
    upper_inverse = hdot(inverse, lower)
    inverted[here, :] = upper_inverse
    work[k, here, :] = inverse
    later = range(k + 1, blocks)
    solved = {j: hdot(inverse, work[j, here, :]) for j in later}
    if k + 1 < blocks:
        rest = pl.ds(BLK * (k + 1), LEAD - BLK * (k + 1))
        left = work[k, rest, :]
        for j in later:
            work[j, rest, :] = work[j, rest, :] - hdot(left, solved[j])
        packed[k, rest, :] = hdot(left, upper_inverse)
    for j in later:
        packed[j, here, :] = hdot(upper, solved[j])
        work[j, here, :] = solved[j]


def first_kernel(info, *refs):
    blocks = LEAD // BLK
    pieces, (work, packed, inverted) = refs[:blocks], refs[blocks:]
    for n in range(blocks):
        work[info[3] ^ n] = pieces[n][...]
    eliminate_block(0, work, packed, inverted)


def next_kernel(k, old_work, old_packed, old_inverted, work, packed, inverted):
    eliminate_block(k, work, packed, inverted)


def last_kernel(info, work, packed, inverted, own_top, *refs):
    blocks = LEAD // BLK
    own, pieces = refs[:2], refs[2 : 2 + 2 * blocks]
    out, rhs, reduced, top = refs[2 + 2 * blocks :]
    is_panel = info[0] == 1
    slot = info[1]
    is_top = info[2] == 1
    rhs[...] = own_top[...]
    size = (BLK, BLK)
    above = lax.broadcasted_iota(jnp.int32, size, 0) <= lax.broadcasted_iota(jnp.int32, size, 1)
    for k in range(blocks):
        here = pl.ds(BLK * k, BLK)
        solved = hdot(work[k, here, :], rhs[here, :])
        for i in range(k + 1, blocks):
            there = pl.ds(BLK * i, BLK)
            rhs[there, :] = rhs[there, :] - hdot(work[k, there, :], solved)
        upper = jnp.where(above, packed[k, here, :], 0.0)
        top[here, :] = jnp.where(is_panel, packed[slot, here, :], hdot(upper, solved))
        mine = jnp.where(slot == k, inverted[here, :], 0.0)
        reduced[here, :] = jnp.where(is_panel, mine, solved)
    for k in range(blocks - 2, -1, -1):
        here = pl.ds(BLK * k, BLK)
        terms = [hdot(work[j, here, :], reduced[pl.ds(BLK * j, BLK), :]) for j in range(k + 1, blocks)]
        reduced[here, :] = reduced[here, :] - tree_sum(terms)
    runs = pieces[0].shape[0] // SPLIT

    def below(part, run):
        where = pl.ds(pl.multiple_of(run * SPLIT, SPLIT), SPLIT)
        terms = []
        for n in range(blocks):
            block = pl.ds(pl.multiple_of((info[3] ^ n) * BLK, BLK), BLK)
            terms.append(hdot(pieces[2 * n + part][where, :], reduced[block, :]))
        total = tree_sum(terms)
        return jnp.where(is_panel, total, own[part][where, :] - total)

    for part in range(2):
        where = pl.ds(SPLIT * part, SPLIT)
        out[where, :] = jnp.where(is_top, top[where, :], below(part, 0))

    def step(run):
        for part in range(2):
            rows = pl.ds(pl.multiple_of(run * LEAD, LEAD) + SPLIT * part, SPLIT)
            out[rows, :] = below(part, run)

    if runs <= 2:
        for run in range(1, runs):
            step(run)
    else:
        pl.loop(1, runs)(step)


def shards(matrix, row_diag, col_diag):
    height, width = matrix.shape
    row_pos = lax.axis_index("row")
    col_pos = lax.axis_index("col")
    half = height // 2
    blocks = LEAD // width
    block_bits = blocks.bit_length() - 1
    high_bit = lax.axis_size("col").bit_length() - 2
    high, low = 2**high_bit, 2 ** (high_bit - 1)
    is_first = row_pos == 0
    in_high = (col_pos & high) != 0
    in_low = (col_pos & low) != 0
    part_rows = half // 2

    def parts_of(values):
        grouped = values.reshape(2, half // LEAD, 2, SPLIT, *values.shape[1:])
        return [grouped[:, :, p].reshape(2, part_rows, *values.shape[1:]) for p in range(2)]

    rows_p, rows_q = parts_of(matrix)
    other_p = swapped(rows_p, "row", 1)
    near_q = swapped(rows_q, "col", low)
    other_rows = swapped(row_diag, "row", 1)
    pair = jnp.concatenate([col_diag, swapped(col_diag, "col", low)], 0)
    far_pair = swapped(pair, "col", high)

    def diag_of(h, l):
        chosen = jnp.where(in_high == h, pair, far_pair)
        return jnp.where(in_low == l, chosen[:2], chosen[2:])

    none, yes = jnp.bool_(False), jnp.bool_(True)

    def of_half(parts, h, l):
        even, odd = parts
        sign = jnp.where(in_high & h, -0.5, 0.5)
        scale_even = sign * diag_of(h, none)[0]
        scale_odd = jnp.where(l, -sign, sign) * diag_of(h, yes)[0]
        return scale_even * even + scale_odd * odd

    def of_bit(parts, h, l):
        scale = jnp.where(in_low & l, -0.5, 0.5) * diag_of(h, in_low)[0]
        return scale * (parts[0] + jnp.where(h, -parts[1], parts[1]))

    first_diag = jnp.where(is_first, row_diag, other_rows)
    own_scales = [parts_of(row_diag[level]) for level in range(2)]
    first_scales = [parts_of(first_diag[level]) for level in range(2)]

    def own_mixed(part, local, remote):
        scale0, scale1 = own_scales[0][part][..., None], own_scales[1][part][..., None]
        mixed = scale0 * jnp.where(is_first, local + remote, remote - local)
        return 0.5 * scale1[0] * (mixed[0] + mixed[1]), 0.5 * scale1[1] * (mixed[0] - mixed[1])

    def lead_mixed(part, values):
        scale0 = first_scales[0][part][:, :SPLIT, None]
        scale1 = first_scales[1][part][0, :SPLIT, None]
        return 0.5 * scale1 * (scale0[0] * values[0][:SPLIT] + scale0[1] * values[1][:SPLIT])

    even_q = jnp.where(in_low, near_q, rows_q)
    odd_q = jnp.where(in_low, rows_q, near_q)
    lead_own = lead_mixed(0, [rows_p[i, :SPLIT] + other_p[i, :SPLIT] for i in range(2)])
    lead_own = (0.5 * diag_of(none, in_low)[0]) * lead_own
    lead_half = lead_mixed(1, of_half((even_q[:, :SPLIT], odd_q[:, :SPLIT]), none, none))
    lead_p = lead_own + swapped(lead_own, "col", high)
    lead_q = lead_half + swapped(lead_half, "row", 1)
    near_lead = swapped(lead_p, "col", low)
    far_lead = swapped(lead_q, "col", high)

    def spread(values):
        for bit in range(block_bits, high_bit - 1):
            arrived = swapped(values, "col", 2**bit)
            values = jnp.where((col_pos & 2**bit) != 0, arrived, values)
        return values

    def gather(values):
        pieces = {0: values}
        for bit in range(block_bits - 1, -1, -1):
            for n in sorted(pieces):
                pieces[n ^ 2**bit] = swapped(pieces[n], "col", 2**bit)
        return [pieces[n] for n in range(blocks)]

    lead_scale = diag_of(none, none)[1]
    lead = lead_scale * jnp.concatenate([lead_p + near_lead, lead_q + far_lead], 0)
    lead_pieces = gather(spread(lead))

    def flat(values):
        return values.reshape(2 * part_rows, width)

    own_p = jnp.stack(own_mixed(0, rows_p, other_p))
    far_own = swapped(own_p, "col", high)
    other_q = swapped(even_q, "row", 1), swapped(odd_q, "row", 1)
    parts_q = [flat(jnp.stack(own_mixed(1, a, b))) for a, b in zip((even_q, odd_q), other_q)]
    panel_q = of_half(parts_q, none, none)
    far_q = swapped(panel_q, "col", high)
    info = jnp.stack(
        [
            (col_pos < blocks).astype(jnp.int32),
            jnp.minimum(col_pos, blocks - 1).astype(jnp.int32),
            is_first.astype(jnp.int32),
            (col_pos & (blocks - 1)).astype(jnp.int32),
        ]
    )
    smem = pl.BlockSpec(memory_space=pltpu.SMEM)
    vmem = pl.BlockSpec(memory_space=pltpu.VMEM)
    cost = pl.CostEstimate(flops=4_000_000_000, bytes_accessed=12_000_000, transcendentals=0)
    size = 4 * width * (5 * blocks * LEAD + (blocks + 4) * (height + LEAD))
    params = pltpu.CompilerParams(vmem_limit_bytes=2 * size)
    stack = jax.ShapeDtypeStruct((blocks, LEAD, width), jnp.float32)
    state_shapes = (stack, stack, jax.ShapeDtypeStruct((LEAD, width), jnp.float32))
    state = pl.pallas_call(
        first_kernel,
        out_shape=state_shapes,
        in_specs=[smem] + [vmem] * blocks,
        out_specs=(vmem,) * 3,
        cost_estimate=cost,
        compiler_params=params,
        name="eliminate_0",
    )(info, *lead_pieces)
    far_own, parts_q, *state = lax.optimization_barrier((far_own, parts_q, *state))
    parts_p = flat(jnp.where(in_high, far_own, own_p)), flat(jnp.where(in_high, own_p, far_own))
    panel_p = of_bit(parts_p, none, none)
    near_p = swapped(panel_p, "col", low)
    received_q = swapped(of_half(parts_q, ~in_high, in_low), "col", high)
    rest_p = of_bit(parts_p, in_high, ~in_low)
    kept_p, kept_q = of_bit(parts_p, in_high, in_low), of_half(parts_q, in_high, in_low)
    scale = diag_of(in_high, in_low)[1]

    for k in range(1, blocks):
        state = pl.pallas_call(
            functools.partial(next_kernel, k),
            out_shape=state_shapes,
            in_specs=[vmem] * 3,
            out_specs=(vmem,) * 3,
            input_output_aliases={0: 0, 1: 1, 2: 2},
            cost_estimate=cost,
            compiler_params=params,
        )(*state)
        if k == 1:
            near_p, far_q, rest_p, *state = lax.optimization_barrier((near_p, far_q, rest_p, *state))
            received_p = swapped(rest_p, "col", low)
            panel_p = spread(lead_scale * (panel_p + near_p))
            pieces_p = gather(panel_p)
            panel_q, _ = lax.optimization_barrier((panel_q, panel_p))
            pieces_q = gather(spread(lead_scale * (panel_q + far_q)))
        if k == blocks - 2:
            received_p, received_q, *state = lax.optimization_barrier((received_p, received_q, *state))
            own = scale * (kept_p + received_p), scale * (kept_q + received_q)
            own_top = jnp.concatenate([v[:SPLIT] for v in own], 0)
            far_top = lax.ppermute(own_top, "row", [(0, 1)])
    far_top, *state = lax.optimization_barrier((far_top, *state))
    own_top = jnp.where(is_first, own_top, far_top)
    panel_pieces = [v for pq in zip(pieces_p, pieces_q) for v in pq]

    return pl.pallas_call(
        last_kernel,
        out_shape=jax.ShapeDtypeStruct((height, width), jnp.float32),
        in_specs=[smem] + [vmem] * (2 * blocks + 6),
        out_specs=vmem,
        scratch_shapes=[pltpu.VMEM((LEAD, width), jnp.float32)] * 3,
        cost_estimate=cost,
        compiler_params=params,
        name="own_columns",
    )(info, *state, own_top, *own, *panel_pieces)


def solution(mesh):
    in_specs = (P("row", "col"), P(None, "row"), P(None, "col"))
    out_specs = P("row", "col")

    return jax.shard_map(shards, mesh=mesh, in_specs=in_specs, out_specs=out_specs, check_vma=False)
```

```python
import functools


import jax
import jax.numpy as jnp
from jax import lax
from jax.experimental import pallas as pl
from jax.experimental.pallas import tpu as pltpu
from jax.sharding import PartitionSpec as P

PW = 256
PANELS = 2
LEAD = PW * PANELS
SPLIT = LEAD // 2

SUB = 8
BLK = 128


def swapped(x, axis, mask):
    return lax.ppermute(x, axis, [(i, i ^ mask) for i in range(lax.axis_size(axis))])


def hdot(left, right):
    return jnp.dot(left, right, precision=lax.Precision.HIGHEST, preferred_element_type=jnp.float32)


def tree_sum(terms):
    while len(terms) > 1:
        terms = [terms[i] + terms[i + 1] if i + 1 < len(terms) else terms[i] for i in range(0, len(terms), 2)]
    return terms[0]


def factor(block):
    count = BLK // SUB
    shape = (SUB, BLK)
    sub = lax.broadcasted_iota(jnp.int32, shape, 0)
    lane = lax.broadcasted_iota(jnp.int32, shape, 1)

    def row(x, j):
        return jnp.broadcast_to(x[j : j + 1, :], shape)

    def col(x, j):
        return jnp.broadcast_to(x[:, j : j + 1], shape)

    strips = [block[SUB * i : SUB * (i + 1)] for i in range(count)]
    extra = [jnp.where(lane == sub + SUB * i, 1.0, 0.0) for i in range(count)]
    pending = [jnp.zeros(shape, jnp.float32) for _ in range(count)]
    upper = []
    small = []
    for t in range(count):
        base = SUB * t
        inside = (lane >= base) & (lane < base + SUB)
        for i in range(t, count):
            pending[i] = jnp.where(inside, strips[i], pending[i])
        c = [col(strips[t], base + m) for m in range(SUB)]
        w, x, forward = strips[t], extra[t], strips[t]
        g = jnp.where(lane == sub + base, 1.0, 0.0)
        for j in range(SUB):
            r = 1.0 / row(c[j], j)
            here = sub == j
            cj = c[j]
            for m in range(j + 1, SUB):
                scaled = row(c[m], j) * r
                c[m] = jnp.where(here, scaled, c[m] - cj * scaled)
            scaled = row(w, j) * r
            w = jnp.where(here, scaled, w - cj * scaled)
            scaled = row(x, j) * r
            x = jnp.where(here, scaled, x - cj * scaled)
            scaled = row(g, j) * r
            g = jnp.where(sub > j, g, jnp.where(here, scaled, g - cj * scaled))
            if j < SUB - 1:
                forward = jnp.where(sub > j, forward - (cj * r) * row(forward, j), forward)
        upper.append(forward)
        small.append(g)
        w_rows = [row(w, m) for m in range(SUB)]
        x_rows = [row(x, m) for m in range(SUB)]
        for i in list(range(t + 1, count)) + list(range(t)):
            b = [col(strips[i], base + m) for m in range(SUB)]
            strips[i] = strips[i] - tree_sum([b[m] * w_rows[m] for m in range(SUB)])
            extra[i] = extra[i] - tree_sum([b[m] * x_rows[m] for m in range(SUB)])
        strips[t], extra[t] = w, x
    upper, pending, small, inverse = (jnp.concatenate(v, 0) for v in (upper, pending, small, extra))
    return upper, hdot(pending, small), inverse


def eliminate_block(k, work, packed, inverted):
    blocks = LEAD // BLK
    here = pl.ds(BLK * k, BLK)
    upper, lower, inverse = factor(work[k, here, :])
    size = (BLK, BLK)
    above = lax.broadcasted_iota(jnp.int32, size, 0) <= lax.broadcasted_iota(jnp.int32, size, 1)
    upper = jnp.where(above, upper, 0.0)
    packed[k, here, :] = jnp.where(above, upper, lower)
    upper_inverse = hdot(inverse, lower)
    inverted[here, :] = upper_inverse
    work[k, here, :] = inverse
    later = range(k + 1, blocks)
    solved = {j: hdot(inverse, work[j, here, :]) for j in later}
    if k + 1 < blocks:
        rest = pl.ds(BLK * (k + 1), LEAD - BLK * (k + 1))
        left = work[k, rest, :]
        for j in later:
            work[j, rest, :] = work[j, rest, :] - hdot(left, solved[j])
        packed[k, rest, :] = hdot(left, upper_inverse)
        work[k, rest, :] = hdot(left, inverse)
    for j in later:
        packed[j, here, :] = hdot(upper, solved[j])
        work[j, here, :] = solved[j]


def first_kernel(info, *refs):
    blocks = LEAD // BLK
    pieces, (work, packed, inverted) = refs[:blocks], refs[blocks:]
    for n in range(blocks):
        work[info[3] ^ n] = pieces[n][...]
    eliminate_block(0, work, packed, inverted)


def next_kernel(k, old_work, old_packed, old_inverted, work, packed, inverted):
    eliminate_block(k, work, packed, inverted)


def last_kernel(info, work, packed, inverted, own_top, *refs):
    blocks = LEAD // BLK
    own, pieces = refs[:2], refs[2 : 2 + 2 * blocks]
    out, rhs, reduced, top = refs[2 + 2 * blocks :]
    is_panel = info[0] == 1
    slot = info[1]
    is_top = info[2] == 1
    rhs[...] = own_top[...]
    size = (BLK, BLK)
    above = lax.broadcasted_iota(jnp.int32, size, 0) <= lax.broadcasted_iota(jnp.int32, size, 1)
    for k in range(blocks):
        here = pl.ds(BLK * k, BLK)
        solved = hdot(work[k, here, :], rhs[here, :])
        for i in range(k + 1, blocks):
            there = pl.ds(BLK * i, BLK)
            rhs[there, :] = rhs[there, :] - hdot(work[k, there, :], rhs[here, :])
        upper = jnp.where(above, packed[k, here, :], 0.0)
        top[here, :] = jnp.where(is_panel, packed[slot, here, :], hdot(upper, solved))
        mine = jnp.where(slot == k, inverted[here, :], 0.0)
        reduced[here, :] = jnp.where(is_panel, mine, solved)
    for k in range(blocks - 2, -1, -1):
        here = pl.ds(BLK * k, BLK)
        terms = [hdot(work[j, here, :], reduced[pl.ds(BLK * j, BLK), :]) for j in range(k + 1, blocks)]
        reduced[here, :] = reduced[here, :] - tree_sum(terms)
    runs = pieces[0].shape[0] // SPLIT

    def below(part, run):
        where = pl.ds(pl.multiple_of(run * SPLIT, SPLIT), SPLIT)
        terms = []
        for n in range(blocks):
            block = pl.ds(pl.multiple_of((info[3] ^ n) * BLK, BLK), BLK)
            terms.append(hdot(pieces[2 * n + part][where, :], reduced[block, :]))
        total = tree_sum(terms)
        return jnp.where(is_panel, total, own[part][where, :] - total)

    for part in range(2):
        where = pl.ds(SPLIT * part, SPLIT)
        out[where, :] = jnp.where(is_top, top[where, :], below(part, 0))

    def step(run):
        for part in range(2):
            rows = pl.ds(pl.multiple_of(run * LEAD, LEAD) + SPLIT * part, SPLIT)
            out[rows, :] = below(part, run)

    if runs <= 2:
        for run in range(1, runs):
            step(run)
    else:
        pl.loop(1, runs)(step)


def shards(matrix, row_diag, col_diag):
    height, width = matrix.shape
    row_pos = lax.axis_index("row")
    col_pos = lax.axis_index("col")
    half = height // 2
    blocks = LEAD // width
    block_bits = blocks.bit_length() - 1
    high_bit = lax.axis_size("col").bit_length() - 2
    high, low = 2**high_bit, 2 ** (high_bit - 1)
    is_first = row_pos == 0
    in_high = (col_pos & high) != 0
    in_low = (col_pos & low) != 0
    part_rows = half // 2

    def parts_of(values):
        grouped = values.reshape(2, half // LEAD, 2, SPLIT, *values.shape[1:])
        return [grouped[:, :, p].reshape(2, part_rows, *values.shape[1:]) for p in range(2)]

    rows_p, rows_q = parts_of(matrix)
    other_p = swapped(rows_p, "row", 1)
    near_q = swapped(rows_q, "col", low)
    other_rows = swapped(row_diag, "row", 1)
    pair = jnp.concatenate([col_diag, swapped(col_diag, "col", low)], 0)
    far_pair = swapped(pair, "col", high)

    def diag_of(h, l):
        chosen = jnp.where(in_high == h, pair, far_pair)
        return jnp.where(in_low == l, chosen[:2], chosen[2:])

    none, yes = jnp.bool_(False), jnp.bool_(True)

    def of_half(parts, h, l):
        even, odd = parts
        sign = jnp.where(in_high & h, -0.5, 0.5)
        scale_even = sign * diag_of(h, none)[0]
        scale_odd = jnp.where(l, -sign, sign) * diag_of(h, yes)[0]
        return scale_even * even + scale_odd * odd

    def of_bit(parts, h, l):
        scale = jnp.where(in_low & l, -0.5, 0.5) * diag_of(h, in_low)[0]
        return scale * (parts[0] + jnp.where(h, -parts[1], parts[1]))

    first_diag = jnp.where(is_first, row_diag, other_rows)
    own_scales = [parts_of(row_diag[level]) for level in range(2)]
    first_scales = [parts_of(first_diag[level]) for level in range(2)]

    def own_mixed(part, local, remote):
        scale0, scale1 = own_scales[0][part][..., None], own_scales[1][part][..., None]
        mixed = scale0 * jnp.where(is_first, local + remote, remote - local)
        return 0.5 * scale1[0] * (mixed[0] + mixed[1]), 0.5 * scale1[1] * (mixed[0] - mixed[1])

    def lead_mixed(part, values):
        scale0 = first_scales[0][part][:, :SPLIT, None]
        scale1 = first_scales[1][part][0, :SPLIT, None]
        return 0.5 * scale1 * (scale0[0] * values[0][:SPLIT] + scale0[1] * values[1][:SPLIT])

    even_q = jnp.where(in_low, near_q, rows_q)
    odd_q = jnp.where(in_low, rows_q, near_q)
    lead_own = lead_mixed(0, [rows_p[i, :SPLIT] + other_p[i, :SPLIT] for i in range(2)])
    lead_own = (0.5 * diag_of(none, in_low)[0]) * lead_own
    lead_half = lead_mixed(1, of_half((even_q[:, :SPLIT], odd_q[:, :SPLIT]), none, none))
    lead_p = lead_own + swapped(lead_own, "col", high)
    lead_q = lead_half + swapped(lead_half, "row", 1)
    near_lead = swapped(lead_p, "col", low)
    far_lead = swapped(lead_q, "col", high)

    def spread(values):
        for bit in range(block_bits, high_bit - 1):
            arrived = swapped(values, "col", 2**bit)
            values = jnp.where((col_pos & 2**bit) != 0, arrived, values)
        return values

    def gather(values):
        pieces = {0: values}
        for bit in range(block_bits - 1, -1, -1):
            for n in sorted(pieces):
                pieces[n ^ 2**bit] = swapped(pieces[n], "col", 2**bit)
        return [pieces[n] for n in range(blocks)]

    lead_scale = diag_of(none, none)[1]
    lead = lead_scale * jnp.concatenate([lead_p + near_lead, lead_q + far_lead], 0)
    lead_pieces = gather(spread(lead))

    def flat(values):
        return values.reshape(2 * part_rows, width)

    own_p = jnp.stack(own_mixed(0, rows_p, other_p))
    far_own = swapped(own_p, "col", high)
    other_q = swapped(even_q, "row", 1), swapped(odd_q, "row", 1)
    parts_q = [flat(jnp.stack(own_mixed(1, a, b))) for a, b in zip((even_q, odd_q), other_q)]
    panel_q = of_half(parts_q, none, none)
    far_q = swapped(panel_q, "col", high)
    parts_p = flat(jnp.where(in_high, far_own, own_p)), flat(jnp.where(in_high, own_p, far_own))
    panel_p = of_bit(parts_p, none, none)
    near_p = swapped(panel_p, "col", low)

    info = jnp.stack(
        [
            (col_pos < blocks).astype(jnp.int32),
            jnp.minimum(col_pos, blocks - 1).astype(jnp.int32),
            is_first.astype(jnp.int32),
            (col_pos & (blocks - 1)).astype(jnp.int32),
        ]
    )
    smem = pl.BlockSpec(memory_space=pltpu.SMEM)
    vmem = pl.BlockSpec(memory_space=pltpu.VMEM)
    cost = pl.CostEstimate(flops=4_000_000_000, bytes_accessed=12_000_000, transcendentals=0)
    size = 4 * width * (5 * blocks * LEAD + (blocks + 4) * (height + LEAD))
    params = pltpu.CompilerParams(vmem_limit_bytes=2 * size)
    stack = jax.ShapeDtypeStruct((blocks, LEAD, width), jnp.float32)
    state_shapes = (stack, stack, jax.ShapeDtypeStruct((LEAD, width), jnp.float32))
    state = pl.pallas_call(
        first_kernel,
        out_shape=state_shapes,
        in_specs=[smem] + [vmem] * blocks,
        out_specs=(vmem,) * 3,
        cost_estimate=cost,
        compiler_params=params,
        name="eliminate_0",
    )(info, *lead_pieces)
    parts_p, parts_q, *state = lax.optimization_barrier((parts_p, parts_q, *state))
    received_q = swapped(of_half(parts_q, ~in_high, in_low), "col", high)
    received_p = swapped(of_bit(parts_p, in_high, ~in_low), "col", low)
    kept_p, kept_q = of_bit(parts_p, in_high, in_low), of_half(parts_q, in_high, in_low)
    scale = diag_of(in_high, in_low)[1]

    for k in range(1, blocks):
        state = pl.pallas_call(
            functools.partial(next_kernel, k),
            out_shape=state_shapes,
            in_specs=[vmem] * 3,
            out_specs=(vmem,) * 3,
            input_output_aliases={0: 0, 1: 1, 2: 2},
            cost_estimate=cost,
            compiler_params=params,
        )(*state)
        if k == 1:
            near_p, far_q, *state = lax.optimization_barrier((near_p, far_q, *state))
            panel_p = spread(lead_scale * (panel_p + near_p))
            pieces_p = gather(panel_p)
            panel_q, _ = lax.optimization_barrier((panel_q, panel_p))
            pieces_q = gather(spread(lead_scale * (panel_q + far_q)))
        if k == blocks - 2:
            received_p, received_q, *state = lax.optimization_barrier((received_p, received_q, *state))
            own = scale * (kept_p + received_p), scale * (kept_q + received_q)
            own_top = jnp.concatenate([v[:SPLIT] for v in own], 0)
            far_top = lax.ppermute(own_top, "row", [(0, 1)])
    far_top, *state = lax.optimization_barrier((far_top, *state))
    own_top = jnp.where(is_first, own_top, far_top)
    panel_pieces = [v for pq in zip(pieces_p, pieces_q) for v in pq]

    return pl.pallas_call(
        last_kernel,
        out_shape=jax.ShapeDtypeStruct((height, width), jnp.float32),
        in_specs=[smem] + [vmem] * (2 * blocks + 6),
        out_specs=vmem,
        scratch_shapes=[pltpu.VMEM((LEAD, width), jnp.float32)] * 3,
        cost_estimate=cost,
        compiler_params=params,
        name="own_columns",
    )(info, *state, own_top, *own, *panel_pieces)


def solution(mesh):
    in_specs = (P("row", "col"), P(None, "row"), P(None, "col"))
    out_specs = P("row", "col")

    return jax.shard_map(shards, mesh=mesh, in_specs=in_specs, out_specs=out_specs, check_vma=False)
```
